32 devices in a mesh: rad: 2 (over core), azi: 16 (over z, y, x).
Axes of the slice: x: 2, y: 2, z: 4, core: 2. Of those that a mesh axis runs over, the one named last changes fastest.
Arguments:
- density: float32 [4, 64, 16384], P(None, 'rad', 'azi'), may hold values from -6 to 6
- radial_velocity: float32 [4, 64, 16384], P(None, 'rad', 'azi'), may hold values from -6 to 6
- azimuthal_velocity: float32 [4, 64, 16384], P(None, 'rad', 'azi'), may hold values from -6 to 6
- cycle_shift: int32 [64], P('rad'), may hold values from 0 to 16383
- remainder: float32 [64], P('rad'), may hold values from 0 to 1
- kernel: bfloat16 [2048, 64, 64], P(('rad', 'azi')), may hold values from -0.75 to 0.75
Outputs:
- density_next: float32 [4, 64, 16384], P(None, 'rad', 'azi')
- radial_next: float32 [4, 64, 16384], P(None, 'rad', 'azi')
- azimuthal_next: float32 [4, 64, 16384], P(None, 'rad', 'azi')
- potential: float32 [64, 16384], P(('rad', 'azi'))
The draws below stay inside these ranges and needn't reach their ends.
All inputs are finite; a program needn't handle non-finite values.
Results may differ from the reference program's by a relative error of at most 0.0003.
The reference program's roundings to bfloat16 on the way (of `spectrum`) count: a program that leaves them out, or rounds other values in their place, can miss the bound.
Values may be sent and summed in bfloat16 or wider, within the bound.
No kernel may reach another device: no remote copies, remote signals or barrier semaphores. Data moves between devices by JAX's collectives and lax.ppermute only.
A program may use at most 256 MiB of HBM per device.

```python
import jax
import jax.numpy as jnp
from jax import lax

NZ = 4
NPHI = 16384
MODES = 2048
NR = 64


def touch_ends(array, key, least, largest):
    extent = array.shape
    index_at = [jax.random.randint(jax.random.fold_in(key, axis), (), 0, extent[axis]) for axis in range(len(extent))]
    array = array.at[tuple(index_at)].set(least)
    longest = extent.index(max(extent))
    index_at[longest] = (index_at[longest] + 1) % extent[longest]
    return array.at[tuple(index_at)].set(largest)


def levels(stream_key, dims, split, low, high):
    loudness, own = 1.0, jax.random.fold_in(stream_key, 6)
    for dim, parts in split:
        steps = jnp.exp(jax.random.uniform(jax.random.fold_in(own, dim), (parts,), jnp.float32, low / len(split), high / len(split)))
        loudness = loudness * jnp.repeat(steps, dims[dim] // parts).reshape([-1 if axis == dim else 1 for axis in range(len(dims))])
    return loudness


def normal_values(key, extent, scale, bound, pieces=(), kind=jnp.bfloat16):
    entries = jax.random.normal(key, extent, jnp.float32) * scale
    if len(pieces) > 0:
        entries = levels(key, extent, pieces, -0.22, 0.18) * entries
    return jnp.clip(entries, min=-bound, max=bound).astype(kind)


def setup_inputs(seed: int = 0) -> dict:
    seeds = jax.random.split(jax.random.key(seed), 7)
    return {
        "density": normal_values(seeds[0], (NZ, NR, NPHI), 1.0, 6.0, ((1, 2), (2, 16)), jnp.float32),
        "radial_velocity": normal_values(seeds[1], (NZ, NR, NPHI), 1.0, 6.0, ((1, 2), (2, 16)), jnp.float32),
        "azimuthal_velocity": normal_values(seeds[2], (NZ, NR, NPHI), 1.0, 6.0, ((1, 2), (2, 16)), jnp.float32),
        "cycle_shift": touch_ends(jax.random.randint(seeds[3], (NR,), 0, NPHI), jax.random.fold_in(seeds[3], 1), 0, NPHI - 1).astype(jnp.int32),
        "remainder": jnp.clip(1.0 * jax.random.uniform(seeds[4], (NR,), jnp.float32) ** levels(seeds[4], (NR,), ((0, 2),), -0.2, 0.2), 0.0, 1.0),
        "kernel": normal_values(seeds[5], (MODES, NR, NR), NR ** -0.5, 0.75, ((0, 32),)),
    }


RADIAL_COURANT = 0.3
VISCOSITY = 0.08


def cycle_coeffs(first_row, row_count, cycle_total):
    cycle_index = first_row + lax.broadcasted_iota(jnp.int32, (row_count, 1), 0)
    radius = 1.0 + 4.0 * (cycle_index.astype(jnp.float32) + 0.5) / cycle_total
    return 0.3 / radius, 0.2 * radius ** -1.5, 0.05 * radius ** -1.5


def rates(padded, coeffs):
    courant, coriolis, epicycle = coeffs
    extended = jnp.concatenate([padded[:, :1], padded, padded[:, -1:]], axis=1)
    center = extended[:, 1:-1, 1:-1, 1:-1]
    rad_diff = 0.5 * (extended[:, 1:-1, 2:, 1:-1] - extended[:, 1:-1, :-2, 1:-1])
    azi_diff = 0.5 * (extended[:, 1:-1, 1:-1, 2:] - extended[:, 1:-1, 1:-1, :-2])
    spread = (extended[:, 2:, 1:-1, 1:-1] + extended[:, :-2, 1:-1, 1:-1]
              + extended[:, 1:-1, 2:, 1:-1] + extended[:, 1:-1, :-2, 1:-1]
              + extended[:, 1:-1, 1:-1, 2:] + extended[:, 1:-1, 1:-1, :-2] - 6.0 * center)
    change_rho = -(RADIAL_COURANT * rad_diff[1] + courant * azi_diff[2]) + VISCOSITY * spread[0]
    change_radial = coriolis * center[2] - RADIAL_COURANT * rad_diff[0] + VISCOSITY * spread[1]
    change_azimuthal = -epicycle * center[1] - courant * azi_diff[0] + VISCOSITY * spread[2]
    return jnp.stack([change_rho, change_radial, change_azimuthal]), center


def pad_fields(fields):
    padded = jnp.pad(fields, ((0, 0), (0, 0), (1, 1), (0, 0)), mode="edge")
    return jnp.pad(padded, ((0, 0), (0, 0), (0, 0), (1, 1)), mode="wrap")


def cubic_weights(remainder):
    moved = -remainder[:, None]
    w_next = moved * (moved + 1.0) * (moved + 2.0) / 6.0
    w_here = -(moved - 1.0) * (moved + 1.0) * (moved + 2.0) / 2.0
    w_prev = (moved - 1.0) * moved * (moved + 2.0) / 2.0
    w_prev_two = -(moved - 1.0) * moved * (moved + 1.0) / 6.0
    return w_next, w_here, w_prev, w_prev_two


def reference(density, radial_velocity, azimuthal_velocity, cycle_shift, remainder, kernel):
    fields = jnp.stack([density, radial_velocity, azimuthal_velocity])
    coeffs = cycle_coeffs(0, NR, NR)
    change, center = rates(pad_fields(fields), coeffs)
    section_one = fields + change
    change_two, center_two = rates(pad_fields(section_one), coeffs)
    hydro = 0.5 * fields + 0.5 * (section_one + change_two)
    rotated = jax.vmap(lambda one_cycle, amount: jnp.roll(one_cycle, amount, axis=-1),
                       in_axes=(2, 0), out_axes=2)(hydro, cycle_shift)
    w_next, w_here, w_prev, w_prev_two = cubic_weights(remainder)
    moved = (w_next * jnp.roll(rotated, -1, axis=3) + w_here * rotated
             + w_prev * jnp.roll(rotated, 1, axis=3) + w_prev_two * jnp.roll(rotated, 2, axis=3))
    surface = jnp.sum(moved[0], axis=0)
    transform = jnp.fft.rfft(surface, axis=-1)[:, :MODES]
    spectrum = jnp.stack([jnp.real(transform), jnp.imag(transform)]).astype(jnp.bfloat16)
    columns = jnp.moveaxis(spectrum, 2, 0)

    def one_mode(pair):
        matrix, column = pair
        return jnp.dot(column.astype(jnp.float32), matrix.astype(jnp.float32).T,
                       precision=lax.Precision.HIGHEST)

    mode_potential = lax.map(one_mode, (kernel, columns))
    complex_modes = lax.complex(mode_potential[:, 0, :], mode_potential[:, 1, :]).T
    complex_modes = jnp.pad(complex_modes, ((0, 0), (0, NPHI // 2 + 1 - MODES)))
    potential = jnp.fft.irfft(complex_modes, n=NPHI, axis=-1)
    return moved[0], moved[1], moved[2], potential
```

```python
import functools
import math

import jax
import jax.numpy as jnp
import numpy as np
from jax import lax
from jax.experimental import pallas as pl
from jax.experimental.pallas import tpu as pltpu
from jax.sharding import PartitionSpec as P

RADIAL_COURANT = 0.3
VISCOSITY = 0.08
LANES = 128
SUB = 8
EXACT = lax.Precision.HIGHEST
F32 = jnp.float32
BF16 = jnp.bfloat16

POWER = 12
TOP = 2.0**10.5
GAIN = 1.25


def encode(value, scale):
    scaled = value * scale
    second = scaled * scaled
    fourth = second * second
    size = fourth * fourth * fourth
    return jnp.where(scaled < 0.0, -size, size)


def decode(code, scale):
    size = jnp.abs(code)
    root = jnp.exp2(jnp.log2(jnp.maximum(size, 1e-37)) * (1.0 / POWER)) * scale
    return jnp.where(size < 2e-38, 0.0, jnp.where(code < 0.0, -root, root))


def row_iota(shape):
    return lax.broadcasted_iota(jnp.int32, shape, 0)


def lane_iota(shape):
    return lax.broadcasted_iota(jnp.int32, shape, 1)


def row_layout(per, tiles):
    used = per * tiles + per + 1
    return -(-used // SUB) * SUB


def hydro_kernel(per, rho, ur, up, low, high, bulk, surf, field, stage, block):
    nz, slab, seg = rho.shape
    width = seg + LANES
    first = 2 * SUB
    last_tile = slab // SUB + 2
    tiles = seg // LANES
    rad = lax.axis_index("rad")
    rad_count = lax.axis_size("rad")
    total = slab * rad_count
    for c, ref in enumerate((rho, ur, up)):
        for z in range(nz):
            field[c, z, SUB : slab + 3 * SUB, seg:width] = jnp.zeros((slab + 2 * SUB, LANES), F32)
            field[c, z, first : first + slab, 0:seg] = ref[z]
            inner = jnp.broadcast_to(ref[z, 0:1, :], (2, seg))
            outer = jnp.broadcast_to(ref[z, slab - 1 : slab, :], (2, seg))
            field[c, z, first - 2 : first, 0:seg] = jnp.where(rad == 0, inner, low[c, z])
            field[c, z, first + slab : first + slab + 2, 0:seg] = jnp.where(
                rad == rad_count - 1, outer, high[c, z]
            )
    sub = row_iota((SUB, width))

    def rates_at(ref, tile, z):
        cycle = rad * slab - first + tile * SUB + row_iota((SUB, LANES))
        radius = 1.0 + 4.0 * (cycle.astype(F32) + 0.5) / total
        power = 1.0 / (radius * jnp.sqrt(radius))
        wide = lambda x: jnp.concatenate([x] * (width // LANES), axis=1)
        courant = wide(0.5 * (0.3 / radius))
        coriolis, epicycle = wide(0.2 * power), wide(0.05 * power)
        here = pl.ds(pl.multiple_of(tile * SUB, SUB), SUB)
        before = pl.ds(pl.multiple_of((tile - 1) * SUB, SUB), SUB)
        after = pl.ds(pl.multiple_of((tile + 1) * SUB, SUB), SUB)
        z_up, z_down = min(z + 1, nz - 1), max(z - 1, 0)
        center, rad_diff, azi_diff, spread = [], [], [], []
        for c in range(3):
            cur = ref[c, z, here, :]
            inward = pltpu.roll(jnp.where(sub == SUB - 1, ref[c, z, before, :], cur), 1, 0)
            outward = pltpu.roll(jnp.where(sub == 0, ref[c, z, after, :], cur), SUB - 1, 0)
            ahead = pltpu.roll(cur, width - 1, 1)
            behind = pltpu.roll(cur, 1, 1)
            near = ref[c, z_up, here, :] + ref[c, z_down, here, :] + inward + outward + ahead + behind
            spread.append(VISCOSITY * near - (6.0 * VISCOSITY) * cur)
            rad_diff.append(outward - inward)
            azi_diff.append(ahead - behind)
            center.append(cur)
        half = 0.5 * RADIAL_COURANT
        return center, (
            spread[0] - (half * rad_diff[1] + courant * azi_diff[2]),
            coriolis * center[2] - half * rad_diff[0] + spread[1],
            spread[2] - epicycle * center[1] - courant * azi_diff[0],
        )

    def first_section(tile, carry):
        for z in range(nz):
            center, change = rates_at(field, tile, z)
            for c in range(3):
                stage[c, z, pl.ds(pl.multiple_of(tile * SUB, SUB), SUB), :] = center[c] + change[c]
        return carry

    lax.fori_loop(1, last_tile + 1, first_section, 0)

    @pl.when(rad == 0)
    def _():
        for c in range(3):
            for z in range(nz):
                stage[c, z, first - 1 : first, :] = stage[c, z, first : first + 1, :]

    @pl.when(rad == rad_count - 1)
    def _():
        for c in range(3):
            for z in range(nz):
                stage[c, z, first + slab : first + slab + 1, :] = stage[
                    c, z, first + slab - 1 : first + slab, :
                ]

    def second_section(tile, largest):
        here = pl.ds(pl.multiple_of(tile * SUB, SUB), SUB)
        for z in range(nz):
            center, change = rates_at(stage, tile, z)
            for c in range(3):
                value = 0.5 * field[c, z, here, :] + 0.5 * (center[c] + change[c])
                field[c, z, here, :] = value
                largest = jnp.maximum(largest, jnp.abs(value))
        return largest

    largest = lax.fori_loop(2, last_tile, second_section, jnp.zeros((SUB, width), F32))
    peak = jnp.maximum(jnp.max(largest, keepdims=True), 1e-30)
    scale = TOP / peak
    dests = SUB // per

    def pack(tile, carry):
        here = pl.ds(pl.multiple_of(tile * SUB, SUB), SUB)
        overflow = jnp.zeros((SUB, LANES), F32)
        column = jnp.zeros((SUB, seg), F32)
        for c in range(3):
            for z in range(nz):
                value = field[c, z, here, 0:seg]
                if c == 0:
                    column = column + value
                code = encode(value, scale)
                plane = c * nz + z
                for d in range(dests):
                    block[(tile - 2) * dests + d, plane * per : (plane + 1) * per, :] = code[
                        d * per : (d + 1) * per, :
                    ]
                overflow = overflow + pltpu.roll(field[c, z, here, seg:width], 2 + 4 * plane, 1)
        rows = surf.shape[1]
        for d in range(dests):
            dest = (tile - 2) * dests + d
            for k in range(per):
                row = d * per + k
                for b in range(tiles):
                    surf[dest, k * tiles + b : k * tiles + b + 1, :] = column[
                        row : row + 1, b * LANES : (b + 1) * LANES
                    ]
                at = per * tiles + k
                surf[dest, at : at + 1, :] = overflow[row : row + 1, :]
            spare = per * tiles + per
            surf[dest, spare:rows, :] = jnp.broadcast_to(peak, (rows - spare, LANES))
        return carry

    lax.fori_loop(2, last_tile, pack, 0)

    def narrow(d, carry):
        bulk[d] = block[d].astype(BF16)
        return carry

    lax.fori_loop(0, bulk.shape[0], narrow, 0)


def advect_kernel(per, nz, shift, remainder, bulk, surf, out, ring, tapped, over):
    sources, rows, seg = bulk.shape
    tiles = seg // LANES
    count = sources * tiles
    group = nz * per
    spare = per * tiles + per
    me = lax.axis_index("azi")

    def widen(a, carry):
        unit = surf[a, spare : spare + 1, :] * (1.0 / TOP)
        unit = jnp.concatenate([unit] * tiles, axis=1)
        value = decode(bulk[a].astype(F32), unit)
        for c in range(3):
            for b in range(tiles):
                ring[c, a * tiles + b] = value[
                    c * group : (c + 1) * group, b * LANES : (b + 1) * LANES
                ]
        packed = surf[a, per * tiles : per * tiles + per, :]
        for c in range(3):
            for z in range(nz):
                turned = pltpu.roll(packed, LANES - 2 - 4 * (c * nz + z), 1)
                over[c, a, z * per : (z + 1) * per, :] = turned
        return carry

    lax.fori_loop(0, sources, widen, 0)
    lane = lane_iota((group, LANES))
    cycle = row_iota((group, LANES)) % per

    def spill(a, carry):
        after = lax.rem((a + 1) * tiles, count)
        before = lax.rem(a * tiles + count - 1, count)
        for c in range(3):
            extra = over[c, a]
            ring[c, after] = ring[c, after] + jnp.where(lane < 2, extra, 0.0)
            ring[c, before] = ring[c, before] + jnp.where(lane >= LANES - 2, extra, 0.0)
        return carry

    lax.fori_loop(0, sources, spill, 0)
    x = jnp.zeros((group, LANES), F32)
    whole, part = [], []
    for k in range(per):
        x = jnp.where(cycle == k, -remainder[me * per + k], x)
        amount = shift[me * per + k]
        whole.append(amount // LANES)
        part.append(lax.rem(amount, LANES))
    w_next = x * (x + 1.0) * (x + 2.0) / 6.0
    w_here = -(x - 1.0) * (x + 1.0) * (x + 2.0) / 2.0
    w_prev = (x - 1.0) * x * (x + 2.0) / 2.0
    w_prev_two = -(x - 1.0) * x * (x + 1.0) / 6.0

    def tap(t, carry):
        after = lax.rem(t + 1, count)
        before = lax.rem(t + count - 1, count)
        for c in range(3):
            cur, nxt, prv = ring[c, t], ring[c, after], ring[c, before]
            next_one = pltpu.roll(jnp.where(lane == 0, nxt, cur), LANES - 1, 1)
            prev_one = pltpu.roll(jnp.where(lane == LANES - 1, prv, cur), 1, 1)
            prev_two = pltpu.roll(jnp.where(lane >= LANES - 2, prv, cur), 2, 1)
            tapped[c, t] = w_next * next_one + w_here * cur + w_prev * prev_one + w_prev_two * prev_two
        return carry

    lax.fori_loop(0, count, tap, 0)
    peak = jnp.max(surf[:, spare, :], axis=0, keepdims=True)
    scale = (TOP / GAIN) / peak

    def turned_tile(c, k, t):
        source = lax.rem(t - whole[k] + 2 * count, count)
        return pltpu.roll(tapped[c, source], part[k], 1)

    def turn(dest, carry):
        carry = list(carry)
        pieces = [[None] * tiles for _ in range(3)]
        for b in range(tiles):
            t = dest * tiles + b
            for c in range(3):
                joined = jnp.zeros((group, LANES), F32)
                for k in range(per):
                    now = turned_tile(c, k, t)
                    value = jnp.where(lane < part[k], carry[c * per + k], now)
                    joined = value if per == 1 else jnp.where(cycle == k, value, joined)
                    carry[c * per + k] = now
                pieces[c][b] = encode(joined, scale)
        columns = [jnp.concatenate([pieces[c][b] for b in range(tiles)], axis=1) for c in range(3)]
        out[dest] = jnp.concatenate(columns, axis=0).astype(BF16)
        return tuple(carry)

    start = tuple(turned_tile(c, k, -1) for c in range(3) for k in range(per))
    lax.fori_loop(0, sources, turn, start)


def settle_kernel(per, bulk, surf, rho, ur, up):
    nz = rho.shape[0]
    sources, rows, seg = bulk.shape
    tiles = seg // LANES
    spare = per * tiles + per
    peak = jnp.max(surf[:, spare, :], axis=0, keepdims=True)
    unit = jnp.concatenate([peak * (GAIN / TOP)] * tiles, axis=1)
    for a in range(sources):
        value = decode(bulk[a].astype(F32), unit)
        for c, ref in enumerate((rho, ur, up)):
            for z in range(nz):
                plane = c * nz + z
                ref[z, a * per : (a + 1) * per, :] = value[plane * per : (plane + 1) * per, :]


def forward_kernel(per, nz, modes, shift, remainder, surf, circle, twiddle, short, out, rows_out):
    sources = surf.shape[0]
    nq = circle.shape[0]
    tiles = nq // sources
    length = nq * LANES
    upper = modes // nq
    dests = out.shape[0]
    me = lax.axis_index("azi")
    lane = lane_iota((sources, LANES))
    q_id, a_id = row_iota((nq, sources)), lane_iota((nq, sources))
    to_after = (q_id == lax.rem((a_id + 1) * tiles, nq)).astype(F32)
    to_before = (q_id == lax.rem(a_id * tiles + nq - 1, nq)).astype(F32)
    mode = row_iota((upper, nq)) * nq + lane_iota((upper, nq))
    dot = functools.partial(jnp.dot, precision=EXACT, preferred_element_type=F32)
    for k in range(per):
        packed = surf[:, per * tiles + k, :]
        extra = jnp.zeros((sources, LANES), F32)
        for z in range(nz):
            extra = extra + pltpu.roll(packed, LANES - 2 - 4 * z, 1)
        grid = surf[:, k * tiles : (k + 1) * tiles, :].reshape(nq, LANES)
        grid = grid + dot(to_after, jnp.where(lane < 2, extra, 0.0))
        grid = grid + dot(to_before, jnp.where(lane >= LANES - 2, extra, 0.0))
        inner = dot(grid.T, circle[...])
        cos_part, sin_part = inner[:, :nq], inner[:, nq:]
        turn_cos, turn_sin = twiddle[:, :nq], twiddle[:, nq:]
        real = cos_part * turn_cos - sin_part * turn_sin
        imag = -(sin_part * turn_cos + cos_part * turn_sin)
        outer = dot(short[...], jnp.concatenate([real, imag], axis=1))
        real = outer[:upper, :nq] + outer[upper:, nq:]
        imag = outer[:upper, nq:] - outer[upper:, :nq]
        amount = shift[me * per + k]
        x = jnp.full((upper, nq), -remainder[me * per + k], F32)
        weights = (
            (-1, x * (x + 1.0) * (x + 2.0) / 6.0),
            (0, -(x - 1.0) * (x + 1.0) * (x + 2.0) / 2.0),
            (1, (x - 1.0) * x * (x + 2.0) / 2.0),
            (2, -(x - 1.0) * x * (x + 1.0) / 6.0),
        )
        gain_cos = jnp.zeros((upper, nq), F32)
        gain_sin = jnp.zeros((upper, nq), F32)
        for offset, weight in weights:
            steps = lax.rem(mode * (amount + offset + length), length)
            angle = steps.astype(F32) * (2.0 * math.pi / length)
            gain_cos = gain_cos + weight * jnp.cos(angle)
            gain_sin = gain_sin + weight * jnp.sin(angle)
        rows_out[:, k, :] = real * gain_cos + imag * gain_sin
        rows_out[:, per + k, :] = imag * gain_cos - real * gain_sin
    share = dests // upper
    for d in range(dests):
        out[d] = rows_out[d // share, 0 : 2 * per, :].astype(BF16)


def couple_kernel(per, local, columns, kernel, out, lines):
    sources, parts, nq = columns.shape
    total = sources * per
    me = lax.axis_index("rad") * lax.axis_size("azi") + lax.axis_index("azi")
    offset = lax.rem(me * local, nq)
    row, col = row_iota((total, total)), lane_iota((total, total))
    spread = (row == lax.rem(col, sources) * per + col // sources).astype(F32)
    lines[...] = columns[...].astype(F32)
    lane = lane_iota((total, nq))
    sides = []
    for c in range(2):
        stacked = jnp.concatenate([lines[:, c * per + k, :] for k in range(per)], axis=0)
        ordered = jnp.dot(spread, stacked, preferred_element_type=F32)
        sides.append(pltpu.roll(ordered, lax.rem(nq - offset + c * local, nq), 1))
    weights = jnp.where(lane < local, sides[0], sides[1]).astype(BF16)
    result = jnp.zeros((total, nq), F32)
    for m in range(local):
        product = jnp.dot(kernel[m], weights, preferred_element_type=F32)
        result = jnp.where((lane == m) | (lane == local + m), product, result)
    out[...] = result


def inverse_kernel(per, local, blocks, mixed, circle, twiddle, across, out):
    count = blocks.shape[0] // per
    nq = circle.shape[0]
    length = nq * LANES
    share = nq // local
    dot = functools.partial(jnp.dot, precision=EXACT, preferred_element_type=F32)
    block_id = row_iota((count, nq))
    first = (block_id == 0) & (lane_iota((count, nq)) % local == 0)
    factor = jnp.where(first, 1.0, 2.0) / length
    for k in range(per):
        values = blocks[pl.ds(k, count, stride=per), :] if per > 1 else blocks[...]
        values = values * factor
        real, imag = [], []
        for h in range(share):
            chosen = jnp.where(block_id % share == h, values, 0.0)
            mid = dot(chosen.T, mixed[...])
            top, bottom = mid[0:local, :], mid[local : 2 * local, :]
            real.append(top[:, :LANES] - bottom[:, LANES:])
            imag.append(top[:, LANES:] + bottom[:, :LANES])
        real = jnp.concatenate(real, axis=0)
        imag = jnp.concatenate(imag, axis=0)
        turn_cos, turn_sin = twiddle[:, :LANES], twiddle[:, LANES:]
        turned = jnp.concatenate(
            [real * turn_cos - imag * turn_sin, real * turn_sin + imag * turn_cos], axis=0
        )
        wave = dot(across[...], turned)
        for q in range(nq):
            out[k : k + 1, q * LANES : (q + 1) * LANES] = wave[q : q + 1, :]


def cos_sin(rows, columns, length):
    steps = np.outer(rows, columns) % length
    angle = 2.0 * np.pi * steps / length
    return np.cos(angle).astype(np.float32), np.sin(angle).astype(np.float32)


def call(body, out_shape, in_specs=None, scratch=(), name=None, **cost):
    return pl.pallas_call(
        body,
        out_shape=out_shape,
        **({} if in_specs is None else {"in_specs": in_specs}),
        scratch_shapes=list(scratch),
        name=name,
        cost_estimate=pl.CostEstimate(**{"flops": 0, "bytes_accessed": 0, "transcendentals": 0, **cost}),
    )


def shape_of(shape, dtype=F32):
    return jax.ShapeDtypeStruct(shape, dtype)


def body(density, radial_velocity, azimuthal_velocity, cycle_shift, remainder, kernel):
    nz, slab, seg = density.shape
    azi, rad = lax.axis_size("azi"), lax.axis_size("rad")
    devices = azi * rad
    per = slab // azi
    tiles = seg // LANES
    length = seg * azi
    nq = length // LANES
    local = kernel.shape[0]
    modes = local * devices
    upper = modes // nq
    width = seg + LANES
    group = nz * per
    rows = row_layout(per, tiles)
    both = ("rad", "azi")
    vmem, smem = pl.BlockSpec(memory_space=pltpu.VMEM), pl.BlockSpec(memory_space=pltpu.SMEM)

    fields = (density, radial_velocity, azimuthal_velocity)
    tail = jnp.stack([f[:, slab - 2 :, :] for f in fields])
    head = jnp.stack([f[:, :2, :] for f in fields])
    low = lax.ppermute(tail, "rad", [(i, (i + 1) % rad) for i in range(rad)])
    high = lax.ppermute(head, "rad", [((i + 1) % rad, i) for i in range(rad)])
    bulk, surf = call(
        functools.partial(hydro_kernel, per),
        (shape_of((azi, 3 * group, seg), BF16), shape_of((azi, rows, LANES))),
        scratch=(
            pltpu.VMEM((3, nz, slab + 4 * SUB, width), F32),
            pltpu.VMEM((3, nz, slab + 4 * SUB, width), F32),
            pltpu.VMEM((azi, 3 * group, seg), F32),
        ),
        name="hydro",
        flops=100 * 3 * nz * slab * seg,
        bytes_accessed=24 * nz * slab * seg,
    )(*fields, low, high)

    surf = lax.all_to_all(surf, "azi", 0, 0, tiled=True)
    bulk = lax.all_to_all(bulk, "azi", 0, 0, tiled=True)

    k_id, l_id = np.arange(nq), np.arange(LANES)
    circle = np.concatenate(cos_sin(k_id, k_id, nq), axis=1)
    twiddle = np.concatenate(cos_sin(l_id, k_id, length), axis=1)
    short = np.concatenate(cos_sin(np.arange(upper), l_id, LANES), axis=0)
    spectrum = call(
        functools.partial(forward_kernel, per, nz, modes),
        shape_of((devices, 2 * per, nq), BF16),
        in_specs=[smem, smem, vmem, vmem, vmem, vmem],
        scratch=(pltpu.VMEM((upper, 2 * per, nq), F32),),
        name="forward",
        flops=100_000_000,
        bytes_accessed=1_000_000,
    )(cycle_shift, remainder, surf, jnp.asarray(circle), jnp.asarray(twiddle), jnp.asarray(short))
    columns = lax.all_to_all(spectrum, both, 0, 0, tiled=True)
    total = devices * per
    coupled = call(
        functools.partial(couple_kernel, per, local),
        shape_of((total, nq)),
        scratch=(pltpu.VMEM((devices, 2 * per, nq), F32),),
        name="couple",
        flops=100_000_000,
        bytes_accessed=1_000_000,
    )(columns, kernel)
    blocks = lax.all_to_all(coupled, both, 0, 0, tiled=True)
    j_of_block = np.arange(devices) * local // nq
    mixed = np.concatenate(cos_sin(j_of_block, l_id, LANES), axis=1)
    turn = np.concatenate(cos_sin(k_id, l_id, length), axis=1)
    cosine, sine = cos_sin(k_id, k_id, nq)
    across = np.concatenate([cosine, -sine], axis=1)
    potential = call(
        functools.partial(inverse_kernel, per, local),
        shape_of((per, length)),
        name="inverse",
        flops=100_000_000,
        bytes_accessed=1_000_000,
    )(blocks, jnp.asarray(mixed), jnp.asarray(circle), jnp.asarray(turn), jnp.asarray(across))

    moved = call(
        functools.partial(advect_kernel, per, nz),
        shape_of((azi, 3 * group, seg), BF16),
        in_specs=[smem, smem, vmem, vmem],
        scratch=(
            pltpu.VMEM((3, nq, group, LANES), F32),
            pltpu.VMEM((3, nq, group, LANES), F32),
            pltpu.VMEM((3, azi, group, LANES), F32),
        ),
        name="advect",
        flops=50 * 3 * nz * slab * seg,
        bytes_accessed=12 * nz * slab * seg,
    )(cycle_shift, remainder, bulk, surf)
    moved = lax.all_to_all(moved, "azi", 0, 0, tiled=True)
    results = call(
        functools.partial(settle_kernel, per),
        tuple(shape_of((nz, slab, seg)) for _ in range(3)),
        name="settle",
        flops=20 * 3 * nz * slab * seg,
        bytes_accessed=18 * nz * slab * seg,
    )(moved, surf)
    return (*results, potential)


def solution(mesh):
    split = P(None, "rad", "azi")
    in_specs = (split, split, split, P("rad"), P("rad"), P(("rad", "azi"), None, None))
    out_specs = (split, split, split, P(("rad", "azi"), None))
    return jax.shard_map(body, mesh=mesh, in_specs=in_specs, out_specs=out_specs, check_vma=False)
```

```python
import functools
import math

import jax
import jax.numpy as jnp
import numpy as np
from jax import lax
from jax.experimental import pallas as pl
from jax.experimental.pallas import tpu as pltpu
from jax.sharding import PartitionSpec as P


RADIAL_COURANT = 0.3
VISCOSITY = 0.08
LANES = 128
SUB = 8
EXACT = lax.Precision.HIGHEST
F32 = jnp.float32
BF16 = jnp.bfloat16

POWER = 12
TOP = 2.0**10.5
GAIN = 1.25


def encode(value, scale):
    scaled = value * scale
    second = scaled * scaled
    fourth = second * second
    size = fourth * fourth * fourth
    return jnp.where(scaled < 0.0, -size, size)


def decode(code, scale):
    size = jnp.abs(code)
    root = jnp.exp2(jnp.log2(jnp.maximum(size, 1e-37)) * (1.0 / POWER)) * scale
    return jnp.where(size < 2e-38, 0.0, jnp.where(code < 0.0, -root, root))


def row_iota(shape):
    return lax.broadcasted_iota(jnp.int32, shape, 0)


def lane_iota(shape):
    return lax.broadcasted_iota(jnp.int32, shape, 1)


def parts_of(value):
    high = value.astype(BF16).astype(F32)
    middle = (value - high).astype(BF16).astype(F32)
    return high, middle, (value - high - middle).astype(BF16).astype(F32)


def joined_parts(tile, per):
    rows = tile.shape[0]
    return tile + pltpu.roll(tile, rows - per, 0) + pltpu.roll(tile, rows - 2 * per, 0)


def hydro_kernel(per, rho, ur, up, low, high, bulk, field, stage, block):
    nz, slab, seg = rho.shape
    width = seg + LANES
    first = 2 * SUB
    last_tile = slab // SUB + 2
    tiles = seg // LANES
    rad = lax.axis_index("rad")
    rad_count = lax.axis_size("rad")
    total = slab * rad_count
    for c, ref in enumerate((rho, ur, up)):
        for z in range(nz):
            field[c, z, SUB : slab + 3 * SUB, seg:width] = jnp.zeros((slab + 2 * SUB, LANES), F32)
            field[c, z, first : first + slab, 0:seg] = ref[z]
            inner = jnp.broadcast_to(ref[z, 0:1, :], (2, seg))
            outer = jnp.broadcast_to(ref[z, slab - 1 : slab, :], (2, seg))
            field[c, z, first - 2 : first, 0:seg] = jnp.where(rad == 0, inner, low[c, z])
            field[c, z, first + slab : first + slab + 2, 0:seg] = jnp.where(
                rad == rad_count - 1, outer, high[c, z]
            )
    sub = row_iota((SUB, width))

    def rates_at(ref, tile, z):
        cycle = rad * slab - first + tile * SUB + row_iota((SUB, LANES))
        radius = 1.0 + 4.0 * (cycle.astype(F32) + 0.5) / total
        power = 1.0 / (radius * jnp.sqrt(radius))
        wide = lambda x: jnp.concatenate([x] * (width // LANES), axis=1)
        courant = wide(0.5 * (0.3 / radius))
        coriolis, epicycle = wide(0.2 * power), wide(0.05 * power)
        here = pl.ds(pl.multiple_of(tile * SUB, SUB), SUB)
        before = pl.ds(pl.multiple_of((tile - 1) * SUB, SUB), SUB)
        after = pl.ds(pl.multiple_of((tile + 1) * SUB, SUB), SUB)
        z_up, z_down = min(z + 1, nz - 1), max(z - 1, 0)
        center, rad_diff, azi_diff, spread = [], [], [], []
        for c in range(3):
            cur = ref[c, z, here, :]
            inward = pltpu.roll(jnp.where(sub == SUB - 1, ref[c, z, before, :], cur), 1, 0)
            outward = pltpu.roll(jnp.where(sub == 0, ref[c, z, after, :], cur), SUB - 1, 0)
            ahead = pltpu.roll(cur, width - 1, 1)
            behind = pltpu.roll(cur, 1, 1)
            near = ref[c, z_up, here, :] + ref[c, z_down, here, :] + inward + outward + ahead + behind
            spread.append(VISCOSITY * near - (6.0 * VISCOSITY) * cur)
            rad_diff.append(outward - inward)
            azi_diff.append(ahead - behind)
            center.append(cur)
        half = 0.5 * RADIAL_COURANT
        return center, (
            spread[0] - (half * rad_diff[1] + courant * azi_diff[2]),
            coriolis * center[2] - half * rad_diff[0] + spread[1],
            spread[2] - epicycle * center[1] - courant * azi_diff[0],
        )

    def first_section(tile, carry):
        for z in range(nz):
            center, change = rates_at(field, tile, z)
            for c in range(3):
                stage[c, z, pl.ds(pl.multiple_of(tile * SUB, SUB), SUB), :] = center[c] + change[c]
        return carry

    lax.fori_loop(1, last_tile + 1, first_section, 0)

    @pl.when(rad == 0)
    def _():
        for c in range(3):
            for z in range(nz):
                stage[c, z, first - 1 : first, :] = stage[c, z, first : first + 1, :]

    @pl.when(rad == rad_count - 1)
    def _():
        for c in range(3):
            for z in range(nz):
                stage[c, z, first + slab : first + slab + 1, :] = stage[
                    c, z, first + slab - 1 : first + slab, :
                ]

    def second_section(tile, largest):
        here = pl.ds(pl.multiple_of(tile * SUB, SUB), SUB)
        for z in range(nz):
            center, change = rates_at(stage, tile, z)
            for c in range(3):
                value = 0.5 * field[c, z, here, :] + 0.5 * (center[c] + change[c])
                field[c, z, here, :] = value
                largest = jnp.maximum(largest, jnp.abs(value))
        return largest

    largest = lax.fori_loop(2, last_tile, second_section, jnp.zeros((SUB, width), F32))
    peak = jnp.maximum(jnp.max(largest, keepdims=True), 1e-30)
    scale = TOP / peak
    dests = SUB // per

    def pack(tile, carry):
        here = pl.ds(pl.multiple_of(tile * SUB, SUB), SUB)
        overflow = jnp.zeros((SUB, LANES), F32)
        column = jnp.zeros((SUB, seg), F32)
        for c in range(3):
            for z in range(nz):
                value = field[c, z, here, 0:seg]
                if c == 0:
                    column = column + value
                code = encode(value, scale)
                plane = c * nz + z
                for d in range(dests):
                    block[(tile - 2) * dests + d, plane * per : (plane + 1) * per, :] = code[
                        d * per : (d + 1) * per, :
                    ]
                overflow = overflow + pltpu.roll(field[c, z, here, seg:width], 2 + 4 * plane, 1)
        overflow = jnp.where(lane_iota((SUB, LANES)) < LANES // 2, overflow, peak)
        base = bulk.shape[1] - SUB
        for part, (tall, over) in enumerate(zip(parts_of(column), parts_of(overflow))):
            for d in range(dests):
                dest = (tile - 2) * dests + d
                for k in range(per):
                    row = d * per + k
                    at = pl.ds((part * per + k) * LANES, LANES)
                    for b in range(tiles):
                        block[dest, base + b : base + b + 1, at] = tall[
                            row : row + 1, b * LANES : (b + 1) * LANES
                        ]
                    at = pl.ds(3 * per * LANES, LANES)
                    line = base + part * per + k
                    block[dest, line : line + 1, at] = over[row : row + 1, :]
        return carry

    lax.fori_loop(2, last_tile, pack, 0)

    def narrow(d, carry):
        bulk[d] = block[d].astype(BF16)
        return carry

    lax.fori_loop(0, bulk.shape[0], narrow, 0)


def advect_kernel(per, nz, shift, remainder, bulk, out, top, ring, tapped, over):
    sources, _, seg = bulk.shape
    tiles = seg // LANES
    count = sources * tiles
    group = nz * per
    base = bulk.shape[1] - SUB
    me = lax.axis_index("azi")

    def widen(a, peak):
        whole_block = bulk[a].astype(F32)
        at = 3 * per * LANES
        packed = joined_parts(whole_block[base : base + SUB, at : at + LANES], per)[0:per, :]
        mine = jnp.where(lane_iota((1, LANES)) >= LANES // 2, packed[0:1, :], 0.0)
        mine = jnp.max(mine, keepdims=True)
        value = decode(whole_block[0:base, :], mine * (1.0 / TOP))
        for c in range(3):
            for b in range(tiles):
                ring[c, a * tiles + b] = value[
                    c * group : (c + 1) * group, b * LANES : (b + 1) * LANES
                ]
        for c in range(3):
            for z in range(nz):
                turned = pltpu.roll(packed, LANES - 2 - 4 * (c * nz + z), 1)
                over[c, a, z * per : (z + 1) * per, :] = turned
        return jnp.maximum(peak, mine)

    peak = lax.fori_loop(0, sources, widen, jnp.zeros((1, 1), F32))
    top[...] = jnp.broadcast_to(peak, top.shape)
    lane = lane_iota((group, LANES))
    cycle = row_iota((group, LANES)) % per

    def spill(a, carry):
        after = lax.rem((a + 1) * tiles, count)
        before = lax.rem(a * tiles + count - 1, count)
        for c in range(3):
            extra = over[c, a]
            ring[c, after] = ring[c, after] + jnp.where(lane < 2, extra, 0.0)
            ring[c, before] = ring[c, before] + jnp.where(lane >= LANES - 2, extra, 0.0)
        return carry

    lax.fori_loop(0, sources, spill, 0)
    x = jnp.zeros((group, LANES), F32)
    whole, part = [], []
    for k in range(per):
        x = jnp.where(cycle == k, -remainder[me * per + k], x)
        amount = shift[me * per + k]
        whole.append(amount // LANES)
        part.append(lax.rem(amount, LANES))
    w_next = x * (x + 1.0) * (x + 2.0) / 6.0
    w_here = -(x - 1.0) * (x + 1.0) * (x + 2.0) / 2.0
    w_prev = (x - 1.0) * x * (x + 2.0) / 2.0
    w_prev_two = -(x - 1.0) * x * (x + 1.0) / 6.0

    def tap(a, carry):
        before = lax.rem(a * tiles + count - 1, count)
        after = lax.rem((a + 1) * tiles, count)
        for c in range(3):
            line = [ring[c, before]]
            line += [ring[c, a * tiles + b] for b in range(tiles)]
            line += [ring[c, after]]
            for b in range(tiles):
                prv, cur, nxt = line[b : b + 3]
                next_one = pltpu.roll(jnp.where(lane == 0, nxt, cur), LANES - 1, 1)
                prev_one = pltpu.roll(jnp.where(lane == LANES - 1, prv, cur), 1, 1)
                prev_two = pltpu.roll(jnp.where(lane >= LANES - 2, prv, cur), 2, 1)
                tapped[c, a * tiles + b] = (
                    w_next * next_one + w_here * cur + w_prev * prev_one + w_prev_two * prev_two
                )
        return carry

    lax.fori_loop(0, sources, tap, 0)
    scale = (TOP / GAIN) / peak

    def turned_tile(c, k, t):
        source = lax.rem(t - whole[k] + 2 * count, count)
        return pltpu.roll(tapped[c, source], part[k], 1)

    def turn(dest, carry):
        carry = list(carry)
        pieces = [[None] * tiles for _ in range(3)]
        for b in range(tiles):
            t = dest * tiles + b
            for c in range(3):
                joined = jnp.zeros((group, LANES), F32)
                for k in range(per):
                    now = turned_tile(c, k, t)
                    value = jnp.where(lane < part[k], carry[c * per + k], now)
                    joined = value if per == 1 else jnp.where(cycle == k, value, joined)
                    carry[c * per + k] = now
                pieces[c][b] = encode(joined, scale)
        columns = [jnp.concatenate([pieces[c][b] for b in range(tiles)], axis=1) for c in range(3)]
        out[dest] = jnp.concatenate(columns, axis=0).astype(BF16)
        return tuple(carry)

    start = tuple(turned_tile(c, k, -1) for c in range(3) for k in range(per))
    lax.fori_loop(0, sources, turn, start)


def settle_kernel(per, bulk, top, rho, ur, up):
    nz = rho.shape[0]
    sources, _, seg = bulk.shape
    unit = jnp.concatenate([top[0:1, :] * (GAIN / TOP)] * (seg // LANES), axis=1)
    for a in range(sources):
        value = decode(bulk[a].astype(F32), unit)
        for c, ref in enumerate((rho, ur, up)):
            for z in range(nz):
                plane = c * nz + z
                ref[z, a * per : (a + 1) * per, :] = value[plane * per : (plane + 1) * per, :]


def forward_kernel(per, nz, modes, shift, remainder, side, circle, twiddle, short, out, rows_out):
    sources = side.shape[0]
    nq = circle.shape[0]
    tiles = nq // sources
    length = nq * LANES
    upper = modes // nq
    dests = out.shape[0]
    me = lax.axis_index("azi")
    lane = lane_iota((sources, LANES))
    q_id, a_id = row_iota((nq, sources)), lane_iota((nq, sources))
    to_after = (q_id == lax.rem((a_id + 1) * tiles, nq)).astype(F32)
    to_before = (q_id == lax.rem(a_id * tiles + nq - 1, nq)).astype(F32)
    mode = row_iota((upper, nq)) * nq + lane_iota((upper, nq))
    dot = functools.partial(jnp.dot, precision=EXACT, preferred_element_type=F32)
    for k in range(per):
        at = 3 * per * LANES
        folded = [
            joined_parts(side[a, :, at : at + LANES].astype(F32), per)[k : k + 1, :]
            for a in range(sources)
        ]
        packed = jnp.concatenate(folded, axis=0)
        extra = jnp.zeros((sources, LANES), F32)
        for z in range(nz):
            extra = extra + pltpu.roll(packed, LANES - 2 - 4 * z, 1)
        grid = []
        for a in range(sources):
            tile = jnp.zeros((SUB, LANES), F32)
            for part in range(3):
                at = (part * per + k) * LANES
                tile = tile + side[a, :, at : at + LANES].astype(F32)
            grid.append(tile[0:tiles, :])
        grid = jnp.concatenate(grid, axis=0)
        grid = grid + dot(to_after, jnp.where(lane < 2, extra, 0.0))
        grid = grid + dot(to_before, jnp.where(lane >= LANES - 2, extra, 0.0))
        inner = dot(grid.T, circle[...])
        cos_part, sin_part = inner[:, :nq], inner[:, nq:]
        turn_cos, turn_sin = twiddle[:, :nq], twiddle[:, nq:]
        real = cos_part * turn_cos - sin_part * turn_sin
        imag = -(sin_part * turn_cos + cos_part * turn_sin)
        outer = dot(short[...], jnp.concatenate([real, imag], axis=1))
        real = outer[:upper, :nq] + outer[upper:, nq:]
        imag = outer[:upper, nq:] - outer[upper:, :nq]
        amount = shift[me * per + k]
        x = jnp.full((upper, nq), -remainder[me * per + k], F32)
        weights = (
            (-1, x * (x + 1.0) * (x + 2.0) / 6.0),
            (0, -(x - 1.0) * (x + 1.0) * (x + 2.0) / 2.0),
            (1, (x - 1.0) * x * (x + 2.0) / 2.0),
            (2, -(x - 1.0) * x * (x + 1.0) / 6.0),
        )
        gain_cos = jnp.zeros((upper, nq), F32)
        gain_sin = jnp.zeros((upper, nq), F32)
        for offset, weight in weights:
            steps = lax.rem(mode * (amount + offset + length), length)
            angle = steps.astype(F32) * (2.0 * math.pi / length)
            gain_cos = gain_cos + weight * jnp.cos(angle)
            gain_sin = gain_sin + weight * jnp.sin(angle)
        rows_out[:, k, :] = real * gain_cos + imag * gain_sin
        rows_out[:, per + k, :] = imag * gain_cos - real * gain_sin
    share = dests // upper
    for d in range(dests):
        out[d] = rows_out[d // share, 0 : 2 * per, :].astype(BF16)


def couple_kernel(per, local, columns, kernel, out, lines):
    sources, _, nq = columns.shape
    total = sources * per
    me = lax.axis_index("rad") * lax.axis_size("azi") + lax.axis_index("azi")
    offset = lax.rem(me * local, nq)
    row, col = row_iota((total, total)), lane_iota((total, total))
    spread = (row == lax.rem(col, sources) * per + col // sources).astype(F32)
    lines[...] = columns[...].astype(F32)
    lane = lane_iota((total, nq))
    sides = []
    for c in range(2):
        stacked = jnp.concatenate([lines[:, c * per + k, :] for k in range(per)], axis=0)
        ordered = jnp.dot(spread, stacked, preferred_element_type=F32)
        sides.append(pltpu.roll(ordered, lax.rem(nq - offset + c * local, nq), 1))
    weights = jnp.where(lane < local, sides[0], sides[1]).astype(BF16)
    result = jnp.zeros((total, nq), F32)
    for m in range(local):
        product = jnp.dot(kernel[m], weights, preferred_element_type=F32)
        result = jnp.where((lane == m) | (lane == local + m), product, result)
    out[...] = result


def inverse_kernel(per, local, blocks, mixed, circle, twiddle, across, out):
    count = blocks.shape[0] // per
    nq = circle.shape[0]
    length = nq * LANES
    share = nq // local
    dot = functools.partial(jnp.dot, precision=EXACT, preferred_element_type=F32)
    block_id = row_iota((count, nq))
    first = (block_id == 0) & (lane_iota((count, nq)) % local == 0)
    factor = jnp.where(first, 1.0, 2.0) / length
    for k in range(per):
        values = blocks[pl.ds(k, count, stride=per), :] if per > 1 else blocks[...]
        values = values * factor
        real, imag = [], []
        for h in range(share):
            chosen = jnp.where(block_id % share == h, values, 0.0)
            mid = dot(chosen.T, mixed[...])
            top, bottom = mid[0:local, :], mid[local : 2 * local, :]
            real.append(top[:, :LANES] - bottom[:, LANES:])
            imag.append(top[:, LANES:] + bottom[:, :LANES])
        real = jnp.concatenate(real, axis=0)
        imag = jnp.concatenate(imag, axis=0)
        turn_cos, turn_sin = twiddle[:, :LANES], twiddle[:, LANES:]
        turned = jnp.concatenate(
            [real * turn_cos - imag * turn_sin, real * turn_sin + imag * turn_cos], axis=0
        )
        wave = dot(across[...], turned)
        for q in range(nq):
            out[k : k + 1, q * LANES : (q + 1) * LANES] = wave[q : q + 1, :]


def cos_sin(rows, columns, length):
    steps = np.outer(rows, columns) % length
    angle = 2.0 * np.pi * steps / length
    return np.cos(angle).astype(np.float32), np.sin(angle).astype(np.float32)


def call(body, out_shape, in_specs=None, scratch=(), grid=(), **cost):
    return pl.pallas_call(
        body,
        out_shape=out_shape,
        grid=grid,
        **({} if in_specs is None else {"in_specs": in_specs}),
        scratch_shapes=list(scratch),
        cost_estimate=pl.CostEstimate(**{"flops": 0, "bytes_accessed": 0, "transcendentals": 0, **cost}),
    )


def exchange(array, axes):
    return lax.all_to_all(array, axes, 0, 0, tiled=True)


def shape_of(shape, dtype=F32):
    return jax.ShapeDtypeStruct(shape, dtype)


def body(density, radial_velocity, azimuthal_velocity, cycle_shift, remainder, kernel):
    nz, slab, seg = density.shape
    azi, rad = lax.axis_size("azi"), lax.axis_size("rad")
    devices = azi * rad
    per = slab // azi
    length = seg * azi
    nq = length // LANES
    local = kernel.shape[0]
    modes = local * devices
    upper = modes // nq
    width = seg + LANES
    group = nz * per
    base = -(-3 * group // SUB) * SUB
    rows = base + SUB
    both = ("rad", "azi")
    vmem, smem = pl.BlockSpec(memory_space=pltpu.VMEM), pl.BlockSpec(memory_space=pltpu.SMEM)

    fields = (density, radial_velocity, azimuthal_velocity)
    tail = jnp.stack([f[:, slab - 2 :, :] for f in fields])
    head = jnp.stack([f[:, :2, :] for f in fields])
    low = lax.ppermute(tail, "rad", [(i, (i + 1) % rad) for i in range(rad)])
    high = lax.ppermute(head, "rad", [((i + 1) % rad, i) for i in range(rad)])
    bulk = call(
        functools.partial(hydro_kernel, per),
        shape_of((azi, rows, seg), BF16),
        scratch=(
            pltpu.VMEM((3, nz, slab + 4 * SUB, width), F32),
            pltpu.VMEM((3, nz, slab + 4 * SUB, width), F32),
            pltpu.VMEM((azi, rows, seg), F32),
        ),
        flops=100 * 3 * nz * slab * seg,
        bytes_accessed=24 * nz * slab * seg,
    )(*fields, low, high)

    bulk = exchange(bulk, "azi")

    k_id, l_id = np.arange(nq), np.arange(LANES)
    circle = np.concatenate(cos_sin(k_id, k_id, nq), axis=1)
    twiddle = np.concatenate(cos_sin(l_id, k_id, length), axis=1)
    short = np.concatenate(cos_sin(np.arange(upper), l_id, LANES), axis=0)
    side = pl.BlockSpec((azi, SUB, seg), lambda i: (0, base // SUB, 0))
    spectrum = call(
        functools.partial(forward_kernel, per, nz, modes),
        shape_of((devices, 2 * per, nq), BF16),
        in_specs=[smem, smem, side, vmem, vmem, vmem],
        scratch=(pltpu.VMEM((upper, 2 * per, nq), F32),),
        grid=(1,),
        flops=100_000_000,
        bytes_accessed=1_000_000,
    )(cycle_shift, remainder, bulk, jnp.asarray(circle), jnp.asarray(twiddle), jnp.asarray(short))
    columns = exchange(spectrum, both)
    total = devices * per
    coupled = call(
        functools.partial(couple_kernel, per, local),
        shape_of((total, nq)),
        scratch=(pltpu.VMEM((devices, 2 * per, nq), F32),),
        flops=100_000_000,
        bytes_accessed=1_000_000,
    )(columns, kernel)
    blocks = exchange(coupled, both)
    j_of_block = np.arange(devices) * local // nq
    mixed = np.concatenate(cos_sin(j_of_block, l_id, LANES), axis=1)
    turn = np.concatenate(cos_sin(k_id, l_id, length), axis=1)
    cosine, sine = cos_sin(k_id, k_id, nq)
    across = np.concatenate([cosine, -sine], axis=1)
    potential = call(
        functools.partial(inverse_kernel, per, local),
        shape_of((per, length)),
        flops=100_000_000,
        bytes_accessed=1_000_000,
    )(blocks, jnp.asarray(mixed), jnp.asarray(circle), jnp.asarray(turn), jnp.asarray(across))

    moved, top = call(
        functools.partial(advect_kernel, per, nz),
        (shape_of((azi, 3 * group, seg), BF16), shape_of((SUB, LANES))),
        in_specs=[smem, smem, vmem],
        scratch=(
            pltpu.VMEM((3, nq, group, LANES), F32),
            pltpu.VMEM((3, nq, group, LANES), F32),
            pltpu.VMEM((3, azi, group, LANES), F32),
        ),
        flops=50 * 3 * nz * slab * seg,
        bytes_accessed=12 * nz * slab * seg,
    )(cycle_shift, remainder, bulk)
    moved = exchange(moved, "azi")
    results = call(
        functools.partial(settle_kernel, per),
        tuple(shape_of((nz, slab, seg)) for _ in range(3)),
        flops=20 * 3 * nz * slab * seg,
        bytes_accessed=18 * nz * slab * seg,
    )(moved, top)
    return (*results, potential)


def solution(mesh):
    split = P(None, "rad", "azi")
    in_specs = (split, split, split, P("rad"), P("rad"), P(("rad", "azi"), None, None))
    out_specs = (split, split, split, P(("rad", "azi"), None))

    return jax.shard_map(body, mesh=mesh, in_specs=in_specs, out_specs=out_specs, check_vma=False)
```

```python
import functools
import math

import jax
import jax.numpy as jnp
import numpy as np
from jax import lax
from jax.experimental import pallas as pl
from jax.experimental.pallas import tpu as pltpu
from jax.sharding import PartitionSpec as P


RADIAL_COURANT = 0.3
VISCOSITY = 0.08
LANES = 128
SUB = 8
EXACT = lax.Precision.HIGHEST
F32 = jnp.float32
BF16 = jnp.bfloat16

POWER = 12
TOP = 2.0**10.5
GAIN = 1.25


def encode(value, scale):
    scaled = value * scale
    second = scaled * scaled
    fourth = second * second
    size = fourth * fourth * fourth
    return jnp.where(scaled < 0.0, -size, size)


def decode(code, scale):
    size = jnp.abs(code)
    root = jnp.exp2(jnp.log2(jnp.maximum(size, 1e-37)) * (1.0 / POWER)) * scale
    return jnp.where(size < 2e-38, 0.0, jnp.where(code < 0.0, -root, root))


def row_iota(shape):
    return lax.broadcasted_iota(jnp.int32, shape, 0)


def lane_iota(shape):
    return lax.broadcasted_iota(jnp.int32, shape, 1)


def parts_of(value):
    high = value.astype(BF16).astype(F32)
    return high, (value - high).astype(BF16).astype(F32)


PARTS = 2


def joined_parts(tile, per):
    return tile + pltpu.roll(tile, tile.shape[0] - per, 0)


def load_kernel(rho, ur, up, rho_near, ur_near, up_near, tail, head, sems):
    slab = rho.shape[1]
    pairs = ((rho, rho_near), (ur, ur_near), (up, up_near))
    copies = [pltpu.make_async_copy(far, near, sems.at[c]) for c, (far, near) in enumerate(pairs)]
    for copy in copies:
        copy.start()
    for c, (_, near) in enumerate(pairs):
        copies[c].wait()
        tail[c] = near[:, slab - 2 :, :]
        head[c] = near[:, 0:2, :]


def hydro_kernel(per, rho, ur, up, low, high, bulk, field, stage, block, narrow, sems):
    nz, slab, seg = rho.shape
    width = seg + LANES
    first = 2 * SUB
    last_tile = slab // SUB + 2
    tiles = seg // LANES
    rad = lax.axis_index("rad")
    rad_count = lax.axis_size("rad")
    total = slab * rad_count
    for c, ref in enumerate((rho, ur, up)):
        for z in range(nz):
            field[c, z, SUB : slab + 3 * SUB, seg:width] = jnp.zeros((slab + 2 * SUB, LANES), F32)
            field[c, z, first : first + slab, 0:seg] = ref[z]
            inner = jnp.broadcast_to(ref[z, 0:1, :], (2, seg))
            outer = jnp.broadcast_to(ref[z, slab - 1 : slab, :], (2, seg))
            field[c, z, first - 2 : first, 0:seg] = jnp.where(rad == 0, inner, low[c, z])
            field[c, z, first + slab : first + slab + 2, 0:seg] = jnp.where(
                rad == rad_count - 1, outer, high[c, z]
            )
    sub = row_iota((SUB, width))

    def rates_at(ref, tile, z):
        cycle = rad * slab - first + tile * SUB + row_iota((SUB, LANES))
        radius = 1.0 + 4.0 * (cycle.astype(F32) + 0.5) / total
        power = 1.0 / (radius * jnp.sqrt(radius))
        wide = lambda x: jnp.concatenate([x] * (width // LANES), axis=1)
        courant = wide(0.5 * (0.3 / radius))
        coriolis, epicycle = wide(0.2 * power), wide(0.05 * power)
        here = pl.ds(pl.multiple_of(tile * SUB, SUB), SUB)
        before = pl.ds(pl.multiple_of((tile - 1) * SUB, SUB), SUB)
        after = pl.ds(pl.multiple_of((tile + 1) * SUB, SUB), SUB)
        z_up, z_down = min(z + 1, nz - 1), max(z - 1, 0)
        center, rad_diff, azi_diff, spread = [], [], [], []
        for c in range(3):
            cur = ref[c, z, here, :]
            inward = pltpu.roll(jnp.where(sub == SUB - 1, ref[c, z, before, :], cur), 1, 0)
            outward = pltpu.roll(jnp.where(sub == 0, ref[c, z, after, :], cur), SUB - 1, 0)
            ahead = pltpu.roll(cur, width - 1, 1)
            behind = pltpu.roll(cur, 1, 1)
            near = ref[c, z_up, here, :] + ref[c, z_down, here, :] + inward + outward + ahead + behind
            spread.append(VISCOSITY * near - (6.0 * VISCOSITY) * cur)
            rad_diff.append(outward - inward)
            azi_diff.append(ahead - behind)
            center.append(cur)
        half = 0.5 * RADIAL_COURANT
        return center, (
            spread[0] - (half * rad_diff[1] + courant * azi_diff[2]),
            coriolis * center[2] - half * rad_diff[0] + spread[1],
            spread[2] - epicycle * center[1] - courant * azi_diff[0],
        )

    def first_section(tile, carry):
        for z in range(nz):
            center, change = rates_at(field, tile, z)
            for c in range(3):
                stage[c, z, pl.ds(pl.multiple_of(tile * SUB, SUB), SUB), :] = center[c] + change[c]
        return carry

    lax.fori_loop(1, last_tile + 1, first_section, 0)

    @pl.when(rad == 0)
    def _():
        for c in range(3):
            for z in range(nz):
                stage[c, z, first - 1 : first, :] = stage[c, z, first : first + 1, :]

    @pl.when(rad == rad_count - 1)
    def _():
        for c in range(3):
            for z in range(nz):
                stage[c, z, first + slab : first + slab + 1, :] = stage[
                    c, z, first + slab - 1 : first + slab, :
                ]

    def second_section(tile, largest):
        here = pl.ds(pl.multiple_of(tile * SUB, SUB), SUB)
        for z in range(nz):
            center, change = rates_at(stage, tile, z)
            for c in range(3):
                value = 0.5 * field[c, z, here, :] + 0.5 * (center[c] + change[c])
                field[c, z, here, :] = value
                largest = jnp.maximum(largest, jnp.abs(value))
        return largest

    largest = lax.fori_loop(2, last_tile, second_section, jnp.zeros((SUB, width), F32))
    peak = jnp.maximum(jnp.max(largest, keepdims=True), 1e-30)
    peak = sum(parts_of(peak))
    scale = TOP / peak
    dests = SUB // per
    stride = -(-3 * nz * per // SUB) * SUB
    base = tiles * stride
    lines = base + PARTS * per * SUB

    def send(index):
        at = pl.ds(index * dests, dests)
        return pltpu.make_async_copy(narrow.at[at], bulk.at[at], sems.at[index])

    def pack(tile, carry):
        here = pl.ds(pl.multiple_of(tile * SUB, SUB), SUB)
        overflow = jnp.zeros((SUB, LANES), F32)
        column = jnp.zeros((SUB, seg), F32)
        for c in range(3):
            for z in range(nz):
                value = field[c, z, here, 0:seg]
                if c == 0:
                    column = column + value
                code = encode(value, scale)
                plane = c * nz + z
                for d in range(dests):
                    for b in range(tiles):
                        line = b * stride + plane * per
                        block[(tile - 2) * dests + d, line : line + per, :] = code[
                            d * per : (d + 1) * per, b * LANES : (b + 1) * LANES
                        ]
                overflow = overflow + pltpu.roll(field[c, z, here, seg:width], 2 + 4 * plane, 1)
        overflow = jnp.where(lane_iota((SUB, LANES)) < LANES // 2, overflow, peak)
        for part, (tall, over) in enumerate(zip(parts_of(column), parts_of(overflow))):
            for d in range(dests):
                dest = (tile - 2) * dests + d
                for k in range(per):
                    row = d * per + k
                    at = base + (part * per + k) * SUB
                    for b in range(tiles):
                        block[dest, at + b : at + b + 1, :] = tall[
                            row : row + 1, b * LANES : (b + 1) * LANES
                        ]
                    line = lines + part * per + k
                    block[dest, line : line + 1, :] = over[row : row + 1, :]
        for d in range(dests):
            dest = (tile - 2) * dests + d
            narrow[dest] = block[dest].astype(BF16)
        send(tile - 2).start()
        return carry

    lax.fori_loop(2, last_tile, pack, 0)
    for index in range(slab // SUB):
        send(index).wait()


def advect_kernel(per, nz, shift, remainder, bulk, out, top, ring, tapped, over):
    sources = bulk.shape[0]
    count = ring.shape[1]
    tiles = count // sources
    group = nz * per
    stride = -(-3 * group // SUB) * SUB
    lines = tiles * stride + PARTS * per * SUB
    me = lax.axis_index("azi")

    def widen(a, peak):
        whole_block = bulk[a].astype(F32)
        packed = joined_parts(whole_block[lines : lines + SUB, :], per)[0:per, :]
        mine = jnp.where(lane_iota((1, LANES)) >= LANES // 2, packed[0:1, :], 0.0)
        mine = jnp.max(mine, keepdims=True)
        unit = mine * (1.0 / TOP)
        for b in range(tiles):
            value = decode(whole_block[b * stride : (b + 1) * stride, :], unit)
            for c in range(3):
                ring[c, a * tiles + b] = value[c * group : (c + 1) * group, :]
        for c in range(3):
            for z in range(nz):
                turned = pltpu.roll(packed, LANES - 2 - 4 * (c * nz + z), 1)
                over[c, a, z * per : (z + 1) * per, :] = turned
        return jnp.maximum(peak, mine)

    peak = lax.fori_loop(0, sources, widen, jnp.zeros((1, 1), F32))
    top[...] = jnp.broadcast_to(peak, top.shape)
    lane = lane_iota((group, LANES))
    cycle = row_iota((group, LANES)) % per

    def spill(a, carry):
        after = lax.rem((a + 1) * tiles, count)
        before = lax.rem(a * tiles + count - 1, count)
        for c in range(3):
            extra = over[c, a]
            ring[c, after] = ring[c, after] + jnp.where(lane < 2, extra, 0.0)
            ring[c, before] = ring[c, before] + jnp.where(lane >= LANES - 2, extra, 0.0)
        return carry

    lax.fori_loop(0, sources, spill, 0, unroll=4)
    x = jnp.zeros((group, LANES), F32)
    whole, part = [], []
    for k in range(per):
        x = jnp.where(cycle == k, -remainder[me * per + k], x)
        amount = shift[me * per + k]
        whole.append(amount // LANES)
        part.append(lax.rem(amount, LANES))
    w_next = x * (x + 1.0) * (x + 2.0) / 6.0
    w_here = -(x - 1.0) * (x + 1.0) * (x + 2.0) / 2.0
    w_prev = (x - 1.0) * x * (x + 2.0) / 2.0
    w_prev_two = -(x - 1.0) * x * (x + 1.0) / 6.0

    def tap(a, carry):
        before = lax.rem(a * tiles + count - 1, count)
        after = lax.rem((a + 1) * tiles, count)
        for c in range(3):
            line = [ring[c, before]]
            line += [ring[c, a * tiles + b] for b in range(tiles)]
            line += [ring[c, after]]
            for b in range(tiles):
                prv, cur, nxt = line[b : b + 3]
                next_one = pltpu.roll(jnp.where(lane == 0, nxt, cur), LANES - 1, 1)
                prev_one = pltpu.roll(jnp.where(lane == LANES - 1, prv, cur), 1, 1)
                prev_two = pltpu.roll(jnp.where(lane >= LANES - 2, prv, cur), 2, 1)
                tapped[c, a * tiles + b] = (
                    w_next * next_one + w_here * cur + w_prev * prev_one + w_prev_two * prev_two
                )
        return carry

    lax.fori_loop(0, sources, tap, 0)
    scale = (TOP / GAIN) / peak

    def turned_tile(c, k, t):
        source = lax.rem(t - whole[k] + 2 * count, count)
        return pltpu.roll(tapped[c, source], part[k], 1)

    def turn(dest, carry):
        carry = list(carry)
        pieces = [[None] * tiles for _ in range(3)]
        for b in range(tiles):
            t = dest * tiles + b
            for c in range(3):
                joined = jnp.zeros((group, LANES), F32)
                for k in range(per):
                    now = turned_tile(c, k, t)
                    value = jnp.where(lane < part[k], carry[c * per + k], now)
                    joined = value if per == 1 else jnp.where(cycle == k, value, joined)
                    carry[c * per + k] = now
                pieces[c][b] = encode(joined, scale)
        columns = [jnp.concatenate([pieces[c][b] for b in range(tiles)], axis=1) for c in range(3)]
        out[dest] = jnp.concatenate(columns, axis=0).astype(BF16)
        return tuple(carry)

    start = tuple(turned_tile(c, k, -1) for c in range(3) for k in range(per))
    lax.fori_loop(0, sources, turn, start)


def settle_kernel(per, bulk, top, rho, ur, up):
    nz = rho.shape[0]
    sources, _, seg = bulk.shape
    unit = jnp.concatenate([top[0:1, :] * (GAIN / TOP)] * (seg // LANES), axis=1)
    for a in range(sources):
        value = decode(bulk[a].astype(F32), unit)
        for c, ref in enumerate((rho, ur, up)):
            for z in range(nz):
                plane = c * nz + z
                ref[z, a * per : (a + 1) * per, :] = value[plane * per : (plane + 1) * per, :]


def forward_kernel(per, nz, modes, shift, remainder, side, circle, twiddle, short, out, rows_out):
    sources = side.shape[0]
    nq = circle.shape[0]
    tiles = nq // sources
    length = nq * LANES
    upper = modes // nq
    dests = out.shape[0]
    base = tiles * (-(-3 * nz * per // SUB) * SUB)
    lines = base + PARTS * per * SUB
    me = lax.axis_index("azi")
    lane = lane_iota((sources, LANES))
    q_id, a_id = row_iota((nq, sources)), lane_iota((nq, sources))
    to_after = (q_id == lax.rem((a_id + 1) * tiles, nq)).astype(F32)
    to_before = (q_id == lax.rem(a_id * tiles + nq - 1, nq)).astype(F32)
    mode = row_iota((upper, nq)) * nq + lane_iota((upper, nq))
    dot = functools.partial(jnp.dot, precision=EXACT, preferred_element_type=F32)
    for k in range(per):
        folded = [
            joined_parts(side[a, lines : lines + SUB, :].astype(F32), per)[k : k + 1, :]
            for a in range(sources)
        ]
        packed = jnp.concatenate(folded, axis=0)
        extra = jnp.zeros((sources, LANES), F32)
        for z in range(nz):
            extra = extra + pltpu.roll(packed, LANES - 2 - 4 * z, 1)
        grid = []
        for a in range(sources):
            tile = jnp.zeros((SUB, LANES), F32)
            for part in range(PARTS):
                at = base + (part * per + k) * SUB
                tile = tile + side[a, at : at + SUB, :].astype(F32)
            grid.append(tile[0:tiles, :])
        grid = jnp.concatenate(grid, axis=0)
        grid = grid + dot(to_after, jnp.where(lane < 2, extra, 0.0))
        grid = grid + dot(to_before, jnp.where(lane >= LANES - 2, extra, 0.0))
        inner = dot(grid.T, circle[...])
        cos_part, sin_part = inner[:, :nq], inner[:, nq:]
        turn_cos, turn_sin = twiddle[:, :nq], twiddle[:, nq:]
        real = cos_part * turn_cos - sin_part * turn_sin
        imag = -(sin_part * turn_cos + cos_part * turn_sin)
        outer = dot(short[...], jnp.concatenate([real, imag], axis=1))
        real = outer[:upper, :nq] + outer[upper:, nq:]
        imag = outer[:upper, nq:] - outer[upper:, :nq]
        amount = shift[me * per + k]
        x = jnp.full((upper, nq), -remainder[me * per + k], F32)
        weights = (
            (-1, x * (x + 1.0) * (x + 2.0) / 6.0),
            (0, -(x - 1.0) * (x + 1.0) * (x + 2.0) / 2.0),
            (1, (x - 1.0) * x * (x + 2.0) / 2.0),
            (2, -(x - 1.0) * x * (x + 1.0) / 6.0),
        )
        gain_cos = jnp.zeros((upper, nq), F32)
        gain_sin = jnp.zeros((upper, nq), F32)
        for offset, weight in weights:
            steps = lax.rem(mode * (amount + offset + length), length)
            angle = steps.astype(F32) * (2.0 * math.pi / length)
            gain_cos = gain_cos + weight * jnp.cos(angle)
            gain_sin = gain_sin + weight * jnp.sin(angle)
        rows_out[:, k, :] = real * gain_cos + imag * gain_sin
        rows_out[:, per + k, :] = imag * gain_cos - real * gain_sin
    share = dests // upper
    for d in range(dests):
        out[d] = rows_out[d // share, 0 : 2 * per, :].astype(BF16)


def pick(values, index):
    chosen = values[0]
    for i, value in enumerate(values[1:]):
        chosen = jnp.where(index == i + 1, value, chosen)
    return chosen


def route_kernel(size, middle, inner, where, *rest):
    count = (len(rest) - 1 - size)
    sources, outs, sorted_rows = rest[:count], rest[count:-1], rest[-1]
    for i, source in enumerate(sources):
        value = source[...]
        for m in range(middle):
            for dest in range(size):
                at = (m * size + dest) * inner
                to = (i * middle + m) * inner
                sorted_rows[dest, to : to + inner, :] = value[at : at + inner, :]
    choices = [sorted_rows[dest] for dest in range(size)]
    index = where()
    for offset, out in enumerate(outs):
        out[...] = pick(choices, lax.rem(index + offset, size))


def couple_kernel(per, local, columns, kernel, *rest):
    outs, lines = rest[:-1], rest[-1]
    sources, _, nq = columns.shape
    total = sources * per
    me = lax.axis_index("rad") * lax.axis_size("azi") + lax.axis_index("azi")
    offset = lax.rem(me * local, nq)
    row, col = row_iota((total, total)), lane_iota((total, total))
    spread = (row == lax.rem(col, sources) * per + col // sources).astype(F32)
    lines[...] = columns[...].astype(F32)
    lane = lane_iota((total, nq))
    sides = []
    for c in range(2):
        stacked = jnp.concatenate([lines[:, c * per + k, :] for k in range(per)], axis=0)
        ordered = jnp.dot(spread, stacked, preferred_element_type=F32)
        sides.append(pltpu.roll(ordered, lax.rem(nq - offset + c * local, nq), 1))
    weights = jnp.where(lane < local, sides[0], sides[1]).astype(BF16)
    result = jnp.zeros((total, nq), F32)
    for m in range(local):
        product = jnp.dot(kernel[m], weights, preferred_element_type=F32)
        result = jnp.where((lane == m) | (lane == local + m), product, result)
    rad = lax.axis_index("rad")
    share = total // len(outs)
    slabs = [result[i * share : (i + 1) * share, :] for i in range(len(outs))]
    for offset, out in enumerate(outs):
        out[...] = pick(slabs, lax.rem(rad + offset, len(outs)))


def inverse_kernel(per, local, fast, *rest):
    blocks, (circle, twiddle, mixed, out) = rest[:-4], rest[-4:]
    slow = len(blocks)
    nq = circle.shape[0]
    length = nq * LANES
    share = nq // local
    rad_count = lax.axis_size("rad")
    count = slow * fast * rad_count
    dot = functools.partial(jnp.dot, precision=EXACT, preferred_element_type=F32)
    block_id = row_iota((count, nq))
    first = (block_id == 0) & (lane_iota((count, nq)) % local == 0)
    factor = jnp.where(first, 1.0, 2.0) / length
    azi, rad = lax.axis_index("azi"), lax.axis_index("rad")
    place = lane_iota((count, count))
    from_rad = lax.rem(rad - place % rad_count + rad_count, rad_count)
    from_fast = lax.rem(azi % fast - place // rad_count % fast + fast, fast)
    from_slow = lax.rem(azi // fast - place // (rad_count * fast) + slow, slow)
    source = (from_rad * slow + from_slow) * fast + from_fast
    order = (source == row_iota((count, count))).astype(F32)
    for k in range(per):
        picked = [
            ref[pl.ds(k, fast * rad_count, stride=per), :] if per > 1 else ref[...] for ref in blocks
        ]
        values = dot(order, jnp.concatenate(picked, axis=0))
        values = values * factor
        real, imag = [], []
        for h in range(share):
            chosen = jnp.where(block_id % share == h, values, 0.0)
            mid = dot(chosen.T, mixed[...])
            top, bottom = mid[0:local, :], mid[local : 2 * local, :]
            real.append(top[:, :LANES] - bottom[:, LANES:])
            imag.append(top[:, LANES:] + bottom[:, :LANES])
        real = jnp.concatenate(real, axis=0)
        imag = jnp.concatenate(imag, axis=0)
        turn_cos, turn_sin = twiddle[:, :LANES], twiddle[:, LANES:]
        turned = jnp.concatenate(
            [real * turn_cos - imag * turn_sin, -(real * turn_sin + imag * turn_cos)], axis=0
        )
        wave = dot(circle[...], turned)
        for q in range(nq):
            out[k : k + 1, q * LANES : (q + 1) * LANES] = wave[q : q + 1, :]


def cos_sin(rows, columns, length):
    steps = np.outer(rows, columns) % length
    angle = 2.0 * np.pi * steps / length
    return np.cos(angle).astype(np.float32), np.sin(angle).astype(np.float32)


def call(body, out_shape, in_specs=None, out_specs=None, scratch=(), name=None, **cost):
    kernel = pl.pallas_call(
        body,
        out_shape=out_shape,
        **({} if in_specs is None else {"in_specs": in_specs}),
        **({} if out_specs is None else {"out_specs": out_specs}),
        scratch_shapes=list(scratch),
        cost_estimate=pl.CostEstimate(**{"flops": 0, "bytes_accessed": 0, "transcendentals": 0, **cost}),
    )

    def run(*operands):
        near = [
            x if x.ndim == 1 or name == "load" else pltpu.with_memory_space_constraint(x, pltpu.VMEM)
            for x in operands
        ]
        return kernel(*near)

    return run


def exchange(array, axes):
    return lax.all_to_all(array, axes, 0, 0, tiled=True)


def shape_of(shape, dtype=F32):
    return jax.ShapeDtypeStruct(shape, dtype)


def body(density, radial_velocity, azimuthal_velocity, cycle_shift, remainder, kernel):
    nz, slab, seg = density.shape
    azi, rad = lax.axis_size("azi"), lax.axis_size("rad")
    devices = azi * rad
    per = slab // azi
    tiles = seg // LANES
    length = seg * azi
    nq = length // LANES
    local = kernel.shape[0]
    modes = local * devices
    upper = modes // nq
    width = seg + LANES
    group = nz * per
    stride = -(-3 * group // SUB) * SUB
    rows = tiles * stride + PARTS * per * SUB + SUB
    fast = min(4, azi)
    slow = azi // fast
    both = ("rad", "azi")
    vmem, smem = pl.BlockSpec(memory_space=pltpu.VMEM), pl.BlockSpec(memory_space=pltpu.SMEM)

    fields = (density, radial_velocity, azimuthal_velocity)
    anywhere = pl.BlockSpec(memory_space=pl.ANY)
    edge = pltpu.VMEM((3, nz, 2, seg), F32)
    *fields, tail, head = call(
        load_kernel,
        (*(pltpu.VMEM((nz, slab, seg), F32) for _ in range(3)), edge, edge),
        in_specs=[anywhere] * 3,
        scratch=(pltpu.SemaphoreType.DMA((3,)),),
        name="load",
        bytes_accessed=12 * nz * slab * seg,
    )(*fields)
    low = lax.ppermute(tail, "rad", [(i, (i + 1) % rad) for i in range(rad)])
    high = lax.ppermute(head, "rad", [((i + 1) % rad, i) for i in range(rad)])
    bulk = call(
        functools.partial(hydro_kernel, per),
        shape_of((azi, rows, LANES), BF16),
        out_specs=anywhere,
        scratch=(
            pltpu.VMEM((3, nz, slab + 4 * SUB, width), F32),
            pltpu.VMEM((3, nz, slab + 4 * SUB, width), F32),
            pltpu.VMEM((azi, rows, LANES), F32),
            pltpu.VMEM((azi, rows, LANES), BF16),
            pltpu.SemaphoreType.DMA((slab // SUB,)),
        ),
        name="hydro",
        flops=100 * 3 * nz * slab * seg,
        bytes_accessed=24 * nz * slab * seg,
    )(*fields, low, high)

    bulk = exchange(bulk, "azi")

    k_id, l_id = np.arange(nq), np.arange(LANES)
    circle = np.concatenate(cos_sin(k_id, k_id, nq), axis=1)
    twiddle = np.concatenate(cos_sin(l_id, k_id, length), axis=1)
    short = np.concatenate(cos_sin(np.arange(upper), l_id, LANES), axis=0)
    spectrum = call(
        functools.partial(forward_kernel, per, nz, modes),
        pltpu.VMEM((devices, 2 * per, nq), BF16),
        in_specs=[smem, smem, vmem, vmem, vmem, vmem],
        scratch=(pltpu.VMEM((upper, 2 * per, nq), F32),),
        name="forward",
        flops=100_000_000,
        bytes_accessed=1_000_000,
    )(cycle_shift, remainder, bulk, jnp.asarray(circle), jnp.asarray(twiddle), jnp.asarray(short))
    columns = exchange(spectrum, both)
    blocks = call(
        functools.partial(couple_kernel, per, local),
        tuple(pltpu.VMEM((azi * per, nq), F32) for _ in range(rad)),
        scratch=(pltpu.VMEM((devices, 2 * per, nq), F32),),
        name="couple",
        flops=100_000_000,
        bytes_accessed=1_000_000,
    )(columns, kernel)

    def hop(buffers, axis, size, step):
        around = range(lax.axis_size(axis))
        return [buffers[0]] + [
            lax.ppermute(
                buffers[o],
                axis,
                [(i, i + ((i // step % size + o) % size - i // step % size) * step) for i in around],
            )
            for o in range(1, size)
        ]

    blocks = hop(blocks, "rad", rad, 1)
    for size, middle, where, step, name in (
        (fast, slow, lambda: lax.axis_index("azi") % fast, 1, "fast"),
        (slow, fast * rad // fast, lambda: lax.axis_index("azi") // fast, fast, "slow"),
    ):
        lines = len(blocks) * blocks[0].shape[0] // size
        middle = blocks[0].shape[0] // (size * per)
        blocks = call(
            functools.partial(route_kernel, size, middle, per, where),
            tuple(pltpu.VMEM((lines, nq), F32) for _ in range(size)),
            scratch=(pltpu.VMEM((size, lines, nq), F32),),
            name="route_" + name,
            bytes_accessed=100_000,
        )(*blocks)
        blocks = hop(blocks, "azi", size, step)
    j_of_block = np.arange(devices) * local // nq
    mixed = np.concatenate(cos_sin(j_of_block, l_id, LANES), axis=1)
    turn = np.concatenate(cos_sin(k_id, l_id, length), axis=1)
    potential = call(
        functools.partial(inverse_kernel, per, local, fast),
        shape_of((per, length)),
        name="inverse",
        flops=100_000_000,
        bytes_accessed=1_000_000,
    )(*blocks, jnp.asarray(circle), jnp.asarray(turn), jnp.asarray(mixed))

    moved, top = call(
        functools.partial(advect_kernel, per, nz),
        (pltpu.VMEM((azi, 3 * group, seg), BF16), pltpu.VMEM((SUB, LANES), F32)),
        in_specs=[smem, smem, vmem],
        scratch=(
            pltpu.VMEM((3, nq, group, LANES), F32),
            pltpu.VMEM((3, nq, group, LANES), F32),
            pltpu.VMEM((3, azi, group, LANES), F32),
        ),
        name="advect",
        flops=50 * 3 * nz * slab * seg,
        bytes_accessed=12 * nz * slab * seg,
    )(cycle_shift, remainder, bulk)
    moved = exchange(moved, "azi")
    results = call(
        functools.partial(settle_kernel, per),
        tuple(shape_of((nz, slab, seg)) for _ in range(3)),
        name="settle",
        flops=20 * 3 * nz * slab * seg,
        bytes_accessed=18 * nz * slab * seg,
    )(moved, top)
    return (*results, potential)


def solution(mesh):
    split = P(None, "rad", "azi")
    in_specs = (split, split, split, P("rad"), P("rad"), P(("rad", "azi"), None, None))
    out_specs = (split, split, split, P(("rad", "azi"), None))

    return jax.shard_map(body, mesh=mesh, in_specs=in_specs, out_specs=out_specs, check_vma=False)
```

```python
import functools
import math

import jax
import jax.numpy as jnp
import numpy as np
from jax import lax
from jax.experimental import pallas as pl
from jax.experimental.pallas import tpu as pltpu
from jax.sharding import PartitionSpec as P


RADIAL_COURANT = 0.3
VISCOSITY = 0.08
LANES = 128
SUB = 8
EXACT = lax.Precision.HIGHEST
F32 = jnp.float32
BF16 = jnp.bfloat16

POWER = 12
TOP = 2.0**10.5
GAIN = 1.25


def encode(value, scale):
    scaled = value * scale
    second = scaled * scaled
    fourth = second * second
    size = fourth * fourth * fourth
    return jnp.where(scaled < 0.0, -size, size)


def decode(code, scale):
    size = jnp.abs(code)
    root = jnp.exp2(jnp.log2(jnp.maximum(size, 1e-37)) * (1.0 / POWER)) * scale
    return jnp.where(size < 2e-38, 0.0, jnp.where(code < 0.0, -root, root))


def row_iota(shape):
    return lax.broadcasted_iota(jnp.int32, shape, 0)


def lane_iota(shape):
    return lax.broadcasted_iota(jnp.int32, shape, 1)


def side_rows(per, tiles):
    return -(-(per * tiles + per) // SUB) * SUB


def load_kernel(rho, ur, up, rho_near, ur_near, up_near, tail, head, sems):
    slab = rho.shape[1]
    pairs = ((rho, rho_near), (ur, ur_near), (up, up_near))
    copies = [pltpu.make_async_copy(far, near, sems.at[c]) for c, (far, near) in enumerate(pairs)]
    for copy in copies:
        copy.start()
    for c, (_, near) in enumerate(pairs):
        copies[c].wait()
        tail[c] = near[:, slab - 2 :, :]
        head[c] = near[:, 0:2, :]


def hydro_kernel(per, rho, ur, up, low, high, bulk, surf, field, stage, block, narrow, sems):
    nz, slab, seg = rho.shape
    width = seg + LANES
    first = 2 * SUB
    last_tile = slab // SUB + 2
    tiles = seg // LANES
    rad = lax.axis_index("rad")
    rad_count = lax.axis_size("rad")
    total = slab * rad_count
    for c, ref in enumerate((rho, ur, up)):
        for z in range(nz):
            field[c, z, SUB : slab + 3 * SUB, seg:width] = jnp.zeros((slab + 2 * SUB, LANES), F32)
            field[c, z, first : first + slab, 0:seg] = ref[z]
            inner = jnp.broadcast_to(ref[z, 0:1, :], (2, seg))
            outer = jnp.broadcast_to(ref[z, slab - 1 : slab, :], (2, seg))
            field[c, z, first - 2 : first, 0:seg] = jnp.where(rad == 0, inner, low[c, z])
            field[c, z, first + slab : first + slab + 2, 0:seg] = jnp.where(
                rad == rad_count - 1, outer, high[c, z]
            )
    sub = row_iota((SUB, width))

    def rates_at(ref, tile, z):
        cycle = rad * slab - first + tile * SUB + row_iota((SUB, LANES))
        radius = 1.0 + 4.0 * (cycle.astype(F32) + 0.5) / total
        power = 1.0 / (radius * jnp.sqrt(radius))
        wide = lambda x: jnp.concatenate([x] * (width // LANES), axis=1)
        courant = wide(0.5 * (0.3 / radius))
        coriolis, epicycle = wide(0.2 * power), wide(0.05 * power)
        here = pl.ds(pl.multiple_of(tile * SUB, SUB), SUB)
        before = pl.ds(pl.multiple_of((tile - 1) * SUB, SUB), SUB)
        after = pl.ds(pl.multiple_of((tile + 1) * SUB, SUB), SUB)
        z_up, z_down = min(z + 1, nz - 1), max(z - 1, 0)
        center, rad_diff, azi_diff, spread = [], [], [], []
        for c in range(3):
            cur = ref[c, z, here, :]
            inward = pltpu.roll(jnp.where(sub == SUB - 1, ref[c, z, before, :], cur), 1, 0)
            outward = pltpu.roll(jnp.where(sub == 0, ref[c, z, after, :], cur), SUB - 1, 0)
            ahead = pltpu.roll(cur, width - 1, 1)
            behind = pltpu.roll(cur, 1, 1)
            near = ref[c, z_up, here, :] + ref[c, z_down, here, :] + inward + outward + ahead + behind
            spread.append(VISCOSITY * near - (6.0 * VISCOSITY) * cur)
            rad_diff.append(outward - inward)
            azi_diff.append(ahead - behind)
            center.append(cur)
        half = 0.5 * RADIAL_COURANT
        return center, (
            spread[0] - (half * rad_diff[1] + courant * azi_diff[2]),
            coriolis * center[2] - half * rad_diff[0] + spread[1],
            spread[2] - epicycle * center[1] - courant * azi_diff[0],
        )

    def first_section(tile, carry):
        for z in range(nz):
            center, change = rates_at(field, tile, z)
            for c in range(3):
                stage[c, z, pl.ds(pl.multiple_of(tile * SUB, SUB), SUB), :] = center[c] + change[c]
        return carry

    lax.fori_loop(1, last_tile + 1, first_section, 0)

    @pl.when(rad == 0)
    def _():
        for c in range(3):
            for z in range(nz):
                stage[c, z, first - 1 : first, :] = stage[c, z, first : first + 1, :]

    @pl.when(rad == rad_count - 1)
    def _():
        for c in range(3):
            for z in range(nz):
                stage[c, z, first + slab : first + slab + 1, :] = stage[
                    c, z, first + slab - 1 : first + slab, :
                ]

    def second_section(tile, largest):
        here = pl.ds(pl.multiple_of(tile * SUB, SUB), SUB)
        for z in range(nz):
            center, change = rates_at(stage, tile, z)
            for c in range(3):
                value = 0.5 * field[c, z, here, :] + 0.5 * (center[c] + change[c])
                field[c, z, here, :] = value
                largest = jnp.maximum(largest, jnp.abs(value))
        return largest

    largest = lax.fori_loop(2, last_tile, second_section, jnp.zeros((SUB, width), F32))
    peak = jnp.maximum(jnp.max(largest, keepdims=True), 1e-30)
    scale = TOP / peak
    dests = SUB // per
    stride = -(-3 * nz * per // SUB) * SUB

    def send(index):
        at = pl.ds(index * dests, dests)
        return pltpu.make_async_copy(narrow.at[at], bulk.at[at], sems.at[index])

    def pack(tile, carry):
        here = pl.ds(pl.multiple_of(tile * SUB, SUB), SUB)
        overflow = jnp.zeros((SUB, LANES), F32)
        column = jnp.zeros((SUB, seg), F32)
        for c in range(3):
            for z in range(nz):
                value = field[c, z, here, 0:seg]
                if c == 0:
                    column = column + value
                code = encode(value, scale)
                plane = c * nz + z
                for d in range(dests):
                    for b in range(tiles):
                        line = b * stride + plane * per
                        block[(tile - 2) * dests + d, line : line + per, :] = code[
                            d * per : (d + 1) * per, b * LANES : (b + 1) * LANES
                        ]
                overflow = overflow + pltpu.roll(field[c, z, here, seg:width], 2 + 4 * plane, 1)
        overflow = jnp.where(lane_iota((SUB, LANES)) < LANES // 2, overflow, peak)
        for d in range(dests):
            dest = (tile - 2) * dests + d
            for k in range(per):
                row = d * per + k
                for b in range(tiles):
                    surf[dest, k * tiles + b : k * tiles + b + 1, :] = column[
                        row : row + 1, b * LANES : (b + 1) * LANES
                    ]
                line = per * tiles + k
                surf[dest, line : line + 1, :] = overflow[row : row + 1, :]
        for d in range(dests):
            dest = (tile - 2) * dests + d
            narrow[dest] = block[dest].astype(BF16)
        send(tile - 2).start()
        return carry

    lax.fori_loop(2, last_tile, pack, 0)
    for index in range(slab // SUB):
        send(index).wait()


def advect_kernel(per, nz, shift, remainder, bulk, sides, out, top, ring, tapped, over):
    sources = bulk.shape[0]
    count = ring.shape[1]
    tiles = count // sources
    group = nz * per
    stride = -(-3 * group // SUB) * SUB
    me = lax.axis_index("azi")

    def widen(a, peak):
        whole_block = bulk[a].astype(F32)
        packed = sides[a, per * tiles : per * tiles + per, :]
        mine = jnp.where(lane_iota((1, LANES)) >= LANES // 2, packed[0:1, :], 0.0)
        mine = jnp.max(mine, keepdims=True)
        unit = mine * (1.0 / TOP)
        for b in range(tiles):
            value = decode(whole_block[b * stride : (b + 1) * stride, :], unit)
            for c in range(3):
                ring[c, a * tiles + b] = value[c * group : (c + 1) * group, :]
        for c in range(3):
            for z in range(nz):
                turned = pltpu.roll(packed, LANES - 2 - 4 * (c * nz + z), 1)
                over[c, a, z * per : (z + 1) * per, :] = turned
        return jnp.maximum(peak, mine)

    peak = lax.fori_loop(0, sources, widen, jnp.zeros((1, 1), F32))
    top[...] = jnp.broadcast_to(peak, top.shape)
    lane = lane_iota((group, LANES))
    cycle = row_iota((group, LANES)) % per

    def spill(a, carry):
        after = lax.rem((a + 1) * tiles, count)
        before = lax.rem(a * tiles + count - 1, count)
        for c in range(3):
            extra = over[c, a]
            ring[c, after] = ring[c, after] + jnp.where(lane < 2, extra, 0.0)
            ring[c, before] = ring[c, before] + jnp.where(lane >= LANES - 2, extra, 0.0)
        return carry

    lax.fori_loop(0, sources, spill, 0, unroll=4)
    x = jnp.zeros((group, LANES), F32)
    whole, part = [], []
    for k in range(per):
        x = jnp.where(cycle == k, -remainder[me * per + k], x)
        amount = shift[me * per + k]
        whole.append(amount // LANES)
        part.append(lax.rem(amount, LANES))
    w_next = x * (x + 1.0) * (x + 2.0) / 6.0
    w_here = -(x - 1.0) * (x + 1.0) * (x + 2.0) / 2.0
    w_prev = (x - 1.0) * x * (x + 2.0) / 2.0
    w_prev_two = -(x - 1.0) * x * (x + 1.0) / 6.0

    def tap(a, carry):
        before = lax.rem(a * tiles + count - 1, count)
        after = lax.rem((a + 1) * tiles, count)
        for c in range(3):
            line = [ring[c, before]]
            line += [ring[c, a * tiles + b] for b in range(tiles)]
            line += [ring[c, after]]
            for b in range(tiles):
                prv, cur, nxt = line[b : b + 3]
                next_one = pltpu.roll(jnp.where(lane == 0, nxt, cur), LANES - 1, 1)
                prev_one = pltpu.roll(jnp.where(lane == LANES - 1, prv, cur), 1, 1)
                prev_two = pltpu.roll(jnp.where(lane >= LANES - 2, prv, cur), 2, 1)
                tapped[c, a * tiles + b] = (
                    w_next * next_one + w_here * cur + w_prev * prev_one + w_prev_two * prev_two
                )
        return carry

    lax.fori_loop(0, sources, tap, 0)
    scale = (TOP / GAIN) / peak

    def turned_tile(c, k, t):
        source = lax.rem(t - whole[k] + 2 * count, count)
        return pltpu.roll(tapped[c, source], part[k], 1)

    def turn(dest, carry):
        carry = list(carry)
        pieces = [[None] * tiles for _ in range(3)]
        for b in range(tiles):
            t = dest * tiles + b
            for c in range(3):
                joined = jnp.zeros((group, LANES), F32)
                for k in range(per):
                    now = turned_tile(c, k, t)
                    value = jnp.where(lane < part[k], carry[c * per + k], now)
                    joined = value if per == 1 else jnp.where(cycle == k, value, joined)
                    carry[c * per + k] = now
                pieces[c][b] = encode(joined, scale)
        columns = [jnp.concatenate([pieces[c][b] for b in range(tiles)], axis=1) for c in range(3)]
        out[dest] = jnp.concatenate(columns, axis=0).astype(BF16)
        return tuple(carry)

    start = tuple(turned_tile(c, k, -1) for c in range(3) for k in range(per))
    lax.fori_loop(0, sources, turn, start)


def settle_kernel(per, bulk, top, rho, ur, up):
    nz = rho.shape[0]
    sources, _, seg = bulk.shape
    unit = jnp.concatenate([top[0:1, :] * (GAIN / TOP)] * (seg // LANES), axis=1)
    for a in range(sources):
        value = decode(bulk[a].astype(F32), unit)
        for c, ref in enumerate((rho, ur, up)):
            for z in range(nz):
                plane = c * nz + z
                ref[z, a * per : (a + 1) * per, :] = value[plane * per : (plane + 1) * per, :]


def forward_kernel(per, nz, modes, fast, shift, remainder, circle, twiddle, short, *rest):
    rad_count = lax.axis_size("rad")
    hops, outs, (sides, rows_out) = rest[:fast], rest[fast:-2], rest[-2:]
    azi = lax.axis_index("azi")
    for o_fast, hop in enumerate(hops):
        for o_slow in range(hop.shape[0]):
            from_slow = lax.rem(azi // fast - o_slow + hop.shape[0], hop.shape[0])
            from_fast = lax.rem(azi % fast - o_fast + fast, fast)
            sides[from_slow * fast + from_fast] = hop[o_slow]
    sources = sides.shape[0]
    nq = circle.shape[0]
    tiles = nq // sources
    length = nq * LANES
    upper = modes // nq
    me = lax.axis_index("azi")
    lane = lane_iota((sources, LANES))
    q_id, a_id = row_iota((nq, sources)), lane_iota((nq, sources))
    to_after = (q_id == lax.rem((a_id + 1) * tiles, nq)).astype(F32)
    to_before = (q_id == lax.rem(a_id * tiles + nq - 1, nq)).astype(F32)
    mode = row_iota((upper, nq)) * nq + lane_iota((upper, nq))
    dot = functools.partial(jnp.dot, precision=EXACT, preferred_element_type=F32)
    for k in range(per):
        packed = sides[:, per * tiles + k, :]
        extra = jnp.zeros((sources, LANES), F32)
        for z in range(nz):
            extra = extra + pltpu.roll(packed, LANES - 2 - 4 * z, 1)
        grid = sides[:, k * tiles : (k + 1) * tiles, :].reshape(nq, LANES)
        grid = grid + dot(to_after, jnp.where(lane < 2, extra, 0.0))
        grid = grid + dot(to_before, jnp.where(lane >= LANES - 2, extra, 0.0))
        inner = dot(grid.T, circle[...])
        cos_part, sin_part = inner[:, :nq], inner[:, nq:]
        turn_cos, turn_sin = twiddle[:, :nq], twiddle[:, nq:]
        real = cos_part * turn_cos - sin_part * turn_sin
        imag = -(sin_part * turn_cos + cos_part * turn_sin)
        outer = dot(short[...], jnp.concatenate([real, imag], axis=1))
        real = outer[:upper, :nq] + outer[upper:, nq:]
        imag = outer[:upper, nq:] - outer[upper:, :nq]
        amount = shift[me * per + k]
        x = jnp.full((upper, nq), -remainder[me * per + k], F32)
        weights = (
            (-1, x * (x + 1.0) * (x + 2.0) / 6.0),
            (0, -(x - 1.0) * (x + 1.0) * (x + 2.0) / 2.0),
            (1, (x - 1.0) * x * (x + 2.0) / 2.0),
            (2, -(x - 1.0) * x * (x + 1.0) / 6.0),
        )
        gain_cos = jnp.zeros((upper, nq), F32)
        gain_sin = jnp.zeros((upper, nq), F32)
        for offset, weight in weights:
            steps = lax.rem(mode * (amount + offset + length), length)
            angle = steps.astype(F32) * (2.0 * math.pi / length)
            gain_cos = gain_cos + weight * jnp.cos(angle)
            gain_sin = gain_sin + weight * jnp.sin(angle)
        rows_out[:, k, :] = real * gain_cos + imag * gain_sin
        rows_out[:, per + k, :] = imag * gain_cos - real * gain_sin
    share = rad_count * sources // upper
    width = upper // rad_count
    rad = lax.axis_index("rad")
    slabs = [
        jnp.concatenate(
            [rows_out[i * width + a // share].astype(BF16).astype(F32) for a in range(sources)], axis=0
        )
        for i in range(rad_count)
    ]
    for offset, out in enumerate(outs):
        out[...] = pick(slabs, lax.rem(rad + offset, rad_count))


def pick(values, index):
    chosen = values[0]
    for i, value in enumerate(values[1:]):
        chosen = jnp.where(index == i + 1, value, chosen)
    return chosen


def route_kernel(size, middle, inner, where, *rest):
    count = (len(rest) - 1 - size)
    sources, outs, sorted_rows = rest[:count], rest[count:-1], rest[-1]
    for i, source in enumerate(sources):
        value = source[...]
        for m in range(middle):
            for dest in range(size):
                at = (m * size + dest) * inner
                to = (i * middle + m) * inner
                sorted_rows[dest, to : to + inner, :] = value[at : at + inner, :]
    choices = [sorted_rows[dest] for dest in range(size)]
    index = where()
    for offset, out in enumerate(outs):
        out[...] = pick(choices, lax.rem(index + offset, size))


def arrival_source(slow, fast, axis_iota):
    rad_count = lax.axis_size("rad")
    azi, rad = lax.axis_index("azi"), lax.axis_index("rad")
    from_rad = lax.rem(rad - axis_iota % rad_count + rad_count, rad_count)
    from_fast = lax.rem(azi % fast - axis_iota // rad_count % fast + fast, fast)
    from_slow = lax.rem(azi // fast - axis_iota // (rad_count * fast) % slow + slow, slow)
    return (from_rad * slow + from_slow) * fast + from_fast


def couple_kernel(per, local, fast, slow, kernel, *rest):
    columns, outs = rest[:slow], rest[slow:]
    rad_count = lax.axis_size("rad")
    sources = slow * fast * rad_count
    nq = columns[0].shape[1]
    total = sources * per
    me = lax.axis_index("rad") * lax.axis_size("azi") + lax.axis_index("azi")
    offset = lax.rem(me * local, nq)
    row, col = row_iota((total, total)), lane_iota((total, total))
    source = arrival_source(slow, fast, col % sources)
    spread = (row == source * per + col // sources).astype(F32)
    lane = lane_iota((total, nq))
    sides = []
    for c in range(2):
        stacked = jnp.concatenate(
            [
                ref[pl.ds(c * per + k, fast * rad_count, stride=2 * per), :]
                for k in range(per)
                for ref in columns
            ],
            axis=0,
        )
        ordered = jnp.dot(spread, stacked, preferred_element_type=F32)
        sides.append(pltpu.roll(ordered, lax.rem(nq - offset + c * local, nq), 1))
    weights = jnp.where(lane < local, sides[0], sides[1]).astype(BF16)
    result = jnp.zeros((total, nq), F32)
    for m in range(local):
        product = jnp.dot(kernel[m], weights, preferred_element_type=F32)
        result = jnp.where((lane == m) | (lane == local + m), product, result)
    rad = lax.axis_index("rad")
    share = total // len(outs)
    slabs = [result[i * share : (i + 1) * share, :] for i in range(len(outs))]
    for offset, out in enumerate(outs):
        out[...] = pick(slabs, lax.rem(rad + offset, len(outs)))


def inverse_kernel(per, local, fast, *rest):
    blocks, (circle, twiddle, mixed, out) = rest[:-4], rest[-4:]
    slow = len(blocks)
    nq = circle.shape[0]
    length = nq * LANES
    share = nq // local
    rad_count = lax.axis_size("rad")
    count = slow * fast * rad_count
    dot = functools.partial(jnp.dot, precision=EXACT, preferred_element_type=F32)
    block_id = row_iota((count, nq))
    first = (block_id == 0) & (lane_iota((count, nq)) % local == 0)
    factor = jnp.where(first, 1.0, 2.0) / length
    source = arrival_source(slow, fast, lane_iota((count, count)))
    order = (source == row_iota((count, count))).astype(F32)
    for k in range(per):
        picked = [
            ref[pl.ds(k, fast * rad_count, stride=per), :] if per > 1 else ref[...] for ref in blocks
        ]
        values = dot(order, jnp.concatenate(picked, axis=0))
        values = values * factor
        real, imag = [], []
        for h in range(share):
            chosen = jnp.where(block_id % share == h, values, 0.0)
            mid = dot(chosen.T, mixed[...])
            top, bottom = mid[0:local, :], mid[local : 2 * local, :]
            real.append(top[:, :LANES] - bottom[:, LANES:])
            imag.append(top[:, LANES:] + bottom[:, :LANES])
        real = jnp.concatenate(real, axis=0)
        imag = jnp.concatenate(imag, axis=0)
        turn_cos, turn_sin = twiddle[:, :LANES], twiddle[:, LANES:]
        turned = jnp.concatenate(
            [real * turn_cos - imag * turn_sin, -(real * turn_sin + imag * turn_cos)], axis=0
        )
        wave = dot(circle[...], turned)
        for q in range(nq):
            out[k : k + 1, q * LANES : (q + 1) * LANES] = wave[q : q + 1, :]


def cos_sin(rows, columns, length):
    steps = np.outer(rows, columns) % length
    angle = 2.0 * np.pi * steps / length
    return np.cos(angle).astype(np.float32), np.sin(angle).astype(np.float32)


def call(body, out_shape, in_specs=None, out_specs=None, scratch=(), name=None, **cost):
    kernel = pl.pallas_call(
        body,
        out_shape=out_shape,
        **({} if in_specs is None else {"in_specs": in_specs}),
        **({} if out_specs is None else {"out_specs": out_specs}),
        scratch_shapes=list(scratch),
        cost_estimate=pl.CostEstimate(**{"flops": 0, "bytes_accessed": 0, "transcendentals": 0, **cost}),
    )

    def run(*operands):
        near = [
            x if x.ndim == 1 or name == "load" else pltpu.with_memory_space_constraint(x, pltpu.VMEM)
            for x in operands
        ]
        return kernel(*near)

    return run


def exchange(array, axes):
    return lax.all_to_all(array, axes, 0, 0, tiled=True)


def shape_of(shape, dtype=F32):
    return jax.ShapeDtypeStruct(shape, dtype)


def body(density, radial_velocity, azimuthal_velocity, cycle_shift, remainder, kernel):
    nz, slab, seg = density.shape
    azi, rad = lax.axis_size("azi"), lax.axis_size("rad")
    devices = azi * rad
    per = slab // azi
    tiles = seg // LANES
    length = seg * azi
    nq = length // LANES
    local = kernel.shape[0]
    modes = local * devices
    upper = modes // nq
    width = seg + LANES
    group = nz * per
    stride = -(-3 * group // SUB) * SUB
    rows = tiles * stride
    side = side_rows(per, tiles)
    fast = min(4, azi)
    slow = azi // fast
    vmem, smem = pl.BlockSpec(memory_space=pltpu.VMEM), pl.BlockSpec(memory_space=pltpu.SMEM)

    fields = (density, radial_velocity, azimuthal_velocity)
    anywhere = pl.BlockSpec(memory_space=pl.ANY)
    edge = pltpu.VMEM((3, nz, 2, seg), F32)
    *fields, tail, head = call(
        load_kernel,
        (*(pltpu.VMEM((nz, slab, seg), F32) for _ in range(3)), edge, edge),
        in_specs=[anywhere] * 3,
        scratch=(pltpu.SemaphoreType.DMA((3,)),),
        name="load",
        bytes_accessed=12 * nz * slab * seg,
    )(*fields)
    low = lax.ppermute(tail, "rad", [(i, (i + 1) % rad) for i in range(rad)])
    high = lax.ppermute(head, "rad", [((i + 1) % rad, i) for i in range(rad)])
    bulk, surf = call(
        functools.partial(hydro_kernel, per),
        (shape_of((azi, rows, LANES), BF16), pltpu.VMEM((azi, side, LANES), F32)),
        out_specs=(anywhere, vmem),
        scratch=(
            pltpu.VMEM((3, nz, slab + 4 * SUB, width), F32),
            pltpu.VMEM((3, nz, slab + 4 * SUB, width), F32),
            pltpu.VMEM((azi, rows, LANES), F32),
            pltpu.VMEM((azi, rows, LANES), BF16),
            pltpu.SemaphoreType.DMA((slab // SUB,)),
        ),
        name="hydro",
        flops=100 * 3 * nz * slab * seg,
        bytes_accessed=24 * nz * slab * seg,
    )(*fields, low, high)

    def hop(buffers, axis, size, step):
        around = range(lax.axis_size(axis))
        return [buffers[0]] + [
            lax.ppermute(
                buffers[o],
                axis,
                [(i, i + ((i // step % size + o) % size - i // step % size) * step) for i in around],
            )
            for o in range(1, size)
        ]

    def route(buffers, size, inner, step, name):
        count = buffers[0].shape[0]
        lines = len(buffers) * count // size
        where = lambda: lax.axis_index("azi") // step % size
        buffers = call(
            functools.partial(route_kernel, size, count // (size * inner), inner, where),
            tuple(pltpu.VMEM((lines, LANES), F32) for _ in range(size)),
            scratch=(pltpu.VMEM((size, lines, LANES), F32),),
            name="route_" + name,
            bytes_accessed=100_000,
        )(*buffers)
        return hop(buffers, "azi", size, step)

    surf = [surf.reshape(azi * side, LANES)]
    surf = route(surf, slow, fast * side, fast, "surf_slow")
    bulk = exchange(bulk, "azi")
    surf = route(surf, fast, side, 1, "surf_fast")
    surf = [x.reshape(slow, side, LANES) for x in surf]

    k_id, l_id = np.arange(nq), np.arange(LANES)
    circle = np.concatenate(cos_sin(k_id, k_id, nq), axis=1)
    twiddle = np.concatenate(cos_sin(l_id, k_id, length), axis=1)
    short = np.concatenate(cos_sin(np.arange(upper), l_id, LANES), axis=0)
    *spectrum, sides = call(
        functools.partial(forward_kernel, per, nz, modes, fast),
        (
            *(pltpu.VMEM((azi * 2 * per, nq), F32) for _ in range(rad)),
            pltpu.VMEM((azi, side, LANES), F32),
        ),
        in_specs=[smem, smem] + [vmem] * (3 + fast),
        scratch=(pltpu.VMEM((upper, 2 * per, nq), F32),),
        name="forward",
        flops=100_000_000,
        bytes_accessed=1_000_000,
    )(cycle_shift, remainder, jnp.asarray(circle), jnp.asarray(twiddle), jnp.asarray(short), *surf)
    columns = hop(spectrum, "rad", rad, 1)
    columns = route(columns, fast, 2 * per, 1, "column_fast")
    columns = route(columns, slow, 2 * per, fast, "column_slow")
    blocks = call(
        functools.partial(couple_kernel, per, local, fast, slow),
        tuple(pltpu.VMEM((azi * per, nq), F32) for _ in range(rad)),
        name="couple",
        flops=100_000_000,
        bytes_accessed=1_000_000,
    )(kernel, *columns)
    blocks = hop(blocks, "rad", rad, 1)
    blocks = route(blocks, fast, per, 1, "block_fast")
    blocks = route(blocks, slow, per, fast, "block_slow")
    j_of_block = np.arange(devices) * local // nq
    mixed = np.concatenate(cos_sin(j_of_block, l_id, LANES), axis=1)
    turn = np.concatenate(cos_sin(k_id, l_id, length), axis=1)
    potential = call(
        functools.partial(inverse_kernel, per, local, fast),
        shape_of((per, length)),
        name="inverse",
        flops=100_000_000,
        bytes_accessed=1_000_000,
    )(*blocks, jnp.asarray(circle), jnp.asarray(turn), jnp.asarray(mixed))

    moved, top = call(
        functools.partial(advect_kernel, per, nz),
        (pltpu.VMEM((azi, 3 * group, seg), BF16), pltpu.VMEM((SUB, LANES), F32)),
        in_specs=[smem, smem, vmem, vmem],
        scratch=(
            pltpu.VMEM((3, nq, group, LANES), F32),
            pltpu.VMEM((3, nq, group, LANES), F32),
            pltpu.VMEM((3, azi, group, LANES), F32),
        ),
        name="advect",
        flops=50 * 3 * nz * slab * seg,
        bytes_accessed=12 * nz * slab * seg,
    )(cycle_shift, remainder, bulk, sides)
    moved = exchange(moved, "azi")
    results = call(
        functools.partial(settle_kernel, per),
        tuple(shape_of((nz, slab, seg)) for _ in range(3)),
        name="settle",
        flops=20 * 3 * nz * slab * seg,
        bytes_accessed=18 * nz * slab * seg,
    )(moved, top)
    return (*results, potential)


def solution(mesh):
    split = P(None, "rad", "azi")
    in_specs = (split, split, split, P("rad"), P("rad"), P(("rad", "azi"), None, None))
    out_specs = (split, split, split, P(("rad", "azi"), None))

    return jax.shard_map(body, mesh=mesh, in_specs=in_specs, out_specs=out_specs, check_vma=False)
```

```python
import functools
import math

import jax
import jax.numpy as jnp
import numpy as np
from jax import lax
from jax.experimental import pallas as pl
from jax.experimental.pallas import tpu as pltpu
from jax.sharding import PartitionSpec as P


RADIAL_COURANT = 0.3
VISCOSITY = 0.08
LANES = 128
SUB = 8
EXACT = lax.Precision.HIGHEST
F32 = jnp.float32
BF16 = jnp.bfloat16

POWER = 12
TOP = 2.0**10.5
GAIN = 1.25


def encode(value, scale):
    scaled = value * scale
    second = scaled * scaled
    fourth = second * second
    size = fourth * fourth * fourth
    return jnp.where(scaled < 0.0, -size, size)


def decode(code, scale):
    root = lax.exp2(lax.log(jnp.abs(code)) * (1.0 / (POWER * math.log(2.0)))) * scale
    return jnp.where(code < 0.0, -root, root)


def sent_to(place, offset, size, ring):
    return (place + offset) % size if ring else place ^ offset


def came_from(place, offset, size, ring):
    return (place - offset + size) % size if ring else place ^ offset


def row_iota(shape):
    return lax.broadcasted_iota(jnp.int32, shape, 0)


def lane_iota(shape):
    return lax.broadcasted_iota(jnp.int32, shape, 1)


def side_rows(per, tiles):
    return -(-(per * tiles + per) // SUB) * SUB


def load_kernel(rho, ur, up, rho_near, ur_near, up_near, tail, head, sems):
    slab = rho.shape[1]
    pairs = ((rho, rho_near), (ur, ur_near), (up, up_near))
    copies = [pltpu.make_async_copy(far, near, sems.at[c]) for c, (far, near) in enumerate(pairs)]
    for copy in copies:
        copy.start()
    for c, (_, near) in enumerate(pairs):
        copies[c].wait()
        tail[c] = near[:, slab - 2 :, :]
        head[c] = near[:, 0:2, :]


def hydro_kernel(per, rho, ur, up, low, high, bulk, surf, field, stage, block, narrow, sems):
    nz, slab, seg = rho.shape
    width = seg + LANES
    first = 2 * SUB
    last_tile = slab // SUB + 2
    tiles = seg // LANES
    rad = lax.axis_index("rad")
    rad_count = lax.axis_size("rad")
    total = slab * rad_count
    for c, ref in enumerate((rho, ur, up)):
        for z in range(nz):
            field[c, z, SUB : slab + 3 * SUB, seg:width] = jnp.zeros((slab + 2 * SUB, LANES), F32)
            field[c, z, first : first + slab, 0:seg] = ref[z]
            inner = jnp.broadcast_to(ref[z, 0:1, :], (2, seg))
            outer = jnp.broadcast_to(ref[z, slab - 1 : slab, :], (2, seg))
            field[c, z, first - 2 : first, 0:seg] = jnp.where(rad == 0, inner, low[c, z])
            field[c, z, first + slab : first + slab + 2, 0:seg] = jnp.where(
                rad == rad_count - 1, outer, high[c, z]
            )
    sub = row_iota((SUB, width))

    def rates_at(ref, tile, z):
        cycle = rad * slab - first + tile * SUB + row_iota((SUB, LANES))
        radius = 1.0 + 4.0 * (cycle.astype(F32) + 0.5) / total
        power = 1.0 / (radius * jnp.sqrt(radius))
        wide = lambda x: jnp.concatenate([x] * (width // LANES), axis=1)
        courant = wide(0.5 * (0.3 / radius))
        coriolis, epicycle = wide(0.2 * power), wide(0.05 * power)
        here = pl.ds(pl.multiple_of(tile * SUB, SUB), SUB)
        before = pl.ds(pl.multiple_of((tile - 1) * SUB, SUB), SUB)
        after = pl.ds(pl.multiple_of((tile + 1) * SUB, SUB), SUB)
        z_up, z_down = min(z + 1, nz - 1), max(z - 1, 0)
        center, rad_diff, azi_diff, spread = [], [], [], []
        for c in range(3):
            cur = ref[c, z, here, :]
            inward = pltpu.roll(jnp.where(sub == SUB - 1, ref[c, z, before, :], cur), 1, 0)
            outward = pltpu.roll(jnp.where(sub == 0, ref[c, z, after, :], cur), SUB - 1, 0)
            ahead = pltpu.roll(cur, width - 1, 1)
            behind = pltpu.roll(cur, 1, 1)
            near = ref[c, z_up, here, :] + ref[c, z_down, here, :] + inward + outward + ahead + behind
            spread.append(VISCOSITY * near - (6.0 * VISCOSITY) * cur)
            rad_diff.append(outward - inward)
            azi_diff.append(ahead - behind)
            center.append(cur)
        half = 0.5 * RADIAL_COURANT
        return center, (
            spread[0] - (half * rad_diff[1] + courant * azi_diff[2]),
            coriolis * center[2] - half * rad_diff[0] + spread[1],
            spread[2] - epicycle * center[1] - courant * azi_diff[0],
        )

    def first_section(tile, carry):
        for z in range(nz):
            center, change = rates_at(field, tile, z)
            for c in range(3):
                stage[c, z, pl.ds(pl.multiple_of(tile * SUB, SUB), SUB), :] = center[c] + change[c]
        return carry

    lax.fori_loop(1, last_tile + 1, first_section, 0)

    @pl.when(rad == 0)
    def _():
        for c in range(3):
            for z in range(nz):
                stage[c, z, first - 1 : first, :] = stage[c, z, first : first + 1, :]

    @pl.when(rad == rad_count - 1)
    def _():
        for c in range(3):
            for z in range(nz):
                stage[c, z, first + slab : first + slab + 1, :] = stage[
                    c, z, first + slab - 1 : first + slab, :
                ]

    def second_section(tile, largest):
        here = pl.ds(pl.multiple_of(tile * SUB, SUB), SUB)
        for z in range(nz):
            center, change = rates_at(stage, tile, z)
            for c in range(3):
                value = 0.5 * field[c, z, here, :] + 0.5 * (center[c] + change[c])
                field[c, z, here, :] = value
                largest = jnp.maximum(largest, jnp.abs(value))
        return largest

    largest = lax.fori_loop(2, last_tile, second_section, jnp.zeros((SUB, width), F32))
    peak = jnp.maximum(jnp.max(largest, keepdims=True), 1e-30)
    scale = TOP / peak
    dests = SUB // per
    stride = -(-3 * nz * per // SUB) * SUB

    def send(index):
        at = pl.ds(index * dests, dests)
        return pltpu.make_async_copy(narrow.at[at], bulk.at[at], sems.at[index])

    def pack(tile, carry):
        here = pl.ds(pl.multiple_of(tile * SUB, SUB), SUB)
        overflow = jnp.zeros((SUB, LANES), F32)
        column = jnp.zeros((SUB, seg), F32)
        for c in range(3):
            for z in range(nz):
                value = field[c, z, here, 0:seg]
                if c == 0:
                    column = column + value
                code = encode(value, scale)
                plane = c * nz + z
                for d in range(dests):
                    for b in range(tiles):
                        line = b * stride + plane * per
                        block[(tile - 2) * dests + d, line : line + per, :] = code[
                            d * per : (d + 1) * per, b * LANES : (b + 1) * LANES
                        ]
                overflow = overflow + pltpu.roll(field[c, z, here, seg:width], 2 + 4 * plane, 1)
        overflow = jnp.where(lane_iota((SUB, LANES)) < LANES // 2, overflow, peak)
        for d in range(dests):
            dest = (tile - 2) * dests + d
            for k in range(per):
                row = d * per + k
                for b in range(tiles):
                    surf[dest, k * tiles + b : k * tiles + b + 1, :] = column[
                        row : row + 1, b * LANES : (b + 1) * LANES
                    ]
                line = per * tiles + k
                surf[dest, line : line + 1, :] = overflow[row : row + 1, :]
        for d in range(dests):
            dest = (tile - 2) * dests + d
            narrow[dest] = block[dest].astype(BF16)
        send(tile - 2).start()
        return carry

    lax.fori_loop(2, last_tile, pack, 0)
    for index in range(slab // SUB):
        send(index).wait()


def advect_kernel(
    per, nz, far_shift, far_remainder, bulk, sides, out, top,
    ring, tapped, over, codes, shift, remainder, scalar_sems, sems,
):
    scalars = [
        pltpu.make_async_copy(far, near, scalar_sems.at[i])
        for i, (far, near) in enumerate(((far_shift, shift), (far_remainder, remainder)))
    ]
    for copy in scalars:
        copy.start()
    sources = bulk.shape[0]
    count = ring.shape[1]
    tiles = count // sources
    group = nz * per
    stride = -(-3 * group // SUB) * SUB
    me = lax.axis_index("azi")

    def widen(a, peak):
        whole_block = bulk[a].astype(F32)
        packed = sides[a, per * tiles : per * tiles + per, :]
        mine = jnp.where(lane_iota((1, LANES)) >= LANES // 2, packed[0:1, :], 0.0)
        mine = jnp.max(mine, keepdims=True)
        unit = mine * (1.0 / TOP)
        for b in range(tiles):
            value = decode(whole_block[b * stride : (b + 1) * stride, :], unit)
            for c in range(3):
                ring[c, a * tiles + b] = value[c * group : (c + 1) * group, :]
        for c in range(3):
            for z in range(nz):
                turned = pltpu.roll(packed, LANES - 2 - 4 * (c * nz + z), 1)
                over[c, a, z * per : (z + 1) * per, :] = turned
        return jnp.maximum(peak, mine)

    peak = lax.fori_loop(0, sources, widen, jnp.zeros((1, 1), F32), unroll=2)
    top[...] = jnp.broadcast_to(peak, top.shape)
    lane = lane_iota((group, LANES))
    cycle = row_iota((group, LANES)) % per

    def spill(a, carry):
        after = lax.rem((a + 1) * tiles, count)
        before = lax.rem(a * tiles + count - 1, count)
        for c in range(3):
            extra = over[c, a]
            ring[c, after] = ring[c, after] + jnp.where(lane < 2, extra, 0.0)
            ring[c, before] = ring[c, before] + jnp.where(lane >= LANES - 2, extra, 0.0)
        return carry

    lax.fori_loop(0, sources, spill, 0, unroll=4)
    for copy in scalars:
        copy.wait()
    x = jnp.zeros((group, LANES), F32)
    whole, part = [], []
    for k in range(per):
        x = jnp.where(cycle == k, -remainder[me * per + k], x)
        amount = shift[me * per + k]
        whole.append(amount // LANES)
        part.append(lax.rem(amount, LANES))
    w_next = x * (x + 1.0) * (x + 2.0) / 6.0
    w_here = -(x - 1.0) * (x + 1.0) * (x + 2.0) / 2.0
    w_prev = (x - 1.0) * x * (x + 2.0) / 2.0
    w_prev_two = -(x - 1.0) * x * (x + 1.0) / 6.0

    def tap(a, carry):
        before = lax.rem(a * tiles + count - 1, count)
        after = lax.rem((a + 1) * tiles, count)
        for c in range(3):
            line = [ring[c, before]]
            line += [ring[c, a * tiles + b] for b in range(tiles)]
            line += [ring[c, after]]
            for b in range(tiles):
                prv, cur, nxt = line[b : b + 3]
                next_one = pltpu.roll(jnp.where(lane == 0, nxt, cur), LANES - 1, 1)
                prev_one = pltpu.roll(jnp.where(lane == LANES - 1, prv, cur), 1, 1)
                prev_two = pltpu.roll(jnp.where(lane >= LANES - 2, prv, cur), 2, 1)
                tapped[c, a * tiles + b] = (
                    w_next * next_one + w_here * cur + w_prev * prev_one + w_prev_two * prev_two
                )
        return carry

    lax.fori_loop(0, sources, tap, 0, unroll=2)
    scale = (TOP / GAIN) / peak

    def send(dest):
        return pltpu.make_async_copy(codes.at[dest], out.at[dest], sems.at[dest])

    def turned_tile(c, k, t):
        source = lax.rem(t - whole[k] + 2 * count, count)
        return pltpu.roll(tapped[c, source], part[k], 1)

    def turn(dest, carry):
        carry = list(carry)
        pieces = [[None] * tiles for _ in range(3)]
        for b in range(tiles):
            t = dest * tiles + b
            for c in range(3):
                joined = jnp.zeros((group, LANES), F32)
                for k in range(per):
                    now = turned_tile(c, k, t)
                    value = jnp.where(lane < part[k], carry[c * per + k], now)
                    joined = value if per == 1 else jnp.where(cycle == k, value, joined)
                    carry[c * per + k] = now
                pieces[c][b] = encode(joined, scale)
        columns = [jnp.concatenate([pieces[c][b] for b in range(tiles)], axis=1) for c in range(3)]
        codes[dest] = jnp.concatenate(columns, axis=0).astype(BF16)
        send(dest).start()
        return tuple(carry)

    start = tuple(turned_tile(c, k, -1) for c in range(3) for k in range(per))
    lax.fori_loop(0, sources, turn, start, unroll=2)
    for dest in range(sources):
        send(dest).wait()


def settle_kernel(per, bulk, top, rho, ur, up, near, sems):
    nz = rho.shape[0]
    sources, _, seg = bulk.shape
    group = nz * per
    unit = jnp.concatenate([top[0:1, :] * (GAIN / TOP)] * (seg // LANES), axis=1)
    copies = [
        pltpu.make_async_copy(near.at[c], far, sems.at[c]) for c, far in enumerate((rho, ur, up))
    ]
    for c in range(3):
        for a in range(sources):
            value = decode(bulk[a, c * group : (c + 1) * group, :].astype(F32), unit)
            for z in range(nz):
                near[c, z, a * per : (a + 1) * per, :] = value[z * per : (z + 1) * per, :]
        copies[c].start()
    for copy in copies:
        copy.wait()


def forward_kernel(per, nz, modes, fast, far_shift, far_remainder, circle, twiddle, short, steps, *rest):
    rad_count = lax.axis_size("rad")
    hops, (out, sides, rows_out, shift, remainder, scalar_sems) = rest[:fast], rest[fast:]
    scalars = [
        pltpu.make_async_copy(far, near, scalar_sems.at[i])
        for i, (far, near) in enumerate(((far_shift, shift), (far_remainder, remainder)))
    ]
    for copy in scalars:
        copy.start()
    me = lax.axis_index("azi")
    azi = lax.axis_index("azi")
    for o_fast, hop in enumerate(hops):
        for o_slow in range(hop.shape[0]):
            from_slow = came_from(azi // fast, o_slow, hop.shape[0], True)
            from_fast = came_from(azi % fast, o_fast, fast, False)
            sides[from_slow * fast + from_fast] = hop[o_slow]
    sources = sides.shape[0]
    nq = circle.shape[0]
    tiles = nq // sources
    length = nq * LANES
    upper = modes // nq
    lane = lane_iota((sources, LANES))
    q_id, a_id = row_iota((nq, 2 * sources)), lane_iota((nq, 2 * sources))
    after = lax.rem((a_id + 1) * tiles, nq)
    before = lax.rem((a_id - sources) * tiles + nq - 1, nq)
    target = (q_id == jnp.where(a_id < sources, after, before)).astype(F32)
    dot = functools.partial(jnp.dot, precision=EXACT, preferred_element_type=F32)
    spilled = []
    for k in range(per):
        packed = sides[:, per * tiles + k, :]
        extra = jnp.zeros((sources, LANES), F32)
        for z in range(nz):
            extra = extra + pltpu.roll(packed, LANES - 2 - 4 * z, 1)
        halves = (jnp.where(lane < 2, extra, 0.0), jnp.where(lane >= LANES - 2, extra, 0.0))
        spilled.append(jnp.concatenate(halves, axis=0))
    spilled = dot(target, jnp.concatenate(spilled, axis=1))
    grids = []
    for k in range(per):
        grid = sides[:, k * tiles : (k + 1) * tiles, :].reshape(nq, LANES)
        grids.append((grid + spilled[:, k * LANES : (k + 1) * LANES]).T)
    inner = dot(jnp.concatenate(grids, axis=0), circle[...])
    turn_cos, turn_sin = twiddle[:, :nq], twiddle[:, nq:]
    turned = []
    for k in range(per):
        cos_part = inner[k * LANES : (k + 1) * LANES, :nq]
        sin_part = inner[k * LANES : (k + 1) * LANES, nq:]
        turned.append(cos_part * turn_cos - sin_part * turn_sin)
        turned.append(-(sin_part * turn_cos + cos_part * turn_sin))
    outer = dot(short[...], jnp.concatenate(turned, axis=1))
    for copy in scalars:
        copy.wait()
    mode = row_iota((upper, nq)) * nq + lane_iota((upper, nq))
    cos_one, sin_one = steps[0:upper, :nq], steps[0:upper, nq:]
    cos_two, sin_two = steps[upper:, :nq], steps[upper:, nq:]
    for k in range(per):
        at = 2 * k * nq
        real = outer[:upper, at : at + nq] + outer[upper:, at + nq : at + 2 * nq]
        imag = outer[:upper, at + nq : at + 2 * nq] - outer[upper:, at : at + nq]
        x = jnp.full((upper, nq), -remainder[me * per + k], F32)
        w_next = x * (x + 1.0) * (x + 2.0) / 6.0
        w_here = -(x - 1.0) * (x + 1.0) * (x + 2.0) / 2.0
        w_prev = (x - 1.0) * x * (x + 2.0) / 2.0
        w_prev_two = -(x - 1.0) * x * (x + 1.0) / 6.0
        tap_cos = w_here + (w_next + w_prev) * cos_one + w_prev_two * cos_two
        tap_sin = (w_prev - w_next) * sin_one + w_prev_two * sin_two
        phase = lax.rem(mode * shift[me * per + k], length)
        phase = jnp.where(phase > length // 2, phase - length, phase)
        angle = phase.astype(F32) * (2.0 * math.pi / length)
        spin_cos, spin_sin = jnp.cos(angle), jnp.sin(angle)
        gain_cos = tap_cos * spin_cos - tap_sin * spin_sin
        gain_sin = tap_sin * spin_cos + tap_cos * spin_sin
        rows_out[:, k, :] = real * gain_cos + imag * gain_sin
        rows_out[:, per + k, :] = imag * gain_cos - real * gain_sin
    share = rad_count * sources // upper
    for rad in range(rad_count):
        for a in range(sources):
            at = (a * rad_count + rad) * 2 * per
            value = rows_out[(rad * sources + a) // share]
            out[at : at + 2 * per, :] = value.astype(BF16).astype(F32)


def pick(values, index):
    chosen = values[0]
    for i, value in enumerate(values[1:]):
        chosen = jnp.where(index == i + 1, value, chosen)
    return chosen


def route_kernel(size, middle, inner, where, ring, *rest):
    count = (len(rest) - 1 - size)
    sources, outs, sorted_rows = rest[:count], rest[count:-1], rest[-1]
    for i, source in enumerate(sources):
        value = source[...]
        for m in range(middle):
            for dest in range(size):
                at = (m * size + dest) * inner
                to = (i * middle + m) * inner
                sorted_rows[dest, to : to + inner, :] = value[at : at + inner, :]
    choices = [sorted_rows[dest] for dest in range(size)]
    index = where()
    for offset, out in enumerate(outs):
        out[...] = pick(choices, sent_to(index, offset, size, ring))


def halve_kernel(inner, *rest):
    rad_count = lax.axis_size("rad")
    outs, sorted_rows = rest[-1 - rad_count : -1], rest[-1]
    to = 0
    for source in rest[: -1 - rad_count]:
        value = source[...]
        for m in range(value.shape[0] // (rad_count * inner)):
            for rad in range(rad_count):
                at = (m * rad_count + rad) * inner
                sorted_rows[rad, to : to + inner, :] = value[at : at + inner, :]
            to += inner
    choices = [sorted_rows[rad] for rad in range(rad_count)]
    for offset, out in enumerate(outs):
        out[...] = pick(choices, sent_to(lax.axis_index("rad"), offset, rad_count, False))


def arrival_source(slow, fast, axis_iota):
    rad_count = lax.axis_size("rad")
    azi, rad = lax.axis_index("azi"), lax.axis_index("rad")
    from_rad = came_from(rad, axis_iota % rad_count, rad_count, False)
    from_fast = came_from(azi % fast, axis_iota // rad_count % fast, fast, False)
    from_slow = came_from(azi // fast, axis_iota // (rad_count * fast) % slow, slow, True)
    return (from_rad * slow + from_slow) * fast + from_fast


def couple_kernel(per, local, fast, slow, kernel, *rest):
    rad_count = lax.axis_size("rad")
    columns, outs = rest[:rad_count], rest[rad_count:]
    sources = slow * fast * rad_count
    nq = columns[0].shape[1]
    total = sources * per
    me = lax.axis_index("rad") * lax.axis_size("azi") + lax.axis_index("azi")
    offset = lax.rem(me * local, nq)
    row, col = row_iota((total, total)), lane_iota((total, total))
    place = col % sources
    azi_count = slow * fast
    place = place % azi_count * rad_count + place // azi_count
    source = arrival_source(slow, fast, place)
    spread = (row == source * per + col // sources).astype(F32)
    lane = lane_iota((total, nq))
    sides = []
    for c in range(2):
        stacked = jnp.concatenate(
            [
                ref[pl.ds(c * per + k, slow * fast, stride=2 * per), :]
                for k in range(per)
                for ref in columns
            ],
            axis=0,
        )
        ordered = jnp.dot(spread, stacked, preferred_element_type=F32)
        sides.append(pltpu.roll(ordered, lax.rem(nq - offset + c * local, nq), 1))
    weights = jnp.where(lane < local, sides[0], sides[1]).astype(BF16)
    result = jnp.zeros((total, nq), F32)
    for m in range(local):
        product = jnp.dot(kernel[m], weights, preferred_element_type=F32)
        result = jnp.where((lane == m) | (lane == local + m), product, result)
    rad = lax.axis_index("rad")
    share = total // len(outs)
    slabs = [result[i * share : (i + 1) * share, :] for i in range(len(outs))]
    for offset, out in enumerate(outs):
        out[...] = pick(slabs, sent_to(rad, offset, len(outs), False))


def inverse_kernel(per, local, fast, *rest):
    blocks, (circle, twiddle, mixed, out) = rest[:-4], rest[-4:]
    slow = len(blocks)
    nq = circle.shape[0]
    length = nq * LANES
    share = nq // local
    rad_count = lax.axis_size("rad")
    count = slow * fast * rad_count
    dot = functools.partial(jnp.dot, precision=EXACT, preferred_element_type=F32)
    block_id = row_iota((count, nq))
    first = (block_id == 0) & (lane_iota((count, nq)) % local == 0)
    factor = jnp.where(first, 1.0, 2.0) / length
    source = arrival_source(slow, fast, lane_iota((count, count)))
    order = (source == row_iota((count, count))).astype(F32)
    picked = []
    for k in range(per):
        rows = [
            ref[pl.ds(k, fast * rad_count, stride=per), :] if per > 1 else ref[...] for ref in blocks
        ]
        picked.append(jnp.concatenate(rows, axis=0))
    values = dot(order, jnp.concatenate(picked, axis=1)) * jnp.concatenate([factor] * per, axis=1)
    tables = mixed[...]
    own = row_iota(tables.shape) % share
    tables = jnp.concatenate([jnp.where(own == h, tables, 0.0) for h in range(share)], axis=1)
    mid = dot(values.T, tables)
    turn_cos, turn_sin = twiddle[:, :LANES], twiddle[:, LANES:]
    turned = []
    for k in range(per):
        real, imag = [], []
        for h in range(share):
            at = 2 * LANES * h
            top = mid[k * nq : k * nq + local, at : at + 2 * LANES]
            bottom = mid[k * nq + local : k * nq + 2 * local, at : at + 2 * LANES]
            real.append(top[:, :LANES] - bottom[:, LANES:])
            imag.append(top[:, LANES:] + bottom[:, :LANES])
        real = jnp.concatenate(real, axis=0)
        imag = jnp.concatenate(imag, axis=0)
        pair = [real * turn_cos - imag * turn_sin, -(real * turn_sin + imag * turn_cos)]
        turned.append(jnp.concatenate(pair, axis=0))
    wave = dot(circle[...], jnp.concatenate(turned, axis=1))
    for k in range(per):
        for q in range(nq):
            out[k : k + 1, q * LANES : (q + 1) * LANES] = wave[
                q : q + 1, k * LANES : (k + 1) * LANES
            ]


def cos_sin(rows, columns, length):
    steps = np.outer(rows, columns) % length
    angle = 2.0 * np.pi * steps / length
    return np.cos(angle).astype(np.float32), np.sin(angle).astype(np.float32)


def call(body, out_shape, in_specs=None, out_specs=None, scratch=(), name=None, **cost):
    kernel = pl.pallas_call(
        body,
        out_shape=out_shape,
        **({} if in_specs is None else {"in_specs": in_specs}),
        **({} if out_specs is None else {"out_specs": out_specs}),
        scratch_shapes=list(scratch),
        cost_estimate=pl.CostEstimate(**{"flops": 0, "bytes_accessed": 0, "transcendentals": 0, **cost}),
    )

    def run(*operands):
        near = [
            x if x.ndim == 1 or name == "load" else pltpu.with_memory_space_constraint(x, pltpu.VMEM)
            for x in operands
        ]
        return kernel(*near)

    return run


def exchange(array, axes):
    return lax.all_to_all(array, axes, 0, 0, tiled=True)


def shape_of(shape, dtype=F32):
    return jax.ShapeDtypeStruct(shape, dtype)


def body(density, radial_velocity, azimuthal_velocity, cycle_shift, remainder, kernel):
    nz, slab, seg = density.shape
    azi, rad = lax.axis_size("azi"), lax.axis_size("rad")
    devices = azi * rad
    per = slab // azi
    tiles = seg // LANES
    length = seg * azi
    nq = length // LANES
    local = kernel.shape[0]
    modes = local * devices
    upper = modes // nq
    width = seg + LANES
    group = nz * per
    stride = -(-3 * group // SUB) * SUB
    rows = tiles * stride
    side = side_rows(per, tiles)
    fast = min(4, azi)
    slow = azi // fast
    vmem, smem = pl.BlockSpec(memory_space=pltpu.VMEM), pl.BlockSpec(memory_space=pltpu.SMEM)

    fields = (density, radial_velocity, azimuthal_velocity)
    anywhere = pl.BlockSpec(memory_space=pl.ANY)
    edge = pltpu.VMEM((3, nz, 2, seg), F32)
    *fields, tail, head = call(
        load_kernel,
        (*(pltpu.VMEM((nz, slab, seg), F32) for _ in range(3)), edge, edge),
        in_specs=[anywhere] * 3,
        scratch=(pltpu.SemaphoreType.DMA((3,)),),
        name="load",
        bytes_accessed=12 * nz * slab * seg,
    )(*fields)
    low = lax.ppermute(tail, "rad", [(i, (i + 1) % rad) for i in range(rad)])
    high = lax.ppermute(head, "rad", [((i + 1) % rad, i) for i in range(rad)])
    bulk, surf = call(
        functools.partial(hydro_kernel, per),
        (shape_of((azi, rows, LANES), BF16), pltpu.VMEM((azi, side, LANES), F32)),
        out_specs=(anywhere, vmem),
        scratch=(
            pltpu.VMEM((3, nz, slab + 4 * SUB, width), F32),
            pltpu.VMEM((3, nz, slab + 4 * SUB, width), F32),
            pltpu.VMEM((azi, rows, LANES), F32),
            pltpu.VMEM((azi, rows, LANES), BF16),
            pltpu.SemaphoreType.DMA((slab // SUB,)),
        ),
        name="hydro",
        flops=100 * 3 * nz * slab * seg,
        bytes_accessed=24 * nz * slab * seg,
    )(*fields, low, high)

    def hop(buffers, axis, size, step, ring=False):
        around = range(lax.axis_size(axis))
        return [buffers[0]] + [
            lax.ppermute(buffers[o], axis, [
                (i, i + (sent_to(i // step % size, o, size, ring) - i // step % size) * step)
                for i in around
            ])
            for o in range(1, size)
        ]

    def route(buffers, size, inner, step, name, ring=False):
        count = buffers[0].shape[0]
        lines = len(buffers) * count // size
        where = lambda: lax.axis_index("azi") // step % size
        buffers = call(
            functools.partial(route_kernel, size, count // (size * inner), inner, where, ring),
            tuple(pltpu.VMEM((lines, LANES), F32) for _ in range(size)),
            scratch=(pltpu.VMEM((size, lines, LANES), F32),),
            name="route_" + name,
            bytes_accessed=100_000,
        )(*buffers)
        return hop(buffers, "azi", size, step, ring)

    surf = [surf.reshape(azi * side, LANES)]
    surf = route(surf, slow, fast * side, fast, "surf_slow", ring=True)
    bulk = exchange(bulk, "azi")
    surf = route(surf, fast, side, 1, "surf_fast")
    surf = [x.reshape(slow, side, LANES) for x in surf]

    k_id, l_id = np.arange(nq), np.arange(LANES)
    circle = np.concatenate(cos_sin(k_id, k_id, nq), axis=1)
    twiddle = np.concatenate(cos_sin(l_id, k_id, length), axis=1)
    short = np.concatenate(cos_sin(np.arange(upper), l_id, LANES), axis=0)
    m_id = np.arange(modes)
    steps = [np.concatenate([t.reshape(upper, nq) for t in cos_sin(m_id, [n], length)], 1) for n in (1, 2)]
    steps = np.concatenate(steps, axis=0)
    spectrum, sides = call(
        functools.partial(forward_kernel, per, nz, modes, fast),
        (
            pltpu.VMEM((devices * 2 * per, nq), F32),
            pltpu.VMEM((azi, side, LANES), F32),
        ),
        in_specs=[anywhere] * 2 + [vmem] * (4 + fast),
        scratch=(
            pltpu.VMEM((upper, 2 * per, nq), F32),
            pltpu.SMEM((slab,), jnp.int32),
            pltpu.SMEM((slab,), F32),
            pltpu.SemaphoreType.DMA((2,)),
        ),
        name="forward",
        flops=100_000_000,
        bytes_accessed=1_000_000,
    )(cycle_shift, remainder, jnp.asarray(circle), jnp.asarray(twiddle), jnp.asarray(short), jnp.asarray(steps), *surf)
    columns = route([spectrum], fast, rad * 2 * per, 1, "column_fast")
    columns = route(columns, slow, rad * 2 * per, fast, "column_slow", ring=True)
    columns = call(
        functools.partial(halve_kernel, 2 * per),
        tuple(pltpu.VMEM((azi * 2 * per, nq), F32) for _ in range(rad)),
        scratch=(pltpu.VMEM((rad, azi * 2 * per, nq), F32),),
        name="route_column_rad",
        bytes_accessed=100_000,
    )(*columns)
    columns = hop(columns, "rad", rad, 1)
    blocks = call(
        functools.partial(couple_kernel, per, local, fast, slow),
        tuple(pltpu.VMEM((azi * per, nq), F32) for _ in range(rad)),
        name="couple",
        flops=100_000_000,
        bytes_accessed=1_000_000,
    )(kernel, *columns)
    blocks = hop(blocks, "rad", rad, 1)
    blocks = route(blocks, fast, per, 1, "block_fast")
    blocks = route(blocks, slow, per, fast, "block_slow", ring=True)
    j_of_block = np.arange(devices) * local // nq
    mixed = np.concatenate(cos_sin(j_of_block, l_id, LANES), axis=1)
    turn = np.concatenate(cos_sin(k_id, l_id, length), axis=1)
    potential = call(
        functools.partial(inverse_kernel, per, local, fast),
        shape_of((per, length)),
        name="inverse",
        flops=100_000_000,
        bytes_accessed=1_000_000,
    )(*blocks, jnp.asarray(circle), jnp.asarray(turn), jnp.asarray(mixed))

    moved, top = call(
        functools.partial(advect_kernel, per, nz),
        (shape_of((azi, 3 * group, seg), BF16), pltpu.VMEM((SUB, LANES), F32)),
        in_specs=[anywhere, anywhere, vmem, vmem],
        out_specs=(anywhere, vmem),
        scratch=(
            pltpu.VMEM((3, nq, group, LANES), F32),
            pltpu.VMEM((3, nq, group, LANES), F32),
            pltpu.VMEM((3, azi, group, LANES), F32),
            pltpu.VMEM((azi, 3 * group, seg), BF16),
            pltpu.SMEM((slab,), jnp.int32),
            pltpu.SMEM((slab,), F32),
            pltpu.SemaphoreType.DMA((2,)),
            pltpu.SemaphoreType.DMA((azi,)),
        ),
        name="advect",
        flops=50 * 3 * nz * slab * seg,
        bytes_accessed=12 * nz * slab * seg,
    )(cycle_shift, remainder, bulk, sides)
    moved = exchange(moved, "azi")
    results = call(
        functools.partial(settle_kernel, per),
        tuple(shape_of((nz, slab, seg)) for _ in range(3)),
        out_specs=(anywhere,) * 3,
        scratch=(pltpu.VMEM((3, nz, slab, seg), F32), pltpu.SemaphoreType.DMA((3,))),
        name="settle",
        flops=20 * 3 * nz * slab * seg,
        bytes_accessed=18 * nz * slab * seg,
    )(moved, top)
    return (*results, potential)


def solution(mesh):
    split = P(None, "rad", "azi")
    in_specs = (split, split, split, P("rad"), P("rad"), P(("rad", "azi"), None, None))
    out_specs = (split, split, split, P(("rad", "azi"), None))

    return jax.shard_map(body, mesh=mesh, in_specs=in_specs, out_specs=out_specs, check_vma=False)
```

```python
import functools
import math

import jax
import jax.numpy as jnp
import numpy as np
from jax import lax
from jax.experimental import pallas as pl
from jax.experimental.pallas import tpu as pltpu
from jax.sharding import PartitionSpec as P


RADIAL_COURANT = 0.3
VISCOSITY = 0.08
LANES = 128
VMEM_BYTES = 67_043_328
SUB = 8
EXACT = lax.Precision.HIGHEST
F32 = jnp.float32
BF16 = jnp.bfloat16

POWER = 12
TOP = 2.0**10.5
GAIN = 1.25


def encode(value, scale):
    scaled = value * scale
    second = scaled * scaled
    fourth = second * second
    size = fourth * fourth * fourth
    return jnp.where(scaled < 0.0, -size, size)


def decode(code, scale):
    root = lax.exp2(lax.log(jnp.abs(code)) * (1.0 / (POWER * math.log(2.0)))) * scale
    return jnp.where(code < 0.0, -root, root)


def sent_to(place, offset, size, ring):
    return (place + offset) % size if ring else place ^ offset


def came_from(place, offset, size, ring):
    return (place - offset + size) % size if ring else place ^ offset


def row_iota(shape):
    return lax.broadcasted_iota(jnp.int32, shape, 0)


def lane_iota(shape):
    return lax.broadcasted_iota(jnp.int32, shape, 1)


def side_rows(per, tiles):
    return -(-(per * tiles + per) // SUB) * SUB


def edges_kernel(rho, ur, up, tail, head, last, first, sems):
    slab = rho.shape[1]
    copies = []
    for c, far in enumerate((rho, ur, up)):
        ends = (far.at[:, pl.ds(slab - SUB, SUB), :], last.at[c]), (far.at[:, pl.ds(0, SUB), :], first.at[c])
        copies += [pltpu.make_async_copy(*end, sems.at[2 * c + i]) for i, end in enumerate(ends)]
    for copy in copies:
        copy.start()
    for c in range(3):
        copies[2 * c].wait()
        tail[c] = last[c, :, SUB - 2 :, :]
        copies[2 * c + 1].wait()
        head[c] = first[c, :, 0:2, :]


def advance(ref, tile, z, slab, scale):
    _, nz, lines, width = ref.shape
    count = lines // SUB
    sub = row_iota((SUB, width))
    near_rows = row_iota((SUB, LANES))
    cycle = tile * SUB + near_rows
    cycle = jnp.where((tile == count - 1) & (near_rows >= SUB // 2), near_rows - SUB, cycle)
    cycle = lax.axis_index("rad") * slab + cycle
    radius = 1.0 + 4.0 * (cycle.astype(F32) + 0.5) / (slab * lax.axis_size("rad"))
    power = 1.0 / (radius * jnp.sqrt(radius))
    wide = lambda x: jnp.concatenate([x] * (width // LANES), axis=1)
    courant = wide((0.5 * scale) * (0.3 / radius))
    coriolis, epicycle = wide((0.2 * scale) * power), wide((0.05 * scale) * power)
    rows = lambda t: pl.ds(pl.multiple_of(t * SUB, SUB), SUB)
    here, before, after = rows(tile), rows(lax.rem(tile + count - 1, count)), rows(lax.rem(tile + 1, count))
    z_up, z_down = min(z + 1, nz - 1), max(z - 1, 0)
    center, base, rad_diff, azi_diff = [], [], [], []
    for c in range(3):
        cur = ref[c, z, here, :]
        inward = pltpu.roll(jnp.where(sub == SUB - 1, ref[c, z, before, :], cur), 1, 0)
        outward = pltpu.roll(jnp.where(sub == 0, ref[c, z, after, :], cur), SUB - 1, 0)
        ahead = pltpu.roll(cur, width - 1, 1)
        behind = pltpu.roll(cur, 1, 1)
        near = ref[c, z_up, here, :] + ref[c, z_down, here, :] + inward + outward + ahead + behind
        base.append((scale * VISCOSITY) * near + (scale * (1.0 - 6.0 * VISCOSITY)) * cur)
        rad_diff.append(outward - inward)
        azi_diff.append(ahead - behind)
        center.append(cur)
    half = 0.5 * scale * RADIAL_COURANT
    return (
        base[0] - (half * rad_diff[1] + courant * azi_diff[2]),
        base[1] + coriolis * center[2] - half * rad_diff[0],
        base[2] - epicycle * center[1] - courant * azi_diff[0],
    )


def store_section(field, stage, slab, tile):
    for z in range(field.shape[1]):
        for c, value in enumerate(advance(field, tile, z, slab, 1.0)):
            stage[c, z, pl.ds(pl.multiple_of(tile * SUB, SUB), SUB), :] = value


def interior_kernel(rho, ur, up, field, stage, sems):
    nz, slab, seg = rho.shape
    copies = [
        pltpu.make_async_copy(far, field.at[c, :, pl.ds(0, slab), pl.ds(0, seg)], sems.at[c])
        for c, far in enumerate((rho, ur, up))
    ]
    for copy in copies:
        copy.start()
    lines, width = field.shape[2:]
    for c in range(3):
        for z in range(nz):
            field[c, z, :, seg:width] = jnp.zeros((lines, width - seg), F32)
    for copy in copies:
        copy.wait()

    def section(tile, carry):
        store_section(field, stage, slab, tile)
        return carry

    lax.fori_loop(1, slab // SUB - 1, section, 0)


def hydro_kernel(
    per, seg, field_in, stage_in, low, high, bulk, surf, field, stage, block, narrow, sems
):
    _, nz, lines, width = field.shape
    slab = lines - SUB
    last = slab // SUB
    tiles = seg // LANES
    rad = lax.axis_index("rad")
    rad_count = lax.axis_size("rad")
    for c in range(3):
        for z in range(nz):
            inner = jnp.broadcast_to(field[c, z, 0:1, 0:seg], (2, seg))
            outer = jnp.broadcast_to(field[c, z, slab - 1 : slab, 0:seg], (2, seg))
            outward = jnp.where(rad == rad_count - 1, outer, high[c, z])
            inward = jnp.where(rad == 0, inner, low[c, z])
            between = jnp.zeros((SUB - 4, seg), F32)
            field[c, z, slab:lines, 0:seg] = jnp.concatenate([outward, between, inward], axis=0)

    def section(index, carry):
        store_section(field, stage, slab, lax.rem(index + last - 1, last + 1))
        return carry

    lax.fori_loop(0, 3, section, 0)

    @pl.when(rad == 0)
    def _():
        for c in range(3):
            for z in range(nz):
                stage[c, z, lines - 1 : lines, :] = stage[c, z, 0:1, :]

    @pl.when(rad == rad_count - 1)
    def _():
        for c in range(3):
            for z in range(nz):
                stage[c, z, slab : slab + 1, :] = stage[c, z, slab - 1 : slab, :]

    def second_section(tile, largest):
        here = pl.ds(pl.multiple_of(tile * SUB, SUB), SUB)
        for z in range(nz):
            for c, value in enumerate(advance(stage, tile, z, slab, 0.5)):
                value = 0.5 * field[c, z, here, :] + value
                field[c, z, here, :] = value
                largest = jnp.maximum(largest, jnp.abs(value))
        return largest

    largest = lax.fori_loop(0, last, second_section, jnp.zeros((SUB, width), F32))
    peak = jnp.maximum(jnp.max(largest, keepdims=True), 1e-30)
    scale = TOP / peak
    dests = SUB // per
    stride = -(-3 * nz * per // SUB) * SUB

    def send(index):
        at = pl.ds(index * dests, dests)
        return pltpu.make_async_copy(narrow.at[at], bulk.at[at], sems.at[index])

    def pack(tile, carry):
        here = pl.ds(pl.multiple_of(tile * SUB, SUB), SUB)
        overflow = jnp.zeros((SUB, LANES), F32)
        column = jnp.zeros((SUB, seg), F32)
        for c in range(3):
            for z in range(nz):
                value = field[c, z, here, 0:seg]
                if c == 0:
                    column = column + value
                code = encode(value, scale)
                plane = c * nz + z
                for d in range(dests):
                    for b in range(tiles):
                        line = b * stride + plane * per
                        block[tile * dests + d, line : line + per, :] = code[
                            d * per : (d + 1) * per, b * LANES : (b + 1) * LANES
                        ]
                overflow = overflow + pltpu.roll(field[c, z, here, seg:width], 2 + 4 * plane, 1)
        overflow = jnp.where(lane_iota((SUB, LANES)) < LANES // 2, overflow, peak)
        for d in range(dests):
            dest = tile * dests + d
            for k in range(per):
                row = d * per + k
                for b in range(tiles):
                    surf[dest, k * tiles + b : k * tiles + b + 1, :] = column[
                        row : row + 1, b * LANES : (b + 1) * LANES
                    ]
                line = per * tiles + k
                surf[dest, line : line + 1, :] = overflow[row : row + 1, :]
        for d in range(dests):
            dest = tile * dests + d
            narrow[dest] = block[dest].astype(BF16)
        send(tile).start()
        return carry

    lax.fori_loop(0, last, pack, 0)
    for index in range(last):
        send(index).wait()


def advect_kernel(
    per, nz, far_shift, far_remainder, bulk, sides, out, top,
    ring, tapped, over, codes, shift, remainder, scalar_sems, sems,
):
    scalars = [
        pltpu.make_async_copy(far, near, scalar_sems.at[i])
        for i, (far, near) in enumerate(((far_shift, shift), (far_remainder, remainder)))
    ]
    for copy in scalars:
        copy.start()
    sources = bulk.shape[0]
    count = ring.shape[1]
    tiles = count // sources
    group = nz * per
    stride = -(-3 * group // SUB) * SUB
    me = lax.axis_index("azi")

    def widen(a, peak):
        whole_block = bulk[a].astype(F32)
        packed = sides[a, per * tiles : per * tiles + per, :]
        mine = jnp.where(lane_iota((1, LANES)) >= LANES // 2, packed[0:1, :], 0.0)
        mine = jnp.max(mine, keepdims=True)
        unit = mine * (1.0 / TOP)
        for b in range(tiles):
            value = decode(whole_block[b * stride : (b + 1) * stride, :], unit)
            for c in range(3):
                ring[c, a * tiles + b] = value[c * group : (c + 1) * group, :]
        for c in range(3):
            for z in range(nz):
                turned = pltpu.roll(packed, LANES - 2 - 4 * (c * nz + z), 1)
                over[c, a, z * per : (z + 1) * per, :] = turned
        return jnp.maximum(peak, mine)

    peak = lax.fori_loop(0, sources, widen, jnp.zeros((1, 1), F32), unroll=2)
    top[...] = jnp.broadcast_to(peak, top.shape)
    lane = lane_iota((group, LANES))
    cycle = row_iota((group, LANES)) % per

    def spill(a, carry):
        after = lax.rem((a + 1) * tiles, count)
        before = lax.rem(a * tiles + count - 1, count)
        for c in range(3):
            extra = over[c, a]
            ring[c, after] = ring[c, after] + jnp.where(lane < 2, extra, 0.0)
            ring[c, before] = ring[c, before] + jnp.where(lane >= LANES - 2, extra, 0.0)
        return carry

    lax.fori_loop(0, sources, spill, 0, unroll=4)
    for copy in scalars:
        copy.wait()
    x = jnp.zeros((group, LANES), F32)
    whole, part = [], []
    for k in range(per):
        x = jnp.where(cycle == k, -remainder[me * per + k], x)
        amount = shift[me * per + k]
        whole.append(amount // LANES)
        part.append(lax.rem(amount, LANES))
    w_next = x * (x + 1.0) * (x + 2.0) / 6.0
    w_here = -(x - 1.0) * (x + 1.0) * (x + 2.0) / 2.0
    w_prev = (x - 1.0) * x * (x + 2.0) / 2.0
    w_prev_two = -(x - 1.0) * x * (x + 1.0) / 6.0

    def tap(a, carry):
        before = lax.rem(a * tiles + count - 1, count)
        after = lax.rem((a + 1) * tiles, count)
        for c in range(3):
            line = [ring[c, before]]
            line += [ring[c, a * tiles + b] for b in range(tiles)]
            line += [ring[c, after]]
            for b in range(tiles):
                prv, cur, nxt = line[b : b + 3]
                next_one = pltpu.roll(jnp.where(lane == 0, nxt, cur), LANES - 1, 1)
                prev_one = pltpu.roll(jnp.where(lane == LANES - 1, prv, cur), 1, 1)
                prev_two = pltpu.roll(jnp.where(lane >= LANES - 2, prv, cur), 2, 1)
                tapped[c, a * tiles + b] = (
                    w_next * next_one + w_here * cur + w_prev * prev_one + w_prev_two * prev_two
                )
        return carry

    lax.fori_loop(0, sources, tap, 0, unroll=2)
    scale = (TOP / GAIN) / peak

    def send(dest):
        return pltpu.make_async_copy(codes.at[dest], out.at[dest], sems.at[dest])

    def turned_tile(c, k, t):
        source = lax.rem(t - whole[k] + 2 * count, count)
        return pltpu.roll(tapped[c, source], part[k], 1)

    def turn(dest, carry):
        carry = list(carry)
        pieces = [[None] * tiles for _ in range(3)]
        for b in range(tiles):
            t = dest * tiles + b
            for c in range(3):
                joined = jnp.zeros((group, LANES), F32)
                for k in range(per):
                    now = turned_tile(c, k, t)
                    value = jnp.where(lane < part[k], carry[c * per + k], now)
                    joined = value if per == 1 else jnp.where(cycle == k, value, joined)
                    carry[c * per + k] = now
                pieces[c][b] = encode(joined, scale)
        columns = [jnp.concatenate([pieces[c][b] for b in range(tiles)], axis=1) for c in range(3)]
        codes[dest] = jnp.concatenate(columns, axis=0).astype(BF16)
        send(dest).start()
        return tuple(carry)

    start = tuple(turned_tile(c, k, -1) for c in range(3) for k in range(per))
    lax.fori_loop(0, sources, turn, start, unroll=2)
    for dest in range(sources):
        send(dest).wait()


def settle_kernel(per, bulk, top, rho, ur, up, near, sems):
    nz = rho.shape[0]
    sources, _, seg = bulk.shape
    group = nz * per
    unit = jnp.concatenate([top[0:1, :] * (GAIN / TOP)] * (seg // LANES), axis=1)
    copies = [
        pltpu.make_async_copy(near.at[c], far, sems.at[c]) for c, far in enumerate((rho, ur, up))
    ]
    for c in range(3):
        for a in range(sources):
            value = decode(bulk[a, c * group : (c + 1) * group, :].astype(F32), unit)
            for z in range(nz):
                near[c, z, a * per : (a + 1) * per, :] = value[z * per : (z + 1) * per, :]
        copies[c].start()
    for copy in copies:
        copy.wait()


def forward_kernel(per, nz, modes, fast, far_shift, far_remainder, circle, twiddle, short, steps, *rest):
    rad_count = lax.axis_size("rad")
    hops, (out, sides, rows_out, shift, remainder, scalar_sems) = rest[:fast], rest[fast:]
    scalars = [
        pltpu.make_async_copy(far, near, scalar_sems.at[i])
        for i, (far, near) in enumerate(((far_shift, shift), (far_remainder, remainder)))
    ]
    for copy in scalars:
        copy.start()
    me = lax.axis_index("azi")
    azi = lax.axis_index("azi")
    for o_fast, hop in enumerate(hops):
        for o_slow in range(hop.shape[0]):
            from_slow = came_from(azi // fast, o_slow, hop.shape[0], True)
            from_fast = came_from(azi % fast, o_fast, fast, False)
            sides[from_slow * fast + from_fast] = hop[o_slow]
    sources = sides.shape[0]
    nq = circle.shape[0]
    tiles = nq // sources
    length = nq * LANES
    upper = modes // nq
    lane = lane_iota((sources, LANES))
    q_id, a_id = row_iota((nq, 2 * sources)), lane_iota((nq, 2 * sources))
    after = lax.rem((a_id + 1) * tiles, nq)
    before = lax.rem((a_id - sources) * tiles + nq - 1, nq)
    target = (q_id == jnp.where(a_id < sources, after, before)).astype(F32)
    dot = functools.partial(jnp.dot, precision=EXACT, preferred_element_type=F32)
    spilled = []
    for k in range(per):
        packed = sides[:, per * tiles + k, :]
        extra = jnp.zeros((sources, LANES), F32)
        for z in range(nz):
            extra = extra + pltpu.roll(packed, LANES - 2 - 4 * z, 1)
        halves = (jnp.where(lane < 2, extra, 0.0), jnp.where(lane >= LANES - 2, extra, 0.0))
        spilled.append(jnp.concatenate(halves, axis=0))
    spilled = dot(target, jnp.concatenate(spilled, axis=1))
    grids = []
    for k in range(per):
        grid = sides[:, k * tiles : (k + 1) * tiles, :].reshape(nq, LANES)
        grids.append((grid + spilled[:, k * LANES : (k + 1) * LANES]).T)
    inner = dot(jnp.concatenate(grids, axis=0), circle[...])
    turn_cos, turn_sin = twiddle[:, :nq], twiddle[:, nq:]
    turned = []
    for k in range(per):
        cos_part = inner[k * LANES : (k + 1) * LANES, :nq]
        sin_part = inner[k * LANES : (k + 1) * LANES, nq:]
        turned.append(cos_part * turn_cos - sin_part * turn_sin)
        turned.append(-(sin_part * turn_cos + cos_part * turn_sin))
    outer = dot(short[...], jnp.concatenate(turned, axis=1))
    for copy in scalars:
        copy.wait()
    mode = row_iota((upper, nq)) * nq + lane_iota((upper, nq))
    cos_one, sin_one = steps[0:upper, :nq], steps[0:upper, nq:]
    cos_two, sin_two = steps[upper:, :nq], steps[upper:, nq:]
    for k in range(per):
        at = 2 * k * nq
        real = outer[:upper, at : at + nq] + outer[upper:, at + nq : at + 2 * nq]
        imag = outer[:upper, at + nq : at + 2 * nq] - outer[upper:, at : at + nq]
        x = jnp.full((upper, nq), -remainder[me * per + k], F32)
        w_next = x * (x + 1.0) * (x + 2.0) / 6.0
        w_here = -(x - 1.0) * (x + 1.0) * (x + 2.0) / 2.0
        w_prev = (x - 1.0) * x * (x + 2.0) / 2.0
        w_prev_two = -(x - 1.0) * x * (x + 1.0) / 6.0
        tap_cos = w_here + (w_next + w_prev) * cos_one + w_prev_two * cos_two
        tap_sin = (w_prev - w_next) * sin_one + w_prev_two * sin_two
        phase = lax.rem(mode * shift[me * per + k], length)
        phase = jnp.where(phase > length // 2, phase - length, phase)
        angle = phase.astype(F32) * (2.0 * math.pi / length)
        spin_cos, spin_sin = jnp.cos(angle), jnp.sin(angle)
        gain_cos = tap_cos * spin_cos - tap_sin * spin_sin
        gain_sin = tap_sin * spin_cos + tap_cos * spin_sin
        rows_out[:, k, :] = real * gain_cos + imag * gain_sin
        rows_out[:, per + k, :] = imag * gain_cos - real * gain_sin
    share = rad_count * sources // upper
    for rad in range(rad_count):
        for a in range(sources):
            at = (a * rad_count + rad) * 2 * per
            value = rows_out[(rad * sources + a) // share]
            out[at : at + 2 * per, :] = value.astype(BF16).astype(F32)


def pick(values, index):
    chosen = values[0]
    for i, value in enumerate(values[1:]):
        chosen = jnp.where(index == i + 1, value, chosen)
    return chosen


def route_kernel(size, middle, inner, where, ring, *rest):
    count = (len(rest) - 1 - size)
    sources, outs, sorted_rows = rest[:count], rest[count:-1], rest[-1]
    for i, source in enumerate(sources):
        value = source[...]
        for m in range(middle):
            for dest in range(size):
                at = (m * size + dest) * inner
                to = (i * middle + m) * inner
                sorted_rows[dest, to : to + inner, :] = value[at : at + inner, :]
    choices = [sorted_rows[dest] for dest in range(size)]
    index = where()
    for offset, out in enumerate(outs):
        out[...] = pick(choices, sent_to(index, offset, size, ring))


def halve_kernel(inner, *rest):
    rad_count = lax.axis_size("rad")
    outs, sorted_rows = rest[-1 - rad_count : -1], rest[-1]
    to = 0
    for source in rest[: -1 - rad_count]:
        value = source[...]
        for m in range(value.shape[0] // (rad_count * inner)):
            for rad in range(rad_count):
                at = (m * rad_count + rad) * inner
                sorted_rows[rad, to : to + inner, :] = value[at : at + inner, :]
            to += inner
    choices = [sorted_rows[rad] for rad in range(rad_count)]
    for offset, out in enumerate(outs):
        out[...] = pick(choices, sent_to(lax.axis_index("rad"), offset, rad_count, False))


def arrival_source(slow, fast, axis_iota):
    rad_count = lax.axis_size("rad")
    azi, rad = lax.axis_index("azi"), lax.axis_index("rad")
    from_rad = came_from(rad, axis_iota % rad_count, rad_count, False)
    from_fast = came_from(azi % fast, axis_iota // rad_count % fast, fast, False)
    from_slow = came_from(azi // fast, axis_iota // (rad_count * fast) % slow, slow, True)
    return (from_rad * slow + from_slow) * fast + from_fast


def couple_kernel(per, local, fast, slow, kernel, *rest):
    rad_count = lax.axis_size("rad")
    columns, outs = rest[:rad_count], rest[rad_count:]
    sources = slow * fast * rad_count
    nq = columns[0].shape[1]
    total = sources * per
    me = lax.axis_index("rad") * lax.axis_size("azi") + lax.axis_index("azi")
    offset = lax.rem(me * local, nq)
    row, col = row_iota((total, total)), lane_iota((total, total))
    place = col % sources
    azi_count = slow * fast
    place = place % azi_count * rad_count + place // azi_count
    source = arrival_source(slow, fast, place)
    spread = (row == source * per + col // sources).astype(F32)
    lane = lane_iota((total, nq))
    sides = []
    for c in range(2):
        stacked = jnp.concatenate(
            [
                ref[pl.ds(c * per + k, slow * fast, stride=2 * per), :]
                for k in range(per)
                for ref in columns
            ],
            axis=0,
        )
        ordered = jnp.dot(spread, stacked, preferred_element_type=F32)
        sides.append(pltpu.roll(ordered, lax.rem(nq - offset + c * local, nq), 1))
    weights = jnp.where(lane < local, sides[0], sides[1]).astype(BF16)
    result = jnp.zeros((total, nq), F32)
    for m in range(local):
        product = jnp.dot(kernel[m], weights, preferred_element_type=F32)
        result = jnp.where((lane == m) | (lane == local + m), product, result)
    rad = lax.axis_index("rad")
    share = total // len(outs)
    slabs = [result[i * share : (i + 1) * share, :] for i in range(len(outs))]
    for offset, out in enumerate(outs):
        out[...] = pick(slabs, sent_to(rad, offset, len(outs), False))


def inverse_kernel(per, local, fast, *rest):
    blocks, (circle, twiddle, mixed, out) = rest[:-4], rest[-4:]
    slow = len(blocks)
    nq = circle.shape[0]
    length = nq * LANES
    share = nq // local
    rad_count = lax.axis_size("rad")
    count = slow * fast * rad_count
    dot = functools.partial(jnp.dot, precision=EXACT, preferred_element_type=F32)
    block_id = row_iota((count, nq))
    first = (block_id == 0) & (lane_iota((count, nq)) % local == 0)
    factor = jnp.where(first, 1.0, 2.0) / length
    source = arrival_source(slow, fast, lane_iota((count, count)))
    order = (source == row_iota((count, count))).astype(F32)
    picked = []
    for k in range(per):
        rows = [
            ref[pl.ds(k, fast * rad_count, stride=per), :] if per > 1 else ref[...] for ref in blocks
        ]
        picked.append(jnp.concatenate(rows, axis=0))
    values = dot(order, jnp.concatenate(picked, axis=1)) * jnp.concatenate([factor] * per, axis=1)
    tables = mixed[...]
    own = row_iota(tables.shape) % share
    tables = jnp.concatenate([jnp.where(own == h, tables, 0.0) for h in range(share)], axis=1)
    mid = dot(values.T, tables)
    turn_cos, turn_sin = twiddle[:, :LANES], twiddle[:, LANES:]
    turned = []
    for k in range(per):
        real, imag = [], []
        for h in range(share):
            at = 2 * LANES * h
            top = mid[k * nq : k * nq + local, at : at + 2 * LANES]
            bottom = mid[k * nq + local : k * nq + 2 * local, at : at + 2 * LANES]
            real.append(top[:, :LANES] - bottom[:, LANES:])
            imag.append(top[:, LANES:] + bottom[:, :LANES])
        real = jnp.concatenate(real, axis=0)
        imag = jnp.concatenate(imag, axis=0)
        pair = [real * turn_cos - imag * turn_sin, -(real * turn_sin + imag * turn_cos)]
        turned.append(jnp.concatenate(pair, axis=0))
    wave = dot(circle[...], jnp.concatenate(turned, axis=1))
    for k in range(per):
        for q in range(nq):
            out[k : k + 1, q * LANES : (q + 1) * LANES] = wave[
                q : q + 1, k * LANES : (k + 1) * LANES
            ]


def cos_sin(rows, columns, length):
    steps = np.outer(rows, columns) % length
    angle = 2.0 * np.pi * steps / length
    return np.cos(angle).astype(np.float32), np.sin(angle).astype(np.float32)


def call(body, out_shape, in_specs=None, out_specs=None, scratch=(), name=None, aliases=None, room=40 * 2**20, **cost):
    kernel = pl.pallas_call(
        body,
        out_shape=out_shape,
        **({} if in_specs is None else {"in_specs": in_specs}),
        **({} if out_specs is None else {"out_specs": out_specs}),
        scratch_shapes=list(scratch),
        input_output_aliases=aliases or {},
        compiler_params=pltpu.CompilerParams(vmem_limit_bytes=VMEM_BYTES - room),
        cost_estimate=pl.CostEstimate(**{"flops": 0, "bytes_accessed": 0, "transcendentals": 0, **cost}),
    )

    def run(*operands):
        places = [
            None if x.ndim == 1 else pltpu.HBM if name in ("edges", "interior") else pltpu.VMEM
            for x in operands
        ]
        near = [
            x if place is None else pltpu.with_memory_space_constraint(x, place)
            for x, place in zip(operands, places)
        ]
        return kernel(*near)

    return run


def exchange(array, axes):
    return lax.all_to_all(array, axes, 0, 0, tiled=True)


def shape_of(shape, dtype=F32):
    return jax.ShapeDtypeStruct(shape, dtype)


def body(density, radial_velocity, azimuthal_velocity, cycle_shift, remainder, kernel):
    nz, slab, seg = density.shape
    azi, rad = lax.axis_size("azi"), lax.axis_size("rad")
    devices = azi * rad
    per = slab // azi
    tiles = seg // LANES
    length = seg * azi
    nq = length // LANES
    local = kernel.shape[0]
    modes = local * devices
    upper = modes // nq
    width = seg + LANES
    group = nz * per
    stride = -(-3 * group // SUB) * SUB
    rows = tiles * stride
    side = side_rows(per, tiles)
    fast = min(4, azi)
    slow = azi // fast
    vmem, smem = pl.BlockSpec(memory_space=pltpu.VMEM), pl.BlockSpec(memory_space=pltpu.SMEM)

    fields = (density, radial_velocity, azimuthal_velocity)
    anywhere = pl.BlockSpec(memory_space=pl.ANY)
    far = pl.BlockSpec(memory_space=pltpu.HBM)
    edge = pltpu.VMEM((3, nz, 2, seg), F32)
    tail, head = call(
        edges_kernel,
        (edge, edge),
        in_specs=[far] * 3,
        scratch=(
            pltpu.VMEM((3, nz, SUB, seg), F32),
            pltpu.VMEM((3, nz, SUB, seg), F32),
            pltpu.SemaphoreType.DMA((6,)),
        ),
        name="edges",
        bytes_accessed=24 * nz * SUB * seg,
    )(*fields)
    low = lax.ppermute(tail, "rad", [(i, (i + 1) % rad) for i in range(rad)])
    high = lax.ppermute(head, "rad", [((i + 1) % rad, i) for i in range(rad)])
    padded = pltpu.VMEM((3, nz, slab + SUB, width), F32)
    field, stage = call(
        interior_kernel,
        (padded, padded),
        in_specs=[far] * 3,
        scratch=(pltpu.SemaphoreType.DMA((3,)),),
        name="interior",
        bytes_accessed=12 * nz * slab * seg,
    )(*fields)
    bulk, surf, *_ = call(
        functools.partial(hydro_kernel, per, seg),
        (pltpu.HBM((azi, rows, LANES), BF16), pltpu.VMEM((azi, side, LANES), F32), padded, padded),
        out_specs=(far, vmem, vmem, vmem),
        aliases={0: 2, 1: 3},
        scratch=(
            pltpu.VMEM((azi, rows, LANES), F32),
            pltpu.VMEM((azi, rows, LANES), BF16),
            pltpu.SemaphoreType.DMA((slab // SUB,)),
        ),
        name="hydro",
        flops=100 * 3 * nz * slab * seg,
        bytes_accessed=24 * nz * slab * seg,
    )(field, stage, low, high)

    def hop(buffers, axis, size, step, ring=False):
        around = range(lax.axis_size(axis))
        return [buffers[0]] + [
            lax.ppermute(buffers[o], axis, [
                (i, i + (sent_to(i // step % size, o, size, ring) - i // step % size) * step)
                for i in around
            ])
            for o in range(1, size)
        ]

    def route(buffers, size, inner, step, name, ring=False):
        count = buffers[0].shape[0]
        lines = len(buffers) * count // size
        where = lambda: lax.axis_index("azi") // step % size
        buffers = call(
            functools.partial(route_kernel, size, count // (size * inner), inner, where, ring),
            tuple(pltpu.VMEM((lines, LANES), F32) for _ in range(size)),
            scratch=(pltpu.VMEM((size, lines, LANES), F32),),
            name="route_" + name,
            bytes_accessed=100_000,
        )(*buffers)
        return hop(buffers, "azi", size, step, ring)

    surf = [surf.reshape(azi * side, LANES)]
    surf = route(surf, slow, fast * side, fast, "surf_slow", ring=True)
    bulk = exchange(bulk, "azi")
    surf = route(surf, fast, side, 1, "surf_fast")
    surf = [x.reshape(slow, side, LANES) for x in surf]

    k_id, l_id = np.arange(nq), np.arange(LANES)
    circle = np.concatenate(cos_sin(k_id, k_id, nq), axis=1)
    twiddle = np.concatenate(cos_sin(l_id, k_id, length), axis=1)
    short = np.concatenate(cos_sin(np.arange(upper), l_id, LANES), axis=0)
    m_id = np.arange(modes)
    steps = [np.concatenate([t.reshape(upper, nq) for t in cos_sin(m_id, [n], length)], 1) for n in (1, 2)]
    steps = np.concatenate(steps, axis=0)
    spectrum, sides = call(
        functools.partial(forward_kernel, per, nz, modes, fast),
        (
            pltpu.VMEM((devices * 2 * per, nq), F32),
            pltpu.VMEM((azi, side, LANES), F32),
        ),
        in_specs=[anywhere] * 2 + [vmem] * (4 + fast),
        scratch=(
            pltpu.VMEM((upper, 2 * per, nq), F32),
            pltpu.SMEM((slab,), jnp.int32),
            pltpu.SMEM((slab,), F32),
            pltpu.SemaphoreType.DMA((2,)),
        ),
        name="forward",
        flops=100_000_000,
        bytes_accessed=1_000_000,
    )(cycle_shift, remainder, jnp.asarray(circle), jnp.asarray(twiddle), jnp.asarray(short), jnp.asarray(steps), *surf)
    columns = route([spectrum], fast, rad * 2 * per, 1, "column_fast")
    columns = route(columns, slow, rad * 2 * per, fast, "column_slow", ring=True)
    columns = call(
        functools.partial(halve_kernel, 2 * per),
        tuple(pltpu.VMEM((azi * 2 * per, nq), F32) for _ in range(rad)),
        scratch=(pltpu.VMEM((rad, azi * 2 * per, nq), F32),),
        name="route_column_rad",
        bytes_accessed=100_000,
    )(*columns)
    columns = hop(columns, "rad", rad, 1)
    blocks = call(
        functools.partial(couple_kernel, per, local, fast, slow),
        tuple(pltpu.VMEM((azi * per, nq), F32) for _ in range(rad)),
        name="couple",
        flops=100_000_000,
        bytes_accessed=1_000_000,
    )(kernel, *columns)
    blocks = hop(blocks, "rad", rad, 1)
    blocks = route(blocks, fast, per, 1, "block_fast")
    blocks = route(blocks, slow, per, fast, "block_slow", ring=True)
    j_of_block = np.arange(devices) * local // nq
    mixed = np.concatenate(cos_sin(j_of_block, l_id, LANES), axis=1)
    turn = np.concatenate(cos_sin(k_id, l_id, length), axis=1)
    potential = call(
        functools.partial(inverse_kernel, per, local, fast),
        shape_of((per, length)),
        name="inverse",
        flops=100_000_000,
        bytes_accessed=1_000_000,
    )(*blocks, jnp.asarray(circle), jnp.asarray(turn), jnp.asarray(mixed))

    moved, top = call(
        functools.partial(advect_kernel, per, nz),
        (pltpu.HBM((azi, 3 * group, seg), BF16), pltpu.VMEM((SUB, LANES), F32)),
        in_specs=[anywhere, anywhere, vmem, vmem],
        out_specs=(far, vmem),
        scratch=(
            pltpu.VMEM((3, nq, group, LANES), F32),
            pltpu.VMEM((3, nq, group, LANES), F32),
            pltpu.VMEM((3, azi, group, LANES), F32),
            pltpu.VMEM((azi, 3 * group, seg), BF16),
            pltpu.SMEM((slab,), jnp.int32),
            pltpu.SMEM((slab,), F32),
            pltpu.SemaphoreType.DMA((2,)),
            pltpu.SemaphoreType.DMA((azi,)),
        ),
        name="advect",
        flops=50 * 3 * nz * slab * seg,
        bytes_accessed=12 * nz * slab * seg,
    )(cycle_shift, remainder, bulk, sides)
    moved = exchange(moved, "azi")
    results = call(
        functools.partial(settle_kernel, per),
        tuple(pltpu.HBM((nz, slab, seg), F32) for _ in range(3)),
        out_specs=(far,) * 3,
        scratch=(pltpu.VMEM((3, nz, slab, seg), F32), pltpu.SemaphoreType.DMA((3,))),
        name="settle",
        flops=20 * 3 * nz * slab * seg,
        bytes_accessed=18 * nz * slab * seg,
    )(moved, top)
    return (*results, potential)


def solution(mesh):
    split = P(None, "rad", "azi")
    in_specs = (split, split, split, P("rad"), P("rad"), P(("rad", "azi"), None, None))
    out_specs = (split, split, split, P(("rad", "azi"), None))

    return jax.shard_map(body, mesh=mesh, in_specs=in_specs, out_specs=out_specs, check_vma=False)
```

```python
import functools
import math

import jax
import jax.numpy as jnp
import numpy as np
from jax import lax
from jax.experimental import pallas as pl
from jax.experimental.pallas import tpu as pltpu
from jax.sharding import PartitionSpec as P


RADIAL_COURANT = 0.3
VISCOSITY = 0.08
LANES = 128
VMEM_BYTES = 67_043_328
SUB = 8
EXACT = lax.Precision.HIGHEST
F32 = jnp.float32
BF16 = jnp.bfloat16

POWER = 13
TOP = 2.0**9.69
GAIN = 1.25


def encode(value, scale):
    scaled = value * scale
    second = scaled * scaled
    fourth = second * second
    return (fourth * fourth) * (fourth * scaled)


def decode(code, scale):
    root = lax.exp2(lax.log(jnp.abs(code)) * (1.0 / (POWER * math.log(2.0)))) * scale
    return jnp.where(code < 0.0, -root, root)


def sent_to(place, offset, size, ring):
    return (place + offset) % size if ring else place ^ offset


def came_from(place, offset, size, ring):
    return (place - offset + size) % size if ring else place ^ offset


def row_iota(shape):
    return lax.broadcasted_iota(jnp.int32, shape, 0)


def lane_iota(shape):
    return lax.broadcasted_iota(jnp.int32, shape, 1)


def side_rows(per, tiles):
    return -(-(per * tiles + per) // SUB) * SUB


def edges_kernel(rho, ur, up, tail, head, last, first, sems):
    slab = rho.shape[1]
    copies = []
    for c, far in enumerate((rho, ur, up)):
        ends = (far.at[:, pl.ds(slab - SUB, SUB), :], last.at[c]), (far.at[:, pl.ds(0, SUB), :], first.at[c])
        copies += [pltpu.make_async_copy(*end, sems.at[2 * c + i]) for i, end in enumerate(ends)]
    for copy in copies:
        copy.start()
    for c in range(3):
        copies[2 * c].wait()
        tail[c] = last[c, :, SUB - 2 :, :]
        copies[2 * c + 1].wait()
        head[c] = first[c, :, 0:2, :]


def advance(ref, tile, z, slab, scale):
    _, nz, lines, width = ref.shape
    count = lines // SUB
    sub = row_iota((SUB, width))
    near_rows = row_iota((SUB, LANES))
    cycle = tile * SUB + near_rows
    cycle = jnp.where((tile == count - 1) & (near_rows >= SUB // 2), near_rows - SUB, cycle)
    cycle = lax.axis_index("rad") * slab + cycle
    radius = 1.0 + 4.0 * (cycle.astype(F32) + 0.5) / (slab * lax.axis_size("rad"))
    power = 1.0 / (radius * jnp.sqrt(radius))
    wide = lambda x: jnp.concatenate([x] * (width // LANES), axis=1)
    courant = wide((0.5 * scale) * (0.3 / radius))
    coriolis, epicycle = wide((0.2 * scale) * power), wide((0.05 * scale) * power)
    rows = lambda t: pl.ds(pl.multiple_of(t * SUB, SUB), SUB)
    here, before, after = rows(tile), rows(lax.rem(tile + count - 1, count)), rows(lax.rem(tile + 1, count))
    z_up, z_down = min(z + 1, nz - 1), max(z - 1, 0)
    center, base, rad_diff, azi_diff = [], [], [], []
    for c in range(3):
        cur = ref[c, z, here, :]
        inward = pltpu.roll(jnp.where(sub == SUB - 1, ref[c, z, before, :], cur), 1, 0)
        outward = pltpu.roll(jnp.where(sub == 0, ref[c, z, after, :], cur), SUB - 1, 0)
        ahead = pltpu.roll(cur, width - 1, 1)
        behind = pltpu.roll(cur, 1, 1)
        near = ref[c, z_up, here, :] + ref[c, z_down, here, :] + inward + outward + ahead + behind
        base.append((scale * VISCOSITY) * near + (scale * (1.0 - 6.0 * VISCOSITY)) * cur)
        rad_diff.append(outward - inward)
        azi_diff.append(ahead - behind)
        center.append(cur)
    half = 0.5 * scale * RADIAL_COURANT
    return (
        base[0] - (half * rad_diff[1] + courant * azi_diff[2]),
        base[1] + coriolis * center[2] - half * rad_diff[0],
        base[2] - epicycle * center[1] - courant * azi_diff[0],
    )


def store_section(field, stage, slab, tile):
    for z in range(field.shape[1]):
        for c, value in enumerate(advance(field, tile, z, slab, 1.0)):
            stage[c, z, pl.ds(pl.multiple_of(tile * SUB, SUB), SUB), :] = value


def interior_kernel(rho, ur, up, field, stage, sems):
    nz, slab, seg = rho.shape
    copies = [
        pltpu.make_async_copy(far, field.at[c, :, pl.ds(0, slab), pl.ds(0, seg)], sems.at[c])
        for c, far in enumerate((rho, ur, up))
    ]
    for copy in copies:
        copy.start()
    lines, width = field.shape[2:]
    for c in range(3):
        for z in range(nz):
            field[c, z, :, seg:width] = jnp.zeros((lines, width - seg), F32)
    for copy in copies:
        copy.wait()

    def section(tile, carry):
        store_section(field, stage, slab, tile)
        return carry

    lax.fori_loop(1, slab // SUB - 1, section, 0)


def hydro_kernel(
    per, seg, field_in, stage_in, low, high, bulk, surf, field, stage, block, narrow, sems
):
    _, nz, lines, width = field.shape
    slab = lines - SUB
    last = slab // SUB
    tiles = seg // LANES
    rad = lax.axis_index("rad")
    rad_count = lax.axis_size("rad")
    for c in range(3):
        for z in range(nz):
            inner = jnp.broadcast_to(field[c, z, 0:1, 0:seg], (2, seg))
            outer = jnp.broadcast_to(field[c, z, slab - 1 : slab, 0:seg], (2, seg))
            outward = jnp.where(rad == rad_count - 1, outer, high[c, z])
            inward = jnp.where(rad == 0, inner, low[c, z])
            between = jnp.zeros((SUB - 4, seg), F32)
            field[c, z, slab:lines, 0:seg] = jnp.concatenate([outward, between, inward], axis=0)

    def section(index, carry):
        store_section(field, stage, slab, lax.rem(index + last - 1, last + 1))
        return carry

    lax.fori_loop(0, 3, section, 0)

    @pl.when(rad == 0)
    def _():
        for c in range(3):
            for z in range(nz):
                stage[c, z, lines - 1 : lines, :] = stage[c, z, 0:1, :]

    @pl.when(rad == rad_count - 1)
    def _():
        for c in range(3):
            for z in range(nz):
                stage[c, z, slab : slab + 1, :] = stage[c, z, slab - 1 : slab, :]

    def second_section(tile, largest):
        here = pl.ds(pl.multiple_of(tile * SUB, SUB), SUB)
        for z in range(nz):
            for c, value in enumerate(advance(stage, tile, z, slab, 0.5)):
                value = 0.5 * field[c, z, here, :] + value
                field[c, z, here, :] = value
                largest = jnp.maximum(largest, jnp.abs(value))
        return largest

    largest = lax.fori_loop(0, last, second_section, jnp.zeros((SUB, width), F32))
    peak = jnp.maximum(jnp.max(largest, keepdims=True), 1e-30)
    scale = TOP / peak
    dests = SUB // per
    stride = -(-3 * nz * per // SUB) * SUB

    def send(index):
        at = pl.ds(index * dests, dests)
        return pltpu.make_async_copy(narrow.at[at], bulk.at[at], sems.at[index])

    def pack(tile, carry):
        here = pl.ds(pl.multiple_of(tile * SUB, SUB), SUB)
        overflow = jnp.zeros((SUB, LANES), F32)
        column = jnp.zeros((SUB, seg), F32)
        for c in range(3):
            for z in range(nz):
                value = field[c, z, here, 0:seg]
                if c == 0:
                    column = column + value
                code = encode(value, scale)
                plane = c * nz + z
                for d in range(dests):
                    for b in range(tiles):
                        line = b * stride + plane * per
                        block[tile * dests + d, line : line + per, :] = code[
                            d * per : (d + 1) * per, b * LANES : (b + 1) * LANES
                        ]
                overflow = overflow + pltpu.roll(field[c, z, here, seg:width], 2 + 4 * plane, 1)
        overflow = jnp.where(lane_iota((SUB, LANES)) < LANES // 2, overflow, peak)
        for d in range(dests):
            dest = tile * dests + d
            for k in range(per):
                row = d * per + k
                for b in range(tiles):
                    surf[dest, k * tiles + b : k * tiles + b + 1, :] = column[
                        row : row + 1, b * LANES : (b + 1) * LANES
                    ]
                line = per * tiles + k
                surf[dest, line : line + 1, :] = overflow[row : row + 1, :]
        for d in range(dests):
            dest = tile * dests + d
            narrow[dest] = block[dest].astype(BF16)
        send(tile).start()
        return carry

    lax.fori_loop(0, last, pack, 0)
    for index in range(last):
        send(index).wait()


def advect_kernel(
    per, nz, far_shift, far_remainder, bulk, sides, out, top,
    ring, tapped, over, codes, shift, remainder, scalar_sems, sems,
):
    scalars = [
        pltpu.make_async_copy(far, near, scalar_sems.at[i])
        for i, (far, near) in enumerate(((far_shift, shift), (far_remainder, remainder)))
    ]
    for copy in scalars:
        copy.start()
    sources = bulk.shape[0]
    count = ring.shape[1]
    tiles = count // sources
    group = nz * per
    stride = -(-3 * group // SUB) * SUB
    me = lax.axis_index("azi")

    def widen(a, peak):
        whole_block = bulk[a].astype(F32)
        packed = sides[a, per * tiles : per * tiles + per, :]
        mine = jnp.where(lane_iota((1, LANES)) >= LANES // 2, packed[0:1, :], 0.0)
        mine = jnp.max(mine, keepdims=True)
        unit = mine * (1.0 / TOP)
        for b in range(tiles):
            value = decode(whole_block[b * stride : (b + 1) * stride, :], unit)
            for c in range(3):
                ring[c, a * tiles + b] = value[c * group : (c + 1) * group, :]
        for c in range(3):
            for z in range(nz):
                turned = pltpu.roll(packed, LANES - 2 - 4 * (c * nz + z), 1)
                over[c, a, z * per : (z + 1) * per, :] = turned
        return jnp.maximum(peak, mine)

    peak = lax.fori_loop(0, sources, widen, jnp.zeros((1, 1), F32), unroll=2)
    top[...] = jnp.broadcast_to(peak, top.shape)
    lane = lane_iota((group, LANES))
    cycle = row_iota((group, LANES)) % per

    def spill(a, carry):
        after = lax.rem((a + 1) * tiles, count)
        before = lax.rem(a * tiles + count - 1, count)
        for c in range(3):
            extra = over[c, a]
            ring[c, after] = ring[c, after] + jnp.where(lane < 2, extra, 0.0)
            ring[c, before] = ring[c, before] + jnp.where(lane >= LANES - 2, extra, 0.0)
        return carry

    lax.fori_loop(0, sources, spill, 0, unroll=4)
    for copy in scalars:
        copy.wait()
    x = jnp.zeros((group, LANES), F32)
    whole, part = [], []
    for k in range(per):
        x = jnp.where(cycle == k, -remainder[me * per + k], x)
        amount = shift[me * per + k]
        whole.append(amount // LANES)
        part.append(lax.rem(amount, LANES))
    w_next = x * (x + 1.0) * (x + 2.0) / 6.0
    w_here = -(x - 1.0) * (x + 1.0) * (x + 2.0) / 2.0
    w_prev = (x - 1.0) * x * (x + 2.0) / 2.0
    w_prev_two = -(x - 1.0) * x * (x + 1.0) / 6.0

    def tap(a, carry):
        before = lax.rem(a * tiles + count - 1, count)
        after = lax.rem((a + 1) * tiles, count)
        for c in range(3):
            line = [ring[c, before]]
            line += [ring[c, a * tiles + b] for b in range(tiles)]
            line += [ring[c, after]]
            for b in range(tiles):
                prv, cur, nxt = line[b : b + 3]
                next_one = pltpu.roll(jnp.where(lane == 0, nxt, cur), LANES - 1, 1)
                prev_one = pltpu.roll(jnp.where(lane == LANES - 1, prv, cur), 1, 1)
                prev_two = pltpu.roll(jnp.where(lane >= LANES - 2, prv, cur), 2, 1)
                tapped[c, a * tiles + b] = (
                    w_next * next_one + w_here * cur + w_prev * prev_one + w_prev_two * prev_two
                )
        return carry

    lax.fori_loop(0, sources, tap, 0, unroll=2)
    scale = (TOP / GAIN) / peak

    def send(dest):
        return pltpu.make_async_copy(codes.at[dest], out.at[dest], sems.at[dest])

    def turned_tile(c, k, t):
        source = lax.rem(t - whole[k] + 2 * count, count)
        return pltpu.roll(tapped[c, source], part[k], 1)

    def turn(dest, carry):
        carry = list(carry)
        pieces = [[None] * tiles for _ in range(3)]
        for b in range(tiles):
            t = dest * tiles + b
            for c in range(3):
                joined = jnp.zeros((group, LANES), F32)
                for k in range(per):
                    now = turned_tile(c, k, t)
                    value = jnp.where(lane < part[k], carry[c * per + k], now)
                    joined = value if per == 1 else jnp.where(cycle == k, value, joined)
                    carry[c * per + k] = now
                pieces[c][b] = encode(joined, scale)
        columns = [jnp.concatenate([pieces[c][b] for b in range(tiles)], axis=1) for c in range(3)]
        codes[dest] = jnp.concatenate(columns, axis=0).astype(BF16)
        send(dest).start()
        return tuple(carry)

    start = tuple(turned_tile(c, k, -1) for c in range(3) for k in range(per))
    lax.fori_loop(0, sources, turn, start, unroll=2)
    for dest in range(sources):
        send(dest).wait()


def forward_kernel(per, nz, modes, fast, far_shift, far_remainder, circle, twiddle, short, steps, *rest):
    rad_count = lax.axis_size("rad")
    hops, (out, sides, rows_out, shift, remainder, scalar_sems) = rest[:fast], rest[fast:]
    scalars = [
        pltpu.make_async_copy(far, near, scalar_sems.at[i])
        for i, (far, near) in enumerate(((far_shift, shift), (far_remainder, remainder)))
    ]
    for copy in scalars:
        copy.start()
    me = lax.axis_index("azi")
    azi = lax.axis_index("azi")
    for o_fast, hop in enumerate(hops):
        for o_slow in range(hop.shape[0]):
            from_slow = came_from(azi // fast, o_slow, hop.shape[0], True)
            from_fast = came_from(azi % fast, o_fast, fast, False)
            sides[from_slow * fast + from_fast] = hop[o_slow]
    sources = sides.shape[0]
    nq = circle.shape[0]
    tiles = nq // sources
    length = nq * LANES
    upper = modes // nq
    lane = lane_iota((sources, LANES))
    q_id, a_id = row_iota((nq, 2 * sources)), lane_iota((nq, 2 * sources))
    after = lax.rem((a_id + 1) * tiles, nq)
    before = lax.rem((a_id - sources) * tiles + nq - 1, nq)
    target = (q_id == jnp.where(a_id < sources, after, before)).astype(F32)
    dot = functools.partial(jnp.dot, precision=EXACT, preferred_element_type=F32)
    spilled = []
    for k in range(per):
        packed = sides[:, per * tiles + k, :]
        extra = jnp.zeros((sources, LANES), F32)
        for z in range(nz):
            extra = extra + pltpu.roll(packed, LANES - 2 - 4 * z, 1)
        halves = (jnp.where(lane < 2, extra, 0.0), jnp.where(lane >= LANES - 2, extra, 0.0))
        spilled.append(jnp.concatenate(halves, axis=0))
    spilled = dot(target, jnp.concatenate(spilled, axis=1))
    grids = []
    for k in range(per):
        grid = sides[:, k * tiles : (k + 1) * tiles, :].reshape(nq, LANES)
        grids.append((grid + spilled[:, k * LANES : (k + 1) * LANES]).T)
    inner = dot(jnp.concatenate(grids, axis=0), circle[...])
    turn_cos, turn_sin = twiddle[:, :nq], twiddle[:, nq:]
    turned = []
    for k in range(per):
        cos_part = inner[k * LANES : (k + 1) * LANES, :nq]
        sin_part = inner[k * LANES : (k + 1) * LANES, nq:]
        turned.append(cos_part * turn_cos - sin_part * turn_sin)
        turned.append(-(sin_part * turn_cos + cos_part * turn_sin))
    outer = dot(short[...], jnp.concatenate(turned, axis=1))
    for copy in scalars:
        copy.wait()
    mode = row_iota((upper, nq)) * nq + lane_iota((upper, nq))
    cos_one, sin_one = steps[0:upper, :nq], steps[0:upper, nq:]
    cos_two, sin_two = steps[upper:, :nq], steps[upper:, nq:]
    for k in range(per):
        at = 2 * k * nq
        real = outer[:upper, at : at + nq] + outer[upper:, at + nq : at + 2 * nq]
        imag = outer[:upper, at + nq : at + 2 * nq] - outer[upper:, at : at + nq]
        x = jnp.full((upper, nq), -remainder[me * per + k], F32)
        w_next = x * (x + 1.0) * (x + 2.0) / 6.0
        w_here = -(x - 1.0) * (x + 1.0) * (x + 2.0) / 2.0
        w_prev = (x - 1.0) * x * (x + 2.0) / 2.0
        w_prev_two = -(x - 1.0) * x * (x + 1.0) / 6.0
        tap_cos = w_here + (w_next + w_prev) * cos_one + w_prev_two * cos_two
        tap_sin = (w_prev - w_next) * sin_one + w_prev_two * sin_two
        phase = lax.rem(mode * shift[me * per + k], length)
        phase = jnp.where(phase > length // 2, phase - length, phase)
        angle = phase.astype(F32) * (2.0 * math.pi / length)
        spin_cos, spin_sin = jnp.cos(angle), jnp.sin(angle)
        gain_cos = tap_cos * spin_cos - tap_sin * spin_sin
        gain_sin = tap_sin * spin_cos + tap_cos * spin_sin
        rows_out[:, k, :] = real * gain_cos + imag * gain_sin
        rows_out[:, per + k, :] = imag * gain_cos - real * gain_sin
    share = rad_count * sources // upper
    for rad in range(rad_count):
        for a in range(sources):
            at = (a * rad_count + rad) * 2 * per
            value = rows_out[(rad * sources + a) // share]
            out[at : at + 2 * per, :] = value.astype(BF16).astype(F32)


def pick(values, index):
    chosen = values[0]
    for i, value in enumerate(values[1:]):
        chosen = jnp.where(index == i + 1, value, chosen)
    return chosen


def route_kernel(size, middle, inner, where, ring, *rest):
    count = (len(rest) - 1 - size)
    sources, outs, sorted_rows = rest[:count], rest[count:-1], rest[-1]
    for i, source in enumerate(sources):
        value = source[...]
        for m in range(middle):
            for dest in range(size):
                at = (m * size + dest) * inner
                to = (i * middle + m) * inner
                sorted_rows[dest, to : to + inner, :] = value[at : at + inner, :]
    choices = [sorted_rows[dest] for dest in range(size)]
    index = where()
    for offset, out in enumerate(outs):
        out[...] = pick(choices, sent_to(index, offset, size, ring))


def halve_kernel(inner, *rest):
    rad_count = lax.axis_size("rad")
    outs, sorted_rows = rest[-1 - rad_count : -1], rest[-1]
    to = 0
    for source in rest[: -1 - rad_count]:
        value = source[...]
        for m in range(value.shape[0] // (rad_count * inner)):
            for rad in range(rad_count):
                at = (m * rad_count + rad) * inner
                sorted_rows[rad, to : to + inner, :] = value[at : at + inner, :]
            to += inner
    choices = [sorted_rows[rad] for rad in range(rad_count)]
    for offset, out in enumerate(outs):
        out[...] = pick(choices, sent_to(lax.axis_index("rad"), offset, rad_count, False))


def arrival_source(slow, fast, axis_iota):
    rad_count = lax.axis_size("rad")
    azi, rad = lax.axis_index("azi"), lax.axis_index("rad")
    from_rad = came_from(rad, axis_iota % rad_count, rad_count, False)
    from_fast = came_from(azi % fast, axis_iota // rad_count % fast, fast, False)
    from_slow = came_from(azi // fast, axis_iota // (rad_count * fast) % slow, slow, True)
    return (from_rad * slow + from_slow) * fast + from_fast


def couple_kernel(per, local, fast, slow, kernel, mixed, *rest):
    rad_count = lax.axis_size("rad")
    columns, outs, (tables, factor) = rest[:rad_count], rest[rad_count:-2], rest[-2:]
    sources = slow * fast * rad_count
    nq = columns[0].shape[1]
    total = sources * per
    me = lax.axis_index("rad") * lax.axis_size("azi") + lax.axis_index("azi")
    offset = lax.rem(me * local, nq)
    row, col = row_iota((total, total)), lane_iota((total, total))
    place = col % sources
    azi_count = slow * fast
    place = place % azi_count * rad_count + place // azi_count
    source = arrival_source(slow, fast, place)
    spread = (row == source * per + col // sources).astype(F32)
    lane = lane_iota((total, nq))
    sides = []
    for c in range(2):
        stacked = jnp.concatenate(
            [
                ref[pl.ds(c * per + k, slow * fast, stride=2 * per), :]
                for k in range(per)
                for ref in columns
            ],
            axis=0,
        )
        ordered = jnp.dot(spread, stacked, preferred_element_type=F32)
        sides.append(pltpu.roll(ordered, lax.rem(nq - offset + c * local, nq), 1))
    weights = jnp.where(lane < local, sides[0], sides[1]).astype(BF16)
    result = jnp.zeros((total, nq), F32)
    for m in range(local):
        product = jnp.dot(kernel[m], weights, preferred_element_type=F32)
        result = jnp.where((lane == m) | (lane == local + m), product, result)
    rad = lax.axis_index("rad")
    share = total // len(outs)
    slabs = [result[i * share : (i + 1) * share, :] for i in range(len(outs))]
    for offset, out in enumerate(outs):
        out[...] = pick(slabs, sent_to(rad, offset, len(outs), False))
    share = nq // local
    source = arrival_source(slow, fast, row_iota((sources, sources)))
    order = (source == lane_iota((sources, sources))).astype(F32)
    ordered = jnp.dot(order, mixed[...], precision=EXACT, preferred_element_type=F32)
    own = arrival_source(slow, fast, row_iota(ordered.shape)) % share
    tables[...] = jnp.concatenate([jnp.where(own == h, ordered, 0.0) for h in range(share)], axis=1)
    source = arrival_source(slow, fast, row_iota((sources, nq)))
    constant = (source == 0) & (lane_iota((sources, nq)) % local == 0)
    factor[...] = jnp.where(constant, 1.0, 2.0) / (nq * LANES)


def three_pass_dot(left, right):
    dot = functools.partial(jnp.dot, preferred_element_type=F32)
    left_high, right_high = left.astype(BF16), right.astype(BF16)
    left_low = (left - left_high.astype(F32)).astype(BF16)
    right_low = (right - right_high.astype(F32)).astype(BF16)
    return dot(left_high, right_high) + (dot(left_low, right_high) + dot(left_high, right_low))


def settle_kernel(per, bulk, top, rho, ur, up, near, sems):
    nz = rho.shape[0]
    sources, _, seg = bulk.shape
    group = nz * per
    unit = jnp.concatenate([top[0:1, :] * (GAIN / TOP)] * (seg // LANES), axis=1)
    half = sources // 2 * per
    copies = [
        pltpu.make_async_copy(
            near.at[c, :, pl.ds(i * half, half), :], far.at[:, pl.ds(i * half, half), :], sems.at[2 * c + i]
        )
        for c, far in enumerate((rho, ur, up))
        for i in range(2)
    ]
    for c in range(3):
        for a in range(sources):
            value = decode(bulk[a, c * group : (c + 1) * group, :].astype(F32), unit)
            for z in range(nz):
                near[c, z, a * per : (a + 1) * per, :] = value[z * per : (z + 1) * per, :]
            if (a + 1) * per % half == 0:
                copies[2 * c + a * per // half].start()
    for copy in copies:
        copy.wait()


def inverse_kernel(per, local, circle, twiddle, tables, factor, *rest):
    blocks, out = rest[:-1], rest[-1]
    slow = len(blocks)
    nq = circle.shape[0]
    share = nq // local
    count = tables.shape[0]
    picked = []
    for k in range(per):
        rows = [
            ref[pl.ds(k, count // slow, stride=per), :] if per > 1 else ref[...] for ref in blocks
        ]
        picked.append(jnp.concatenate(rows, axis=0) * factor[...])
    mid = three_pass_dot(jnp.concatenate(picked, axis=1).T, tables[...])
    turn_cos, turn_sin = twiddle[:, :LANES], twiddle[:, LANES:]
    turned = []
    for k in range(per):
        real, imag = [], []
        for h in range(share):
            at = 2 * LANES * h
            upper = mid[k * nq : k * nq + local, at : at + 2 * LANES]
            lower = mid[k * nq + local : k * nq + 2 * local, at : at + 2 * LANES]
            real.append(upper[:, :LANES] - lower[:, LANES:])
            imag.append(upper[:, LANES:] + lower[:, :LANES])
        real = jnp.concatenate(real, axis=0)
        imag = jnp.concatenate(imag, axis=0)
        pair = [real * turn_cos - imag * turn_sin, -(real * turn_sin + imag * turn_cos)]
        turned.append(jnp.concatenate(pair, axis=0))
    wave = three_pass_dot(circle[...], jnp.concatenate(turned, axis=1))
    for k in range(per):
        for q in range(nq):
            out[k : k + 1, q * LANES : (q + 1) * LANES] = wave[
                q : q + 1, k * LANES : (k + 1) * LANES
            ]


def cos_sin(rows, columns, length):
    steps = np.outer(rows, columns) % length
    angle = 2.0 * np.pi * steps / length
    return np.cos(angle).astype(np.float32), np.sin(angle).astype(np.float32)


def call(body, out_shape, in_specs=None, out_specs=None, scratch=(), name=None, aliases=None, room=40 * 2**20, **cost):
    kernel = pl.pallas_call(
        body,
        out_shape=out_shape,
        **({} if in_specs is None else {"in_specs": in_specs}),
        **({} if out_specs is None else {"out_specs": out_specs}),
        scratch_shapes=list(scratch),
        input_output_aliases=aliases or {},
        compiler_params=pltpu.CompilerParams(vmem_limit_bytes=VMEM_BYTES - room),
        cost_estimate=pl.CostEstimate(**{"flops": 0, "bytes_accessed": 0, "transcendentals": 0, **cost}),
    )

    def run(*operands):
        places = [
            None if x.ndim == 1 else pltpu.HBM if name in ("edges", "interior") else pltpu.VMEM
            for x in operands
        ]
        near = [
            x if place is None else pltpu.with_memory_space_constraint(x, place)
            for x, place in zip(operands, places)
        ]
        return kernel(*near)

    return run


def exchange(array, axes):
    return lax.all_to_all(array, axes, 0, 0, tiled=True)


def shape_of(shape, dtype=F32):
    return jax.ShapeDtypeStruct(shape, dtype)


def body(density, radial_velocity, azimuthal_velocity, cycle_shift, remainder, kernel):
    nz, slab, seg = density.shape
    azi, rad = lax.axis_size("azi"), lax.axis_size("rad")
    devices = azi * rad
    per = slab // azi
    tiles = seg // LANES
    length = seg * azi
    nq = length // LANES
    local = kernel.shape[0]
    modes = local * devices
    upper = modes // nq
    width = seg + LANES
    group = nz * per
    stride = -(-3 * group // SUB) * SUB
    rows = tiles * stride
    side = side_rows(per, tiles)
    fast = min(4, azi)
    slow = azi // fast
    vmem, smem = pl.BlockSpec(memory_space=pltpu.VMEM), pl.BlockSpec(memory_space=pltpu.SMEM)

    fields = (density, radial_velocity, azimuthal_velocity)
    anywhere = pl.BlockSpec(memory_space=pl.ANY)
    far = pl.BlockSpec(memory_space=pltpu.HBM)
    edge = pltpu.VMEM((3, nz, 2, seg), F32)
    tail, head = call(
        edges_kernel,
        (edge, edge),
        in_specs=[far] * 3,
        scratch=(
            pltpu.VMEM((3, nz, SUB, seg), F32),
            pltpu.VMEM((3, nz, SUB, seg), F32),
            pltpu.SemaphoreType.DMA((6,)),
        ),
        name="edges",
        bytes_accessed=24 * nz * SUB * seg,
    )(*fields)
    low = lax.ppermute(tail, "rad", [(i, (i + 1) % rad) for i in range(rad)])
    high = lax.ppermute(head, "rad", [((i + 1) % rad, i) for i in range(rad)])
    padded = pltpu.VMEM((3, nz, slab + SUB, width), F32)
    field, stage = call(
        interior_kernel,
        (padded, padded),
        in_specs=[far] * 3,
        scratch=(pltpu.SemaphoreType.DMA((3,)),),
        name="interior",
        bytes_accessed=12 * nz * slab * seg,
    )(*fields)
    bulk, surf, *_ = call(
        functools.partial(hydro_kernel, per, seg),
        (pltpu.HBM((azi, rows, LANES), BF16), pltpu.VMEM((azi, side, LANES), F32), padded, padded),
        out_specs=(far, vmem, vmem, vmem),
        aliases={0: 2, 1: 3},
        scratch=(
            pltpu.VMEM((azi, rows, LANES), F32),
            pltpu.VMEM((azi, rows, LANES), BF16),
            pltpu.SemaphoreType.DMA((slab // SUB,)),
        ),
        name="hydro",
        flops=100 * 3 * nz * slab * seg,
        bytes_accessed=24 * nz * slab * seg,
    )(field, stage, low, high)

    def hop(buffers, axis, size, step, ring=False):
        around = range(lax.axis_size(axis))
        return [buffers[0]] + [
            lax.ppermute(buffers[o], axis, [
                (i, i + (sent_to(i // step % size, o, size, ring) - i // step % size) * step)
                for i in around
            ])
            for o in range(1, size)
        ]

    def route(buffers, size, inner, step, name, ring=False):
        count = buffers[0].shape[0]
        lines = len(buffers) * count // size
        where = lambda: lax.axis_index("azi") // step % size
        buffers = call(
            functools.partial(route_kernel, size, count // (size * inner), inner, where, ring),
            tuple(pltpu.VMEM((lines, LANES), F32) for _ in range(size)),
            scratch=(pltpu.VMEM((size, lines, LANES), F32),),
            name="route_" + name,
            bytes_accessed=100_000,
        )(*buffers)
        return hop(buffers, "azi", size, step, ring)

    surf = [surf.reshape(azi * side, LANES)]
    surf = route(surf, slow, fast * side, fast, "surf_slow", ring=True)
    bulk = exchange(bulk, "azi")
    surf = route(surf, fast, side, 1, "surf_fast")
    surf = [x.reshape(slow, side, LANES) for x in surf]

    k_id, l_id = np.arange(nq), np.arange(LANES)
    circle = np.concatenate(cos_sin(k_id, k_id, nq), axis=1)
    twiddle = np.concatenate(cos_sin(l_id, k_id, length), axis=1)
    short = np.concatenate(cos_sin(np.arange(upper), l_id, LANES), axis=0)
    m_id = np.arange(modes)
    steps = [np.concatenate([t.reshape(upper, nq) for t in cos_sin(m_id, [n], length)], 1) for n in (1, 2)]
    steps = np.concatenate(steps, axis=0)
    spectrum, sides = call(
        functools.partial(forward_kernel, per, nz, modes, fast),
        (
            pltpu.VMEM((devices * 2 * per, nq), F32),
            pltpu.VMEM((azi, side, LANES), F32),
        ),
        in_specs=[anywhere] * 2 + [vmem] * (4 + fast),
        scratch=(
            pltpu.VMEM((upper, 2 * per, nq), F32),
            pltpu.SMEM((slab,), jnp.int32),
            pltpu.SMEM((slab,), F32),
            pltpu.SemaphoreType.DMA((2,)),
        ),
        name="forward",
        flops=100_000_000,
        bytes_accessed=1_000_000,
    )(cycle_shift, remainder, jnp.asarray(circle), jnp.asarray(twiddle), jnp.asarray(short), jnp.asarray(steps), *surf)
    columns = route([spectrum], fast, rad * 2 * per, 1, "column_fast")
    columns = route(columns, slow, rad * 2 * per, fast, "column_slow", ring=True)
    columns = call(
        functools.partial(halve_kernel, 2 * per),
        tuple(pltpu.VMEM((azi * 2 * per, nq), F32) for _ in range(rad)),
        scratch=(pltpu.VMEM((rad, azi * 2 * per, nq), F32),),
        name="route_column_rad",
        bytes_accessed=100_000,
    )(*columns)
    columns = hop(columns, "rad", rad, 1)
    j_of_block = np.arange(devices) * local // nq
    mixed = np.concatenate(cos_sin(j_of_block, l_id, LANES), axis=1)
    *blocks, tables, factor = call(
        functools.partial(couple_kernel, per, local, fast, slow),
        (
            *(pltpu.VMEM((azi * per, nq), F32) for _ in range(rad)),
            pltpu.VMEM((devices, nq // local * 2 * LANES), F32),
            pltpu.VMEM((devices, nq), F32),
        ),
        name="couple",
        flops=100_000_000,
        bytes_accessed=1_000_000,
    )(kernel, jnp.asarray(mixed), *columns)
    blocks = hop(blocks, "rad", rad, 1)
    blocks = route(blocks, fast, per, 1, "block_fast")
    blocks = route(blocks, slow, per, fast, "block_slow", ring=True)

    moved, top = call(
        functools.partial(advect_kernel, per, nz),
        (pltpu.HBM((azi, 3 * group, seg), BF16), pltpu.VMEM((SUB, LANES), F32)),
        in_specs=[anywhere, anywhere, vmem, vmem],
        out_specs=(far, vmem),
        scratch=(
            pltpu.VMEM((3, nq, group, LANES), F32),
            pltpu.VMEM((3, nq, group, LANES), F32),
            pltpu.VMEM((3, azi, group, LANES), F32),
            pltpu.VMEM((azi, 3 * group, seg), BF16),
            pltpu.SMEM((slab,), jnp.int32),
            pltpu.SMEM((slab,), F32),
            pltpu.SemaphoreType.DMA((2,)),
            pltpu.SemaphoreType.DMA((azi,)),
        ),
        name="advect",
        flops=50 * 3 * nz * slab * seg,
        bytes_accessed=12 * nz * slab * seg,
    )(cycle_shift, remainder, bulk, sides)
    moved = exchange(moved, "azi")
    turn = np.concatenate(cos_sin(k_id, l_id, length), axis=1)
    potential = call(
        functools.partial(inverse_kernel, per, local),
        shape_of((per, length)),
        name="inverse",
        flops=100_000_000,
        bytes_accessed=1_000_000,
    )(jnp.asarray(circle), jnp.asarray(turn), tables, factor, *blocks)
    results = call(
        functools.partial(settle_kernel, per),
        tuple(pltpu.HBM((nz, slab, seg), F32) for _ in range(3)),
        out_specs=(far,) * 3,
        scratch=(pltpu.VMEM((3, nz, slab, seg), F32), pltpu.SemaphoreType.DMA((6,))),
        name="settle",
        flops=20 * 3 * nz * slab * seg,
        bytes_accessed=18 * nz * slab * seg,
    )(moved, top)
    return (*results, potential)


def solution(mesh):
    split = P(None, "rad", "azi")
    in_specs = (split, split, split, P("rad"), P("rad"), P(("rad", "azi"), None, None))
    out_specs = (split, split, split, P(("rad", "azi"), None))

    return jax.shard_map(body, mesh=mesh, in_specs=in_specs, out_specs=out_specs, check_vma=False)
```

```python
import functools
import math

import jax
import jax.numpy as jnp
import numpy as np
from jax import lax
from jax.experimental import pallas as pl
from jax.experimental.pallas import tpu as pltpu
from jax.sharding import PartitionSpec as P


RADIAL_COURANT = 0.3
VISCOSITY = 0.08
LANES = 128
VMEM_BYTES = 67_043_328
SUB = 8
EXACT = lax.Precision.HIGHEST
F32 = jnp.float32
BF16 = jnp.bfloat16

POWER = 13
TOP = 2.0**9.69
GAIN = 1.25


def encode(value, scale):
    scaled = value * scale
    second = scaled * scaled
    fourth = second * second
    return (fourth * fourth) * (fourth * scaled)


def decode(code, scale):
    root = lax.exp2(lax.log(jnp.abs(code)) * (1.0 / (POWER * math.log(2.0)))) * scale
    return jnp.where(code < 0.0, -root, root)


def sent_to(place, offset, size, ring):
    return (place + offset) % size if ring else place ^ offset


def came_from(place, offset, size, ring):
    return (place - offset + size) % size if ring else place ^ offset


def row_iota(shape):
    return lax.broadcasted_iota(jnp.int32, shape, 0)


def lane_iota(shape):
    return lax.broadcasted_iota(jnp.int32, shape, 1)


def side_rows(per, tiles):
    return -(-(per * tiles + per) // SUB) * SUB


def edges_kernel(rho, ur, up, tail, head, last, first, sems):
    slab = rho.shape[1]
    copies = []
    for c, far in enumerate((rho, ur, up)):
        ends = (far.at[:, pl.ds(slab - SUB, SUB), :], last.at[c]), (far.at[:, pl.ds(0, SUB), :], first.at[c])
        copies += [pltpu.make_async_copy(*end, sems.at[2 * c + i]) for i, end in enumerate(ends)]
    for copy in copies:
        copy.start()
    for c in range(3):
        copies[2 * c].wait()
        tail[c] = last[c, :, SUB - 2 :, :]
        copies[2 * c + 1].wait()
        head[c] = first[c, :, 0:2, :]


def advance(ref, tile, z, slab, scale):
    _, nz, lines, width = ref.shape
    count = lines // SUB
    sub = row_iota((SUB, width))
    near_rows = row_iota((SUB, LANES))
    cycle = tile * SUB + near_rows
    cycle = jnp.where((tile == count - 1) & (near_rows >= SUB // 2), near_rows - SUB, cycle)
    cycle = lax.axis_index("rad") * slab + cycle
    radius = 1.0 + 4.0 * (cycle.astype(F32) + 0.5) / (slab * lax.axis_size("rad"))
    power = 1.0 / (radius * jnp.sqrt(radius))
    wide = lambda x: jnp.concatenate([x] * (width // LANES), axis=1)
    courant = wide((0.5 * scale) * (0.3 / radius))
    coriolis, epicycle = wide((0.2 * scale) * power), wide((0.05 * scale) * power)
    rows = lambda t: pl.ds(pl.multiple_of(t * SUB, SUB), SUB)
    here, before, after = rows(tile), rows(lax.rem(tile + count - 1, count)), rows(lax.rem(tile + 1, count))
    z_up, z_down = min(z + 1, nz - 1), max(z - 1, 0)
    center, base, rad_diff, azi_diff = [], [], [], []
    for c in range(3):
        cur = ref[c, z, here, :]
        inward = pltpu.roll(jnp.where(sub == SUB - 1, ref[c, z, before, :], cur), 1, 0)
        outward = pltpu.roll(jnp.where(sub == 0, ref[c, z, after, :], cur), SUB - 1, 0)
        ahead = pltpu.roll(cur, width - 1, 1)
        behind = pltpu.roll(cur, 1, 1)
        near = ref[c, z_up, here, :] + ref[c, z_down, here, :] + inward + outward + ahead + behind
        base.append((scale * VISCOSITY) * near + (scale * (1.0 - 6.0 * VISCOSITY)) * cur)
        rad_diff.append(outward - inward)
        azi_diff.append(ahead - behind)
        center.append(cur)
    half = 0.5 * scale * RADIAL_COURANT
    return (
        base[0] - (half * rad_diff[1] + courant * azi_diff[2]),
        base[1] + coriolis * center[2] - half * rad_diff[0],
        base[2] - epicycle * center[1] - courant * azi_diff[0],
    )


def store_section(field, stage, slab, tile):
    for z in range(field.shape[1]):
        for c, value in enumerate(advance(field, tile, z, slab, 1.0)):
            stage[c, z, pl.ds(pl.multiple_of(tile * SUB, SUB), SUB), :] = value


def interior_kernel(rho, ur, up, field, stage, sems):
    nz, slab, seg = rho.shape
    copies = [
        pltpu.make_async_copy(far, field.at[c, :, pl.ds(0, slab), pl.ds(0, seg)], sems.at[c])
        for c, far in enumerate((rho, ur, up))
    ]
    for copy in copies:
        copy.start()
    lines, width = field.shape[2:]
    for c in range(3):
        for z in range(nz):
            field[c, z, :, seg:width] = jnp.zeros((lines, width - seg), F32)
    for copy in copies:
        copy.wait()

    def section(tile, carry):
        store_section(field, stage, slab, tile)
        return carry

    lax.fori_loop(1, slab // SUB - 1, section, 0)


def hydro_kernel(
    per, seg, field_in, stage_in, low, high, bulk, surf, field, stage, block, narrow, sems
):
    _, nz, lines, width = field.shape
    slab = lines - SUB
    last = slab // SUB
    tiles = seg // LANES
    rad = lax.axis_index("rad")
    rad_count = lax.axis_size("rad")
    for c in range(3):
        for z in range(nz):
            inner = jnp.broadcast_to(field[c, z, 0:1, 0:seg], (2, seg))
            outer = jnp.broadcast_to(field[c, z, slab - 1 : slab, 0:seg], (2, seg))
            outward = jnp.where(rad == rad_count - 1, outer, high[c, z])
            inward = jnp.where(rad == 0, inner, low[c, z])
            between = jnp.zeros((SUB - 4, seg), F32)
            field[c, z, slab:lines, 0:seg] = jnp.concatenate([outward, between, inward], axis=0)

    def section(index, carry):
        store_section(field, stage, slab, lax.rem(index + last - 1, last + 1))
        return carry

    lax.fori_loop(0, 3, section, 0)

    @pl.when(rad == 0)
    def _():
        for c in range(3):
            for z in range(nz):
                stage[c, z, lines - 1 : lines, :] = stage[c, z, 0:1, :]

    @pl.when(rad == rad_count - 1)
    def _():
        for c in range(3):
            for z in range(nz):
                stage[c, z, slab : slab + 1, :] = stage[c, z, slab - 1 : slab, :]

    def second_section(tile, largest):
        here = pl.ds(pl.multiple_of(tile * SUB, SUB), SUB)
        for z in range(nz):
            for c, value in enumerate(advance(stage, tile, z, slab, 0.5)):
                value = 0.5 * field[c, z, here, :] + value
                field[c, z, here, :] = value
                largest = jnp.maximum(largest, jnp.abs(value))
        return largest

    largest = lax.fori_loop(0, last, second_section, jnp.zeros((SUB, width), F32))
    peak = jnp.maximum(jnp.max(largest, keepdims=True), 1e-30)
    scale = TOP / peak
    dests = SUB // per
    stride = -(-3 * nz * per // SUB) * SUB

    def send(index):
        at = pl.ds(index * dests, dests)
        return pltpu.make_async_copy(narrow.at[at], bulk.at[at], sems.at[index])

    def pack(tile, carry):
        here = pl.ds(pl.multiple_of(tile * SUB, SUB), SUB)
        overflow = jnp.zeros((SUB, LANES), F32)
        column = jnp.zeros((SUB, seg), F32)
        for c in range(3):
            for z in range(nz):
                value = field[c, z, here, 0:seg]
                if c == 0:
                    column = column + value
                code = encode(value, scale)
                plane = c * nz + z
                for d in range(dests):
                    for b in range(tiles):
                        line = b * stride + plane * per
                        block[tile * dests + d, line : line + per, :] = code[
                            d * per : (d + 1) * per, b * LANES : (b + 1) * LANES
                        ]
                overflow = overflow + pltpu.roll(field[c, z, here, seg:width], 2 + 4 * plane, 1)
        overflow = jnp.where(lane_iota((SUB, LANES)) < LANES // 2, overflow, peak)
        for d in range(dests):
            dest = tile * dests + d
            for k in range(per):
                row = d * per + k
                for b in range(tiles):
                    surf[dest, k * tiles + b : k * tiles + b + 1, :] = column[
                        row : row + 1, b * LANES : (b + 1) * LANES
                    ]
                line = per * tiles + k
                surf[dest, line : line + 1, :] = overflow[row : row + 1, :]
        for d in range(dests):
            dest = tile * dests + d
            narrow[dest] = block[dest].astype(BF16)
        send(tile).start()
        return carry

    lax.fori_loop(0, last, pack, 0)
    for index in range(last):
        send(index).wait()


def advect_kernel(
    per, nz, far_shift, far_remainder, bulk, sides, out, top,
    ring, tapped, over, codes, shift, remainder, scalar_sems, sems,
):
    scalars = [
        pltpu.make_async_copy(far, near, scalar_sems.at[i])
        for i, (far, near) in enumerate(((far_shift, shift), (far_remainder, remainder)))
    ]
    for copy in scalars:
        copy.start()
    sources = bulk.shape[0]
    count = ring.shape[1]
    tiles = count // sources
    group = nz * per
    stride = -(-3 * group // SUB) * SUB
    me = lax.axis_index("azi")

    def widen(a, peak):
        whole_block = bulk[a].astype(F32)
        packed = sides[a, per * tiles : per * tiles + per, :]
        mine = jnp.where(lane_iota((1, LANES)) >= LANES // 2, packed[0:1, :], 0.0)
        mine = jnp.max(mine, keepdims=True)
        unit = mine * (1.0 / TOP)
        for b in range(tiles):
            value = decode(whole_block[b * stride : (b + 1) * stride, :], unit)
            for c in range(3):
                ring[c, a * tiles + b] = value[c * group : (c + 1) * group, :]
        for c in range(3):
            for z in range(nz):
                turned = pltpu.roll(packed, LANES - 2 - 4 * (c * nz + z), 1)
                over[c, a, z * per : (z + 1) * per, :] = turned
        return jnp.maximum(peak, mine)

    peak = lax.fori_loop(0, sources, widen, jnp.zeros((1, 1), F32), unroll=8)
    top[...] = jnp.broadcast_to(peak, top.shape)
    lane = lane_iota((group, LANES))
    cycle = row_iota((group, LANES)) % per

    def spill(a, carry):
        after = lax.rem((a + 1) * tiles, count)
        before = lax.rem(a * tiles + count - 1, count)
        for c in range(3):
            extra = over[c, a]
            ring[c, after] = ring[c, after] + jnp.where(lane < 2, extra, 0.0)
            ring[c, before] = ring[c, before] + jnp.where(lane >= LANES - 2, extra, 0.0)
        return carry

    lax.fori_loop(0, sources, spill, 0, unroll=16)
    for copy in scalars:
        copy.wait()
    x = jnp.zeros((group, LANES), F32)
    whole, part = [], []
    for k in range(per):
        x = jnp.where(cycle == k, -remainder[me * per + k], x)
        amount = shift[me * per + k]
        whole.append(amount // LANES)
        part.append(lax.rem(amount, LANES))
    w_next = x * (x + 1.0) * (x + 2.0) / 6.0
    w_here = -(x - 1.0) * (x + 1.0) * (x + 2.0) / 2.0
    w_prev = (x - 1.0) * x * (x + 2.0) / 2.0
    w_prev_two = -(x - 1.0) * x * (x + 1.0) / 6.0

    def tap(a, carry):
        before = lax.rem(a * tiles + count - 1, count)
        after = lax.rem((a + 1) * tiles, count)
        for c in range(3):
            line = [ring[c, before]]
            line += [ring[c, a * tiles + b] for b in range(tiles)]
            line += [ring[c, after]]
            for b in range(tiles):
                prv, cur, nxt = line[b : b + 3]
                next_one = pltpu.roll(jnp.where(lane == 0, nxt, cur), LANES - 1, 1)
                prev_one = pltpu.roll(jnp.where(lane == LANES - 1, prv, cur), 1, 1)
                prev_two = pltpu.roll(jnp.where(lane >= LANES - 2, prv, cur), 2, 1)
                tapped[c, a * tiles + b] = (
                    w_next * next_one + w_here * cur + w_prev * prev_one + w_prev_two * prev_two
                )
        return carry

    lax.fori_loop(0, sources, tap, 0, unroll=8)
    scale = (TOP / GAIN) / peak

    def send(dest):
        return pltpu.make_async_copy(codes.at[dest], out.at[dest], sems.at[dest])

    def turned_tile(c, k, t):
        source = lax.rem(t - whole[k] + 2 * count, count)
        return pltpu.roll(tapped[c, source], part[k], 1)

    def turn(dest, carry):
        carry = list(carry)
        pieces = [[None] * tiles for _ in range(3)]
        for b in range(tiles):
            t = dest * tiles + b
            for c in range(3):
                joined = jnp.zeros((group, LANES), F32)
                for k in range(per):
                    now = turned_tile(c, k, t)
                    value = jnp.where(lane < part[k], carry[c * per + k], now)
                    joined = value if per == 1 else jnp.where(cycle == k, value, joined)
                    carry[c * per + k] = now
                pieces[c][b] = encode(joined, scale)
        columns = [jnp.concatenate([pieces[c][b] for b in range(tiles)], axis=1) for c in range(3)]
        codes[dest] = jnp.concatenate(columns, axis=0).astype(BF16)
        send(dest).start()
        return tuple(carry)

    start = tuple(turned_tile(c, k, -1) for c in range(3) for k in range(per))
    lax.fori_loop(0, sources, turn, start, unroll=8)
    for dest in range(sources):
        send(dest).wait()


def forward_kernel(per, nz, modes, fast, far_shift, far_remainder, circle, twiddle, short, steps, *rest):
    rad_count = lax.axis_size("rad")
    hops, (out, sides, rows_out, shift, remainder, scalar_sems) = rest[:fast], rest[fast:]
    scalars = [
        pltpu.make_async_copy(far, near, scalar_sems.at[i])
        for i, (far, near) in enumerate(((far_shift, shift), (far_remainder, remainder)))
    ]
    for copy in scalars:
        copy.start()
    me = lax.axis_index("azi")
    azi = lax.axis_index("azi")
    for o_fast, hop in enumerate(hops):
        for o_slow in range(hop.shape[0]):
            from_slow = came_from(azi // fast, o_slow, hop.shape[0], True)
            from_fast = came_from(azi % fast, o_fast, fast, False)
            sides[from_slow * fast + from_fast] = hop[o_slow]
    sources = sides.shape[0]
    nq = circle.shape[0]
    tiles = nq // sources
    length = nq * LANES
    upper = modes // nq
    lane = lane_iota((sources, LANES))
    q_id, a_id = row_iota((nq, 2 * sources)), lane_iota((nq, 2 * sources))
    after = lax.rem((a_id + 1) * tiles, nq)
    before = lax.rem((a_id - sources) * tiles + nq - 1, nq)
    target = (q_id == jnp.where(a_id < sources, after, before)).astype(F32)
    dot = functools.partial(jnp.dot, precision=EXACT, preferred_element_type=F32)
    spilled = []
    for k in range(per):
        packed = sides[:, per * tiles + k, :]
        extra = jnp.zeros((sources, LANES), F32)
        for z in range(nz):
            extra = extra + pltpu.roll(packed, LANES - 2 - 4 * z, 1)
        halves = (jnp.where(lane < 2, extra, 0.0), jnp.where(lane >= LANES - 2, extra, 0.0))
        spilled.append(jnp.concatenate(halves, axis=0))
    spilled = dot(target, jnp.concatenate(spilled, axis=1))
    grids = []
    for k in range(per):
        grid = sides[:, k * tiles : (k + 1) * tiles, :].reshape(nq, LANES)
        grids.append((grid + spilled[:, k * LANES : (k + 1) * LANES]).T)
    inner = dot(jnp.concatenate(grids, axis=0), circle[...])
    turn_cos, turn_sin = twiddle[:, :nq], twiddle[:, nq:]
    turned = []
    for k in range(per):
        cos_part = inner[k * LANES : (k + 1) * LANES, :nq]
        sin_part = inner[k * LANES : (k + 1) * LANES, nq:]
        turned.append(cos_part * turn_cos - sin_part * turn_sin)
        turned.append(-(sin_part * turn_cos + cos_part * turn_sin))
    outer = dot(short[...], jnp.concatenate(turned, axis=1))
    for copy in scalars:
        copy.wait()
    mode = row_iota((upper, nq)) * nq + lane_iota((upper, nq))
    cos_one, sin_one = steps[0:upper, :nq], steps[0:upper, nq:]
    cos_two, sin_two = steps[upper:, :nq], steps[upper:, nq:]
    for k in range(per):
        at = 2 * k * nq
        real = outer[:upper, at : at + nq] + outer[upper:, at + nq : at + 2 * nq]
        imag = outer[:upper, at + nq : at + 2 * nq] - outer[upper:, at : at + nq]
        x = jnp.full((upper, nq), -remainder[me * per + k], F32)
        w_next = x * (x + 1.0) * (x + 2.0) / 6.0
        w_here = -(x - 1.0) * (x + 1.0) * (x + 2.0) / 2.0
        w_prev = (x - 1.0) * x * (x + 2.0) / 2.0
        w_prev_two = -(x - 1.0) * x * (x + 1.0) / 6.0
        tap_cos = w_here + (w_next + w_prev) * cos_one + w_prev_two * cos_two
        tap_sin = (w_prev - w_next) * sin_one + w_prev_two * sin_two
        phase = lax.rem(mode * shift[me * per + k], length)
        phase = jnp.where(phase > length // 2, phase - length, phase)
        angle = phase.astype(F32) * (2.0 * math.pi / length)
        spin_cos, spin_sin = jnp.cos(angle), jnp.sin(angle)
        gain_cos = tap_cos * spin_cos - tap_sin * spin_sin
        gain_sin = tap_sin * spin_cos + tap_cos * spin_sin
        rows_out[:, k, :] = real * gain_cos + imag * gain_sin
        rows_out[:, per + k, :] = imag * gain_cos - real * gain_sin
    share = rad_count * sources // upper
    for rad in range(rad_count):
        for a in range(sources):
            at = (a * rad_count + rad) * 2 * per
            value = rows_out[(rad * sources + a) // share]
            out[at : at + 2 * per, :] = value.astype(BF16).astype(F32)


def pick(values, index):
    chosen = values[0]
    for i, value in enumerate(values[1:]):
        chosen = jnp.where(index == i + 1, value, chosen)
    return chosen


def route_kernel(size, middle, inner, where, ring, *rest):
    count = (len(rest) - 1 - size)
    sources, outs, sorted_rows = rest[:count], rest[count:-1], rest[-1]
    for i, source in enumerate(sources):
        value = source[...]
        for m in range(middle):
            for dest in range(size):
                at = (m * size + dest) * inner
                to = (i * middle + m) * inner
                sorted_rows[dest, to : to + inner, :] = value[at : at + inner, :]
    choices = [sorted_rows[dest] for dest in range(size)]
    index = where()
    for offset, out in enumerate(outs):
        out[...] = pick(choices, sent_to(index, offset, size, ring))


def halve_kernel(inner, *rest):
    rad_count = lax.axis_size("rad")
    outs, sorted_rows = rest[-1 - rad_count : -1], rest[-1]
    to = 0
    for source in rest[: -1 - rad_count]:
        value = source[...]
        for m in range(value.shape[0] // (rad_count * inner)):
            for rad in range(rad_count):
                at = (m * rad_count + rad) * inner
                sorted_rows[rad, to : to + inner, :] = value[at : at + inner, :]
            to += inner
    choices = [sorted_rows[rad] for rad in range(rad_count)]
    for offset, out in enumerate(outs):
        out[...] = pick(choices, sent_to(lax.axis_index("rad"), offset, rad_count, False))


def arrival_source(slow, fast, axis_iota):
    rad_count = lax.axis_size("rad")
    azi, rad = lax.axis_index("azi"), lax.axis_index("rad")
    from_rad = came_from(rad, axis_iota % rad_count, rad_count, False)
    from_fast = came_from(azi % fast, axis_iota // rad_count % fast, fast, False)
    from_slow = came_from(azi // fast, axis_iota // (rad_count * fast) % slow, slow, True)
    return (from_rad * slow + from_slow) * fast + from_fast


def couple_kernel(per, local, fast, slow, kernel, mixed, *rest):
    rad_count = lax.axis_size("rad")
    columns, outs, (tables, factor) = rest[:rad_count], rest[rad_count:-2], rest[-2:]
    sources = slow * fast * rad_count
    nq = columns[0].shape[1]
    total = sources * per
    me = lax.axis_index("rad") * lax.axis_size("azi") + lax.axis_index("azi")
    offset = lax.rem(me * local, nq)
    row, col = row_iota((total, total)), lane_iota((total, total))
    place = col % sources
    azi_count = slow * fast
    place = place % azi_count * rad_count + place // azi_count
    source = arrival_source(slow, fast, place)
    spread = (row == source * per + col // sources).astype(F32)
    lane = lane_iota((total, nq))
    sides = []
    for c in range(2):
        stacked = jnp.concatenate(
            [
                ref[pl.ds(c * per + k, slow * fast, stride=2 * per), :]
                for k in range(per)
                for ref in columns
            ],
            axis=0,
        )
        ordered = jnp.dot(spread, stacked, preferred_element_type=F32)
        sides.append(pltpu.roll(ordered, lax.rem(nq - offset + c * local, nq), 1))
    weights = jnp.where(lane < local, sides[0], sides[1]).astype(BF16)
    result = jnp.zeros((total, nq), F32)
    for m in range(local):
        product = jnp.dot(kernel[m], weights, preferred_element_type=F32)
        result = jnp.where((lane == m) | (lane == local + m), product, result)
    rad = lax.axis_index("rad")
    share = total // len(outs)
    slabs = [result[i * share : (i + 1) * share, :] for i in range(len(outs))]
    for offset, out in enumerate(outs):
        out[...] = pick(slabs, sent_to(rad, offset, len(outs), False))
    share = nq // local
    source = arrival_source(slow, fast, row_iota((sources, sources)))
    order = (source == lane_iota((sources, sources))).astype(F32)
    ordered = jnp.dot(order, mixed[...], precision=EXACT, preferred_element_type=F32)
    own = arrival_source(slow, fast, row_iota(ordered.shape)) % share
    tables[...] = jnp.concatenate([jnp.where(own == h, ordered, 0.0) for h in range(share)], axis=1)
    source = arrival_source(slow, fast, row_iota((sources, nq)))
    constant = (source == 0) & (lane_iota((sources, nq)) % local == 0)
    factor[...] = jnp.where(constant, 1.0, 2.0) / (nq * LANES)


def three_pass_dot(left, right):
    dot = functools.partial(jnp.dot, preferred_element_type=F32)
    left_high, right_high = left.astype(BF16), right.astype(BF16)
    left_low = (left - left_high.astype(F32)).astype(BF16)
    right_low = (right - right_high.astype(F32)).astype(BF16)
    return dot(left_high, right_high) + (dot(left_low, right_high) + dot(left_high, right_low))


def settle_kernel(per, bulk, top, rho, ur, up, near, sems):
    nz = rho.shape[0]
    sources, _, seg = bulk.shape
    group = nz * per
    unit = jnp.concatenate([top[0:1, :] * (GAIN / TOP)] * (seg // LANES), axis=1)
    half = sources // 2 * per
    copies = [
        pltpu.make_async_copy(
            near.at[c, :, pl.ds(i * half, half), :], far.at[:, pl.ds(i * half, half), :], sems.at[2 * c + i]
        )
        for c, far in enumerate((rho, ur, up))
        for i in range(2)
    ]
    for c in range(3):
        for a in range(sources):
            value = decode(bulk[a, c * group : (c + 1) * group, :].astype(F32), unit)
            for z in range(nz):
                near[c, z, a * per : (a + 1) * per, :] = value[z * per : (z + 1) * per, :]
            if (a + 1) * per % half == 0:
                copies[2 * c + a * per // half].start()
    for copy in copies:
        copy.wait()


def inverse_kernel(per, local, circle, twiddle, tables, factor, *rest):
    blocks, out = rest[:-1], rest[-1]
    slow = len(blocks)
    nq = circle.shape[0]
    share = nq // local
    count = tables.shape[0]
    picked = []
    for k in range(per):
        rows = [
            ref[pl.ds(k, count // slow, stride=per), :] if per > 1 else ref[...] for ref in blocks
        ]
        picked.append(jnp.concatenate(rows, axis=0) * factor[...])
    mid = three_pass_dot(jnp.concatenate(picked, axis=1).T, tables[...])
    turn_cos, turn_sin = twiddle[:, :LANES], twiddle[:, LANES:]
    turned = []
    for k in range(per):
        real, imag = [], []
        for h in range(share):
            at = 2 * LANES * h
            upper = mid[k * nq : k * nq + local, at : at + 2 * LANES]
            lower = mid[k * nq + local : k * nq + 2 * local, at : at + 2 * LANES]
            real.append(upper[:, :LANES] - lower[:, LANES:])
            imag.append(upper[:, LANES:] + lower[:, :LANES])
        real = jnp.concatenate(real, axis=0)
        imag = jnp.concatenate(imag, axis=0)
        pair = [real * turn_cos - imag * turn_sin, -(real * turn_sin + imag * turn_cos)]
        turned.append(jnp.concatenate(pair, axis=0))
    wave = three_pass_dot(circle[...], jnp.concatenate(turned, axis=1))
    for k in range(per):
        for q in range(nq):
            out[k : k + 1, q * LANES : (q + 1) * LANES] = wave[
                q : q + 1, k * LANES : (k + 1) * LANES
            ]


def cos_sin(rows, columns, length):
    steps = np.outer(rows, columns) % length
    angle = 2.0 * np.pi * steps / length
    return np.cos(angle).astype(np.float32), np.sin(angle).astype(np.float32)


def call(body, out_shape, in_specs=None, out_specs=None, scratch=(), name=None, aliases=None, room=40 * 2**20, **cost):
    kernel = pl.pallas_call(
        body,
        out_shape=out_shape,
        **({} if in_specs is None else {"in_specs": in_specs}),
        **({} if out_specs is None else {"out_specs": out_specs}),
        scratch_shapes=list(scratch),
        input_output_aliases=aliases or {},
        compiler_params=pltpu.CompilerParams(vmem_limit_bytes=VMEM_BYTES - room),
        cost_estimate=pl.CostEstimate(**{"flops": 0, "bytes_accessed": 0, "transcendentals": 0, **cost}),
    )

    def run(*operands):
        places = [
            None if x.ndim == 1 else pltpu.HBM if name in ("edges", "interior") else pltpu.VMEM
            for x in operands
        ]
        near = [
            x if place is None else pltpu.with_memory_space_constraint(x, place)
            for x, place in zip(operands, places)
        ]
        return kernel(*near)

    return run


def exchange(array, axes):
    return lax.all_to_all(array, axes, 0, 0, tiled=True)


def shape_of(shape, dtype=F32):
    return jax.ShapeDtypeStruct(shape, dtype)


def body(density, radial_velocity, azimuthal_velocity, cycle_shift, remainder, kernel):
    nz, slab, seg = density.shape
    azi, rad = lax.axis_size("azi"), lax.axis_size("rad")
    devices = azi * rad
    per = slab // azi
    tiles = seg // LANES
    length = seg * azi
    nq = length // LANES
    local = kernel.shape[0]
    modes = local * devices
    upper = modes // nq
    width = seg + LANES
    group = nz * per
    stride = -(-3 * group // SUB) * SUB
    rows = tiles * stride
    side = side_rows(per, tiles)
    fast = min(4, azi)
    slow = azi // fast
    vmem, smem = pl.BlockSpec(memory_space=pltpu.VMEM), pl.BlockSpec(memory_space=pltpu.SMEM)

    fields = (density, radial_velocity, azimuthal_velocity)
    anywhere = pl.BlockSpec(memory_space=pl.ANY)
    far = pl.BlockSpec(memory_space=pltpu.HBM)
    edge = pltpu.VMEM((3, nz, 2, seg), F32)
    tail, head = call(
        edges_kernel,
        (edge, edge),
        in_specs=[far] * 3,
        scratch=(
            pltpu.VMEM((3, nz, SUB, seg), F32),
            pltpu.VMEM((3, nz, SUB, seg), F32),
            pltpu.SemaphoreType.DMA((6,)),
        ),
        name="edges",
        bytes_accessed=24 * nz * SUB * seg,
    )(*fields)
    low = lax.ppermute(tail, "rad", [(i, (i + 1) % rad) for i in range(rad)])
    high = lax.ppermute(head, "rad", [((i + 1) % rad, i) for i in range(rad)])
    padded = pltpu.VMEM((3, nz, slab + SUB, width), F32)
    field, stage = call(
        interior_kernel,
        (padded, padded),
        in_specs=[far] * 3,
        scratch=(pltpu.SemaphoreType.DMA((3,)),),
        name="interior",
        bytes_accessed=12 * nz * slab * seg,
    )(*fields)
    bulk, surf, *_ = call(
        functools.partial(hydro_kernel, per, seg),
        (pltpu.HBM((azi, rows, LANES), BF16), pltpu.VMEM((azi, side, LANES), F32), padded, padded),
        out_specs=(far, vmem, vmem, vmem),
        aliases={0: 2, 1: 3},
        scratch=(
            pltpu.VMEM((azi, rows, LANES), F32),
            pltpu.VMEM((azi, rows, LANES), BF16),
            pltpu.SemaphoreType.DMA((slab // SUB,)),
        ),
        name="hydro",
        flops=100 * 3 * nz * slab * seg,
        bytes_accessed=24 * nz * slab * seg,
    )(field, stage, low, high)

    def hop(buffers, axis, size, step, ring=False):
        around = range(lax.axis_size(axis))
        return [buffers[0]] + [
            lax.ppermute(buffers[o], axis, [
                (i, i + (sent_to(i // step % size, o, size, ring) - i // step % size) * step)
                for i in around
            ])
            for o in range(1, size)
        ]

    def route(buffers, size, inner, step, name, ring=False):
        count = buffers[0].shape[0]
        lines = len(buffers) * count // size
        where = lambda: lax.axis_index("azi") // step % size
        buffers = call(
            functools.partial(route_kernel, size, count // (size * inner), inner, where, ring),
            tuple(pltpu.VMEM((lines, LANES), F32) for _ in range(size)),
            scratch=(pltpu.VMEM((size, lines, LANES), F32),),
            name="route_" + name,
            bytes_accessed=100_000,
        )(*buffers)
        return hop(buffers, "azi", size, step, ring)

    surf = [surf.reshape(azi * side, LANES)]
    surf = route(surf, slow, fast * side, fast, "surf_slow", ring=True)
    bulk = exchange(bulk, "azi")
    surf = route(surf, fast, side, 1, "surf_fast")
    surf = [x.reshape(slow, side, LANES) for x in surf]

    k_id, l_id = np.arange(nq), np.arange(LANES)
    circle = np.concatenate(cos_sin(k_id, k_id, nq), axis=1)
    twiddle = np.concatenate(cos_sin(l_id, k_id, length), axis=1)
    short = np.concatenate(cos_sin(np.arange(upper), l_id, LANES), axis=0)
    m_id = np.arange(modes)
    steps = [np.concatenate([t.reshape(upper, nq) for t in cos_sin(m_id, [n], length)], 1) for n in (1, 2)]
    steps = np.concatenate(steps, axis=0)
    spectrum, sides = call(
        functools.partial(forward_kernel, per, nz, modes, fast),
        (
            pltpu.VMEM((devices * 2 * per, nq), F32),
            pltpu.VMEM((azi, side, LANES), F32),
        ),
        in_specs=[anywhere] * 2 + [vmem] * (4 + fast),
        scratch=(
            pltpu.VMEM((upper, 2 * per, nq), F32),
            pltpu.SMEM((slab,), jnp.int32),
            pltpu.SMEM((slab,), F32),
            pltpu.SemaphoreType.DMA((2,)),
        ),
        name="forward",
        flops=100_000_000,
        bytes_accessed=1_000_000,
    )(cycle_shift, remainder, jnp.asarray(circle), jnp.asarray(twiddle), jnp.asarray(short), jnp.asarray(steps), *surf)
    columns = route([spectrum], fast, rad * 2 * per, 1, "column_fast")
    columns = route(columns, slow, rad * 2 * per, fast, "column_slow", ring=True)
    columns = call(
        functools.partial(halve_kernel, 2 * per),
        tuple(pltpu.VMEM((azi * 2 * per, nq), F32) for _ in range(rad)),
        scratch=(pltpu.VMEM((rad, azi * 2 * per, nq), F32),),
        name="route_column_rad",
        bytes_accessed=100_000,
    )(*columns)
    columns = hop(columns, "rad", rad, 1)
    j_of_block = np.arange(devices) * local // nq
    mixed = np.concatenate(cos_sin(j_of_block, l_id, LANES), axis=1)
    *blocks, tables, factor = call(
        functools.partial(couple_kernel, per, local, fast, slow),
        (
            *(pltpu.VMEM((azi * per, nq), F32) for _ in range(rad)),
            pltpu.VMEM((devices, nq // local * 2 * LANES), F32),
            pltpu.VMEM((devices, nq), F32),
        ),
        name="couple",
        flops=100_000_000,
        bytes_accessed=1_000_000,
    )(kernel, jnp.asarray(mixed), *columns)
    blocks = hop(blocks, "rad", rad, 1)
    blocks = route(blocks, fast, per, 1, "block_fast")
    blocks = route(blocks, slow, per, fast, "block_slow", ring=True)

    moved, top = call(
        functools.partial(advect_kernel, per, nz),
        (pltpu.HBM((azi, 3 * group, seg), BF16), pltpu.VMEM((SUB, LANES), F32)),
        in_specs=[anywhere, anywhere, vmem, vmem],
        out_specs=(far, vmem),
        scratch=(
            pltpu.VMEM((3, nq, group, LANES), F32),
            pltpu.VMEM((3, nq, group, LANES), F32),
            pltpu.VMEM((3, azi, group, LANES), F32),
            pltpu.VMEM((azi, 3 * group, seg), BF16),
            pltpu.SMEM((slab,), jnp.int32),
            pltpu.SMEM((slab,), F32),
            pltpu.SemaphoreType.DMA((2,)),
            pltpu.SemaphoreType.DMA((azi,)),
        ),
        name="advect",
        flops=50 * 3 * nz * slab * seg,
        bytes_accessed=12 * nz * slab * seg,
    )(cycle_shift, remainder, bulk, sides)
    moved = exchange(moved, "azi")
    turn = np.concatenate(cos_sin(k_id, l_id, length), axis=1)
    potential = call(
        functools.partial(inverse_kernel, per, local),
        shape_of((per, length)),
        name="inverse",
        flops=100_000_000,
        bytes_accessed=1_000_000,
    )(jnp.asarray(circle), jnp.asarray(turn), tables, factor, *blocks)
    results = call(
        functools.partial(settle_kernel, per),
        tuple(pltpu.HBM((nz, slab, seg), F32) for _ in range(3)),
        out_specs=(far,) * 3,
        scratch=(pltpu.VMEM((3, nz, slab, seg), F32), pltpu.SemaphoreType.DMA((6,))),
        name="settle",
        flops=20 * 3 * nz * slab * seg,
        bytes_accessed=18 * nz * slab * seg,
    )(moved, top)
    return (*results, potential)


def solution(mesh):
    split = P(None, "rad", "azi")
    in_specs = (split, split, split, P("rad"), P("rad"), P(("rad", "azi"), None, None))
    out_specs = (split, split, split, P(("rad", "azi"), None))

    return jax.shard_map(body, mesh=mesh, in_specs=in_specs, out_specs=out_specs, check_vma=False)
```

```python
import functools
import math

import jax
import jax.numpy as jnp
import numpy as np
from jax import lax
from jax.experimental import pallas as pl
from jax.experimental.pallas import tpu as pltpu
from jax.sharding import PartitionSpec as P


RADIAL_COURANT = 0.3
VISCOSITY = 0.08
LANES = 128
VMEM_BYTES = 67_043_328
SUB = 8
EXACT = lax.Precision.HIGHEST
F32 = jnp.float32
BF16 = jnp.bfloat16

POWER = 13
TOP = 2.0**9.69
GAIN = 1.25


def encode(value, scale):
    scaled = value * scale
    second = scaled * scaled
    fourth = second * second
    return (fourth * fourth) * (fourth * scaled)


def decode(code, scale):
    root = lax.exp2(lax.log(jnp.abs(code)) * (1.0 / (POWER * math.log(2.0)))) * scale
    return jnp.where(code < 0.0, -root, root)


def sent_to(place, offset, size, ring):
    return (place + offset) % size if ring else place ^ offset


def came_from(place, offset, size, ring):
    return (place - offset + size) % size if ring else place ^ offset


def row_iota(shape):
    return lax.broadcasted_iota(jnp.int32, shape, 0)


def lane_iota(shape):
    return lax.broadcasted_iota(jnp.int32, shape, 1)


def side_rows(per, tiles):
    return -(-(per * tiles + per) // SUB) * SUB


def load_kernel(rho, ur, up, field, tail, head, sems):
    nz, slab, seg = rho.shape
    lines, width = field.shape[2:]
    copies = [
        pltpu.make_async_copy(far, field.at[c, :, pl.ds(0, slab), pl.ds(0, seg)], sems.at[c])
        for c, far in enumerate((rho, ur, up))
    ]
    for copy in copies:
        copy.start()
    for c in range(3):
        for z in range(nz):
            field[c, z, :, seg:width] = jnp.zeros((lines, width - seg), F32)
    for c in range(3):
        copies[c].wait()
        tail[c] = field[c, :, slab - 2 : slab, 0:seg]
        head[c] = field[c, :, 0:2, 0:seg]


def advance(ref, tile, z, slab, scale):
    _, nz, lines, width = ref.shape
    count = lines // SUB
    sub = row_iota((SUB, width))
    near_rows = row_iota((SUB, LANES))
    cycle = tile * SUB + near_rows
    cycle = jnp.where((tile == count - 1) & (near_rows >= SUB // 2), near_rows - SUB, cycle)
    cycle = lax.axis_index("rad") * slab + cycle
    radius = 1.0 + 4.0 * (cycle.astype(F32) + 0.5) / (slab * lax.axis_size("rad"))
    power = 1.0 / (radius * jnp.sqrt(radius))
    wide = lambda x: jnp.concatenate([x] * (width // LANES), axis=1)
    courant = wide((0.5 * scale) * (0.3 / radius))
    coriolis, epicycle = wide((0.2 * scale) * power), wide((0.05 * scale) * power)
    rows = lambda t: pl.ds(pl.multiple_of(t * SUB, SUB), SUB)
    here, before, after = rows(tile), rows(lax.rem(tile + count - 1, count)), rows(lax.rem(tile + 1, count))
    z_up, z_down = min(z + 1, nz - 1), max(z - 1, 0)
    center, base, rad_diff, azi_diff = [], [], [], []
    for c in range(3):
        cur = ref[c, z, here, :]
        inward = pltpu.roll(jnp.where(sub == SUB - 1, ref[c, z, before, :], cur), 1, 0)
        outward = pltpu.roll(jnp.where(sub == 0, ref[c, z, after, :], cur), SUB - 1, 0)
        ahead = pltpu.roll(cur, width - 1, 1)
        behind = pltpu.roll(cur, 1, 1)
        near = ref[c, z_up, here, :] + ref[c, z_down, here, :] + inward + outward + ahead + behind
        base.append((scale * VISCOSITY) * near + (scale * (1.0 - 6.0 * VISCOSITY)) * cur)
        rad_diff.append(outward - inward)
        azi_diff.append(ahead - behind)
        center.append(cur)
    half = 0.5 * scale * RADIAL_COURANT
    return (
        base[0] - (half * rad_diff[1] + courant * azi_diff[2]),
        base[1] + coriolis * center[2] - half * rad_diff[0],
        base[2] - epicycle * center[1] - courant * azi_diff[0],
    )


def store_section(field, stage, slab, tile):
    for z in range(field.shape[1]):
        for c, value in enumerate(advance(field, tile, z, slab, 1.0)):
            stage[c, z, pl.ds(pl.multiple_of(tile * SUB, SUB), SUB), :] = value


def interior_kernel(field, stage):
    slab = field.shape[2] - SUB

    def section(tile, carry):
        store_section(field, stage, slab, tile)
        return carry

    lax.fori_loop(1, slab // SUB - 1, section, 0)


def hydro_kernel(
    per, seg, field_in, stage_in, low, high, bulk, surf, field, stage, block, narrow, sems
):
    _, nz, lines, width = field.shape
    slab = lines - SUB
    last = slab // SUB
    tiles = seg // LANES
    rad = lax.axis_index("rad")
    rad_count = lax.axis_size("rad")
    for c in range(3):
        for z in range(nz):
            inner = jnp.broadcast_to(field[c, z, 0:1, 0:seg], (2, seg))
            outer = jnp.broadcast_to(field[c, z, slab - 1 : slab, 0:seg], (2, seg))
            outward = jnp.where(rad == rad_count - 1, outer, high[c, z])
            inward = jnp.where(rad == 0, inner, low[c, z])
            between = jnp.zeros((SUB - 4, seg), F32)
            field[c, z, slab:lines, 0:seg] = jnp.concatenate([outward, between, inward], axis=0)

    def section(index, carry):
        store_section(field, stage, slab, lax.rem(index + last - 1, last + 1))
        return carry

    lax.fori_loop(0, 3, section, 0)

    @pl.when(rad == 0)
    def _():
        for c in range(3):
            for z in range(nz):
                stage[c, z, lines - 1 : lines, :] = stage[c, z, 0:1, :]

    @pl.when(rad == rad_count - 1)
    def _():
        for c in range(3):
            for z in range(nz):
                stage[c, z, slab : slab + 1, :] = stage[c, z, slab - 1 : slab, :]

    def second_section(tile, largest):
        here = pl.ds(pl.multiple_of(tile * SUB, SUB), SUB)
        for z in range(nz):
            for c, value in enumerate(advance(stage, tile, z, slab, 0.5)):
                value = 0.5 * field[c, z, here, :] + value
                field[c, z, here, :] = value
                largest = jnp.maximum(largest, jnp.abs(value))
        return largest

    largest = lax.fori_loop(0, last, second_section, jnp.zeros((SUB, width), F32))
    peak = jnp.maximum(jnp.max(largest, keepdims=True), 1e-30)
    scale = TOP / peak
    dests = SUB // per
    stride = -(-3 * nz * per // SUB) * SUB

    def send(index):
        at = pl.ds(index * dests, dests)
        return pltpu.make_async_copy(narrow.at[at], bulk.at[at], sems.at[index])

    def pack(tile, carry):
        here = pl.ds(pl.multiple_of(tile * SUB, SUB), SUB)
        overflow = jnp.zeros((SUB, LANES), F32)
        column = jnp.zeros((SUB, seg), F32)
        for c in range(3):
            for z in range(nz):
                value = field[c, z, here, 0:seg]
                if c == 0:
                    column = column + value
                code = encode(value, scale)
                plane = c * nz + z
                for d in range(dests):
                    for b in range(tiles):
                        line = b * stride + plane * per
                        block[tile * dests + d, line : line + per, :] = code[
                            d * per : (d + 1) * per, b * LANES : (b + 1) * LANES
                        ]
                overflow = overflow + pltpu.roll(field[c, z, here, seg:width], 2 + 4 * plane, 1)
        overflow = jnp.where(lane_iota((SUB, LANES)) < LANES // 2, overflow, peak)
        for d in range(dests):
            dest = tile * dests + d
            for k in range(per):
                row = d * per + k
                for b in range(tiles):
                    surf[dest, k * tiles + b : k * tiles + b + 1, :] = column[
                        row : row + 1, b * LANES : (b + 1) * LANES
                    ]
                line = per * tiles + k
                surf[dest, line : line + 1, :] = overflow[row : row + 1, :]
        for d in range(dests):
            dest = tile * dests + d
            narrow[dest] = block[dest].astype(BF16)
        send(tile).start()
        return carry

    lax.fori_loop(0, last, pack, 0)
    for index in range(last):
        send(index).wait()


def advect_kernel(
    per, nz, far_shift, far_remainder, bulk, sides, out, top,
    ring, tapped, over, codes, shift, remainder, scalar_sems, sems,
):
    scalars = [
        pltpu.make_async_copy(far, near, scalar_sems.at[i])
        for i, (far, near) in enumerate(((far_shift, shift), (far_remainder, remainder)))
    ]
    for copy in scalars:
        copy.start()
    sources = bulk.shape[0]
    count = ring.shape[1]
    tiles = count // sources
    group = nz * per
    stride = -(-3 * group // SUB) * SUB
    me = lax.axis_index("azi")

    def widen(a, peak):
        whole_block = bulk[a].astype(F32)
        packed = sides[a, per * tiles : per * tiles + per, :]
        mine = jnp.where(lane_iota((1, LANES)) >= LANES // 2, packed[0:1, :], 0.0)
        mine = jnp.max(mine, keepdims=True)
        unit = mine * (1.0 / TOP)
        for b in range(tiles):
            value = decode(whole_block[b * stride : (b + 1) * stride, :], unit)
            for c in range(3):
                ring[c, a * tiles + b] = value[c * group : (c + 1) * group, :]
        for c in range(3):
            for z in range(nz):
                turned = pltpu.roll(packed, LANES - 2 - 4 * (c * nz + z), 1)
                over[c, a, z * per : (z + 1) * per, :] = turned
        return jnp.maximum(peak, mine)

    peak = lax.fori_loop(0, sources, widen, jnp.zeros((1, 1), F32), unroll=8)
    top[...] = jnp.broadcast_to(peak, top.shape)
    lane = lane_iota((group, LANES))
    cycle = row_iota((group, LANES)) % per

    def spill(a, carry):
        after = lax.rem((a + 1) * tiles, count)
        before = lax.rem(a * tiles + count - 1, count)
        for c in range(3):
            extra = over[c, a]
            ring[c, after] = ring[c, after] + jnp.where(lane < 2, extra, 0.0)
            ring[c, before] = ring[c, before] + jnp.where(lane >= LANES - 2, extra, 0.0)
        return carry

    lax.fori_loop(0, sources, spill, 0, unroll=16)
    for copy in scalars:
        copy.wait()
    x = jnp.zeros((group, LANES), F32)
    whole, part = [], []
    for k in range(per):
        x = jnp.where(cycle == k, -remainder[me * per + k], x)
        amount = shift[me * per + k]
        whole.append(amount // LANES)
        part.append(lax.rem(amount, LANES))
    w_next = x * (x + 1.0) * (x + 2.0) / 6.0
    w_here = -(x - 1.0) * (x + 1.0) * (x + 2.0) / 2.0
    w_prev = (x - 1.0) * x * (x + 2.0) / 2.0
    w_prev_two = -(x - 1.0) * x * (x + 1.0) / 6.0

    def tap(a, carry):
        before = lax.rem(a * tiles + count - 1, count)
        after = lax.rem((a + 1) * tiles, count)
        for c in range(3):
            line = [ring[c, before]]
            line += [ring[c, a * tiles + b] for b in range(tiles)]
            line += [ring[c, after]]
            for b in range(tiles):
                prv, cur, nxt = line[b : b + 3]
                next_one = pltpu.roll(jnp.where(lane == 0, nxt, cur), LANES - 1, 1)
                prev_one = pltpu.roll(jnp.where(lane == LANES - 1, prv, cur), 1, 1)
                prev_two = pltpu.roll(jnp.where(lane >= LANES - 2, prv, cur), 2, 1)
                tapped[c, a * tiles + b] = (
                    w_next * next_one + w_here * cur + w_prev * prev_one + w_prev_two * prev_two
                )
        return carry

    lax.fori_loop(0, sources, tap, 0, unroll=8)
    scale = (TOP / GAIN) / peak

    def send(dest):
        return pltpu.make_async_copy(codes.at[dest], out.at[dest], sems.at[dest])

    def turned_tile(c, k, t):
        source = lax.rem(t - whole[k] + 2 * count, count)
        return pltpu.roll(tapped[c, source], part[k], 1)

    def turn(dest, carry):
        carry = list(carry)
        pieces = [[None] * tiles for _ in range(3)]
        for b in range(tiles):
            t = dest * tiles + b
            for c in range(3):
                joined = jnp.zeros((group, LANES), F32)
                for k in range(per):
                    now = turned_tile(c, k, t)
                    value = jnp.where(lane < part[k], carry[c * per + k], now)
                    joined = value if per == 1 else jnp.where(cycle == k, value, joined)
                    carry[c * per + k] = now
                pieces[c][b] = encode(joined, scale)
        columns = [jnp.concatenate([pieces[c][b] for b in range(tiles)], axis=1) for c in range(3)]
        codes[dest] = jnp.concatenate(columns, axis=0).astype(BF16)
        send(dest).start()
        return tuple(carry)

    start = tuple(turned_tile(c, k, -1) for c in range(3) for k in range(per))
    lax.fori_loop(0, sources, turn, start, unroll=8)
    for dest in range(sources):
        send(dest).wait()


def forward_kernel(per, nz, modes, fast, far_shift, far_remainder, circle, twiddle, short, steps, *rest):
    rad_count = lax.axis_size("rad")
    hops, (out, sides, rows_out, shift, remainder, scalar_sems) = rest[:fast], rest[fast:]
    scalars = [
        pltpu.make_async_copy(far, near, scalar_sems.at[i])
        for i, (far, near) in enumerate(((far_shift, shift), (far_remainder, remainder)))
    ]
    for copy in scalars:
        copy.start()
    me = lax.axis_index("azi")
    azi = lax.axis_index("azi")
    for o_fast, hop in enumerate(hops):
        for o_slow in range(hop.shape[0]):
            from_slow = came_from(azi // fast, o_slow, hop.shape[0], True)
            from_fast = came_from(azi % fast, o_fast, fast, False)
            sides[from_slow * fast + from_fast] = hop[o_slow]
    sources = sides.shape[0]
    nq = circle.shape[0]
    tiles = nq // sources
    length = nq * LANES
    upper = modes // nq
    lane = lane_iota((sources, LANES))
    q_id, a_id = row_iota((nq, 2 * sources)), lane_iota((nq, 2 * sources))
    after = lax.rem((a_id + 1) * tiles, nq)
    before = lax.rem((a_id - sources) * tiles + nq - 1, nq)
    target = (q_id == jnp.where(a_id < sources, after, before)).astype(F32)
    dot = functools.partial(jnp.dot, precision=EXACT, preferred_element_type=F32)
    spilled = []
    for k in range(per):
        packed = sides[:, per * tiles + k, :]
        extra = jnp.zeros((sources, LANES), F32)
        for z in range(nz):
            extra = extra + pltpu.roll(packed, LANES - 2 - 4 * z, 1)
        halves = (jnp.where(lane < 2, extra, 0.0), jnp.where(lane >= LANES - 2, extra, 0.0))
        spilled.append(jnp.concatenate(halves, axis=0))
    spilled = dot(target, jnp.concatenate(spilled, axis=1))
    grids = []
    for k in range(per):
        grid = sides[:, k * tiles : (k + 1) * tiles, :].reshape(nq, LANES)
        grids.append((grid + spilled[:, k * LANES : (k + 1) * LANES]).T)
    inner = dot(jnp.concatenate(grids, axis=0), circle[...])
    turn_cos, turn_sin = twiddle[:, :nq], twiddle[:, nq:]
    turned = []
    for k in range(per):
        cos_part = inner[k * LANES : (k + 1) * LANES, :nq]
        sin_part = inner[k * LANES : (k + 1) * LANES, nq:]
        turned.append(cos_part * turn_cos - sin_part * turn_sin)
        turned.append(-(sin_part * turn_cos + cos_part * turn_sin))
    outer = dot(short[...], jnp.concatenate(turned, axis=1))
    for copy in scalars:
        copy.wait()
    mode = row_iota((upper, nq)) * nq + lane_iota((upper, nq))
    cos_one, sin_one = steps[0:upper, :nq], steps[0:upper, nq:]
    cos_two, sin_two = steps[upper:, :nq], steps[upper:, nq:]
    for k in range(per):
        at = 2 * k * nq
        real = outer[:upper, at : at + nq] + outer[upper:, at + nq : at + 2 * nq]
        imag = outer[:upper, at + nq : at + 2 * nq] - outer[upper:, at : at + nq]
        x = jnp.full((upper, nq), -remainder[me * per + k], F32)
        w_next = x * (x + 1.0) * (x + 2.0) / 6.0
        w_here = -(x - 1.0) * (x + 1.0) * (x + 2.0) / 2.0
        w_prev = (x - 1.0) * x * (x + 2.0) / 2.0
        w_prev_two = -(x - 1.0) * x * (x + 1.0) / 6.0
        tap_cos = w_here + (w_next + w_prev) * cos_one + w_prev_two * cos_two
        tap_sin = (w_prev - w_next) * sin_one + w_prev_two * sin_two
        phase = lax.rem(mode * shift[me * per + k], length)
        phase = jnp.where(phase > length // 2, phase - length, phase)
        angle = phase.astype(F32) * (2.0 * math.pi / length)
        spin_cos, spin_sin = jnp.cos(angle), jnp.sin(angle)
        gain_cos = tap_cos * spin_cos - tap_sin * spin_sin
        gain_sin = tap_sin * spin_cos + tap_cos * spin_sin
        rows_out[:, k, :] = real * gain_cos + imag * gain_sin
        rows_out[:, per + k, :] = imag * gain_cos - real * gain_sin
    share = rad_count * sources // upper
    for rad in range(rad_count):
        for a in range(sources):
            at = (a * rad_count + rad) * 2 * per
            value = rows_out[(rad * sources + a) // share]
            out[at : at + 2 * per, :] = value.astype(BF16).astype(F32)


def pick(values, index):
    chosen = values[0]
    for i, value in enumerate(values[1:]):
        chosen = jnp.where(index == i + 1, value, chosen)
    return chosen


def route_kernel(size, middle, inner, where, ring, *rest):
    count = (len(rest) - 1 - size)
    sources, outs, sorted_rows = rest[:count], rest[count:-1], rest[-1]
    for i, source in enumerate(sources):
        value = source[...]
        for m in range(middle):
            for dest in range(size):
                at = (m * size + dest) * inner
                to = (i * middle + m) * inner
                sorted_rows[dest, to : to + inner, :] = value[at : at + inner, :]
    choices = [sorted_rows[dest] for dest in range(size)]
    index = where()
    for offset, out in enumerate(outs):
        out[...] = pick(choices, sent_to(index, offset, size, ring))


def halve_kernel(inner, *rest):
    rad_count = lax.axis_size("rad")
    outs, sorted_rows = rest[-1 - rad_count : -1], rest[-1]
    to = 0
    for source in rest[: -1 - rad_count]:
        value = source[...]
        for m in range(value.shape[0] // (rad_count * inner)):
            for rad in range(rad_count):
                at = (m * rad_count + rad) * inner
                sorted_rows[rad, to : to + inner, :] = value[at : at + inner, :]
            to += inner
    choices = [sorted_rows[rad] for rad in range(rad_count)]
    for offset, out in enumerate(outs):
        out[...] = pick(choices, sent_to(lax.axis_index("rad"), offset, rad_count, False))


def arrival_source(slow, fast, axis_iota):
    rad_count = lax.axis_size("rad")
    azi, rad = lax.axis_index("azi"), lax.axis_index("rad")
    from_rad = came_from(rad, axis_iota % rad_count, rad_count, False)
    from_fast = came_from(azi % fast, axis_iota // rad_count % fast, fast, False)
    from_slow = came_from(azi // fast, axis_iota // (rad_count * fast) % slow, slow, True)
    return (from_rad * slow + from_slow) * fast + from_fast


def couple_kernel(per, local, fast, slow, kernel, mixed, *rest):
    rad_count = lax.axis_size("rad")
    columns, outs, (tables, factor) = rest[:rad_count], rest[rad_count:-2], rest[-2:]
    sources = slow * fast * rad_count
    nq = columns[0].shape[1]
    total = sources * per
    me = lax.axis_index("rad") * lax.axis_size("azi") + lax.axis_index("azi")
    offset = lax.rem(me * local, nq)
    row, col = row_iota((total, total)), lane_iota((total, total))
    place = col % sources
    azi_count = slow * fast
    place = place % azi_count * rad_count + place // azi_count
    source = arrival_source(slow, fast, place)
    spread = (row == source * per + col // sources).astype(F32)
    lane = lane_iota((total, nq))
    sides = []
    for c in range(2):
        stacked = jnp.concatenate(
            [
                ref[pl.ds(c * per + k, slow * fast, stride=2 * per), :]
                for k in range(per)
                for ref in columns
            ],
            axis=0,
        )
        ordered = jnp.dot(spread, stacked, preferred_element_type=F32)
        sides.append(pltpu.roll(ordered, lax.rem(nq - offset + c * local, nq), 1))
    weights = jnp.where(lane < local, sides[0], sides[1]).astype(BF16)
    result = jnp.zeros((total, nq), F32)
    for m in range(local):
        product = jnp.dot(kernel[m], weights, preferred_element_type=F32)
        result = jnp.where((lane == m) | (lane == local + m), product, result)
    rad = lax.axis_index("rad")
    share = total // len(outs)
    slabs = [result[i * share : (i + 1) * share, :] for i in range(len(outs))]
    for offset, out in enumerate(outs):
        out[...] = pick(slabs, sent_to(rad, offset, len(outs), False))
    share = nq // local
    source = arrival_source(slow, fast, row_iota((sources, sources)))
    order = (source == lane_iota((sources, sources))).astype(F32)
    ordered = jnp.dot(order, mixed[...], precision=EXACT, preferred_element_type=F32)
    own = arrival_source(slow, fast, row_iota(ordered.shape)) % share
    tables[...] = jnp.concatenate([jnp.where(own == h, ordered, 0.0) for h in range(share)], axis=1)
    source = arrival_source(slow, fast, row_iota((sources, nq)))
    constant = (source == 0) & (lane_iota((sources, nq)) % local == 0)
    factor[...] = jnp.where(constant, 1.0, 2.0) / (nq * LANES)


def three_pass_dot(left, right):
    dot = functools.partial(jnp.dot, preferred_element_type=F32)
    left_high, right_high = left.astype(BF16), right.astype(BF16)
    left_low = (left - left_high.astype(F32)).astype(BF16)
    right_low = (right - right_high.astype(F32)).astype(BF16)
    return dot(left_high, right_high) + (dot(left_low, right_high) + dot(left_high, right_low))


def settle_kernel(per, bulk, top, rho, ur, up, near, sems):
    nz = rho.shape[0]
    sources, _, seg = bulk.shape
    group = nz * per
    unit = jnp.concatenate([top[0:1, :] * (GAIN / TOP)] * (seg // LANES), axis=1)
    half = sources // 2 * per
    copies = [
        pltpu.make_async_copy(
            near.at[c, :, pl.ds(i * half, half), :], far.at[:, pl.ds(i * half, half), :], sems.at[2 * c + i]
        )
        for c, far in enumerate((rho, ur, up))
        for i in range(2)
    ]
    for c in range(3):
        for a in range(sources):
            value = decode(bulk[a, c * group : (c + 1) * group, :].astype(F32), unit)
            for z in range(nz):
                near[c, z, a * per : (a + 1) * per, :] = value[z * per : (z + 1) * per, :]
            if (a + 1) * per % half == 0:
                copies[2 * c + a * per // half].start()
    for copy in copies:
        copy.wait()


def inverse_kernel(per, local, circle, twiddle, tables, factor, *rest):
    blocks, out = rest[:-1], rest[-1]
    slow = len(blocks)
    nq = circle.shape[0]
    share = nq // local
    count = tables.shape[0]
    picked = []
    for k in range(per):
        rows = [
            ref[pl.ds(k, count // slow, stride=per), :] if per > 1 else ref[...] for ref in blocks
        ]
        picked.append(jnp.concatenate(rows, axis=0) * factor[...])
    mid = three_pass_dot(jnp.concatenate(picked, axis=1).T, tables[...])
    turn_cos, turn_sin = twiddle[:, :LANES], twiddle[:, LANES:]
    turned = []
    for k in range(per):
        real, imag = [], []
        for h in range(share):
            at = 2 * LANES * h
            upper = mid[k * nq : k * nq + local, at : at + 2 * LANES]
            lower = mid[k * nq + local : k * nq + 2 * local, at : at + 2 * LANES]
            real.append(upper[:, :LANES] - lower[:, LANES:])
            imag.append(upper[:, LANES:] + lower[:, :LANES])
        real = jnp.concatenate(real, axis=0)
        imag = jnp.concatenate(imag, axis=0)
        pair = [real * turn_cos - imag * turn_sin, -(real * turn_sin + imag * turn_cos)]
        turned.append(jnp.concatenate(pair, axis=0))
    wave = three_pass_dot(circle[...], jnp.concatenate(turned, axis=1))
    for k in range(per):
        for q in range(nq):
            out[k : k + 1, q * LANES : (q + 1) * LANES] = wave[
                q : q + 1, k * LANES : (k + 1) * LANES
            ]


def cos_sin(rows, columns, length):
    steps = np.outer(rows, columns) % length
    angle = 2.0 * np.pi * steps / length
    return np.cos(angle).astype(np.float32), np.sin(angle).astype(np.float32)


def call(body, out_shape, in_specs=None, out_specs=None, scratch=(), name=None, aliases=None, room=40 * 2**20, **cost):
    kernel = pl.pallas_call(
        body,
        out_shape=out_shape,
        **({} if in_specs is None else {"in_specs": in_specs}),
        **({} if out_specs is None else {"out_specs": out_specs}),
        scratch_shapes=list(scratch),
        input_output_aliases=aliases or {},
        compiler_params=pltpu.CompilerParams(vmem_limit_bytes=VMEM_BYTES - room),
        cost_estimate=pl.CostEstimate(**{"flops": 0, "bytes_accessed": 0, "transcendentals": 0, **cost}),
    )

    def run(*operands):
        places = [
            None if x.ndim == 1 else pltpu.HBM if name == "load" else pltpu.VMEM
            for x in operands
        ]
        near = [
            x if place is None else pltpu.with_memory_space_constraint(x, place)
            for x, place in zip(operands, places)
        ]
        return kernel(*near)

    return run


def exchange(array, axes):
    return lax.all_to_all(array, axes, 0, 0, tiled=True)


def shape_of(shape, dtype=F32):
    return jax.ShapeDtypeStruct(shape, dtype)


def body(density, radial_velocity, azimuthal_velocity, cycle_shift, remainder, kernel):
    nz, slab, seg = density.shape
    azi, rad = lax.axis_size("azi"), lax.axis_size("rad")
    devices = azi * rad
    per = slab // azi
    tiles = seg // LANES
    length = seg * azi
    nq = length // LANES
    local = kernel.shape[0]
    modes = local * devices
    upper = modes // nq
    width = seg + LANES
    group = nz * per
    stride = -(-3 * group // SUB) * SUB
    rows = tiles * stride
    side = side_rows(per, tiles)
    fast = min(4, azi)
    slow = azi // fast
    vmem, smem = pl.BlockSpec(memory_space=pltpu.VMEM), pl.BlockSpec(memory_space=pltpu.SMEM)

    fields = (density, radial_velocity, azimuthal_velocity)
    anywhere = pl.BlockSpec(memory_space=pl.ANY)
    far = pl.BlockSpec(memory_space=pltpu.HBM)
    edge = pltpu.VMEM((3, nz, 2, seg), F32)
    padded = pltpu.VMEM((3, nz, slab + SUB, width), F32)
    field, tail, head = call(
        load_kernel,
        (padded, edge, edge),
        in_specs=[far] * 3,
        scratch=(pltpu.SemaphoreType.DMA((3,)),),
        name="load",
        bytes_accessed=12 * nz * slab * seg,
    )(*fields)
    low = lax.ppermute(tail, "rad", [(i, (i + 1) % rad) for i in range(rad)])
    high = lax.ppermute(head, "rad", [((i + 1) % rad, i) for i in range(rad)])
    stage = call(interior_kernel, padded, name="interior", bytes_accessed=12 * nz * slab * seg)(field)
    bulk, surf, *_ = call(
        functools.partial(hydro_kernel, per, seg),
        (pltpu.HBM((azi, rows, LANES), BF16), pltpu.VMEM((azi, side, LANES), F32), padded, padded),
        out_specs=(far, vmem, vmem, vmem),
        aliases={0: 2, 1: 3},
        scratch=(
            pltpu.VMEM((azi, rows, LANES), F32),
            pltpu.VMEM((azi, rows, LANES), BF16),
            pltpu.SemaphoreType.DMA((slab // SUB,)),
        ),
        name="hydro",
        flops=100 * 3 * nz * slab * seg,
        bytes_accessed=24 * nz * slab * seg,
    )(field, stage, low, high)

    def hop(buffers, axis, size, step, ring=False):
        around = range(lax.axis_size(axis))
        return [buffers[0]] + [
            lax.ppermute(buffers[o], axis, [
                (i, i + (sent_to(i // step % size, o, size, ring) - i // step % size) * step)
                for i in around
            ])
            for o in range(1, size)
        ]

    def route(buffers, size, inner, step, name, ring=False):
        count = buffers[0].shape[0]
        lines = len(buffers) * count // size
        where = lambda: lax.axis_index("azi") // step % size
        buffers = call(
            functools.partial(route_kernel, size, count // (size * inner), inner, where, ring),
            tuple(pltpu.VMEM((lines, LANES), F32) for _ in range(size)),
            scratch=(pltpu.VMEM((size, lines, LANES), F32),),
            name="route_" + name,
            bytes_accessed=100_000,
        )(*buffers)
        return hop(buffers, "azi", size, step, ring)

    surf = [surf.reshape(azi * side, LANES)]
    surf = route(surf, slow, fast * side, fast, "surf_slow", ring=True)
    bulk = exchange(bulk, "azi")
    surf = route(surf, fast, side, 1, "surf_fast")
    surf = [x.reshape(slow, side, LANES) for x in surf]

    k_id, l_id = np.arange(nq), np.arange(LANES)
    circle = np.concatenate(cos_sin(k_id, k_id, nq), axis=1)
    twiddle = np.concatenate(cos_sin(l_id, k_id, length), axis=1)
    short = np.concatenate(cos_sin(np.arange(upper), l_id, LANES), axis=0)
    m_id = np.arange(modes)
    steps = [np.concatenate([t.reshape(upper, nq) for t in cos_sin(m_id, [n], length)], 1) for n in (1, 2)]
    steps = np.concatenate(steps, axis=0)
    spectrum, sides = call(
        functools.partial(forward_kernel, per, nz, modes, fast),
        (
            pltpu.VMEM((devices * 2 * per, nq), F32),
            pltpu.VMEM((azi, side, LANES), F32),
        ),
        in_specs=[anywhere] * 2 + [vmem] * (4 + fast),
        scratch=(
            pltpu.VMEM((upper, 2 * per, nq), F32),
            pltpu.SMEM((slab,), jnp.int32),
            pltpu.SMEM((slab,), F32),
            pltpu.SemaphoreType.DMA((2,)),
        ),
        name="forward",
        flops=100_000_000,
        bytes_accessed=1_000_000,
    )(cycle_shift, remainder, jnp.asarray(circle), jnp.asarray(twiddle), jnp.asarray(short), jnp.asarray(steps), *surf)
    columns = route([spectrum], fast, rad * 2 * per, 1, "column_fast")
    columns = route(columns, slow, rad * 2 * per, fast, "column_slow", ring=True)
    columns = call(
        functools.partial(halve_kernel, 2 * per),
        tuple(pltpu.VMEM((azi * 2 * per, nq), F32) for _ in range(rad)),
        scratch=(pltpu.VMEM((rad, azi * 2 * per, nq), F32),),
        name="route_column_rad",
        bytes_accessed=100_000,
    )(*columns)
    columns = hop(columns, "rad", rad, 1)
    j_of_block = np.arange(devices) * local // nq
    mixed = np.concatenate(cos_sin(j_of_block, l_id, LANES), axis=1)
    *blocks, tables, factor = call(
        functools.partial(couple_kernel, per, local, fast, slow),
        (
            *(pltpu.VMEM((azi * per, nq), F32) for _ in range(rad)),
            pltpu.VMEM((devices, nq // local * 2 * LANES), F32),
            pltpu.VMEM((devices, nq), F32),
        ),
        name="couple",
        flops=100_000_000,
        bytes_accessed=1_000_000,
    )(kernel, jnp.asarray(mixed), *columns)
    blocks = hop(blocks, "rad", rad, 1)
    blocks = route(blocks, fast, per, 1, "block_fast")
    blocks = route(blocks, slow, per, fast, "block_slow", ring=True)

    moved, top = call(
        functools.partial(advect_kernel, per, nz),
        (pltpu.HBM((azi, 3 * group, seg), BF16), pltpu.VMEM((SUB, LANES), F32)),
        in_specs=[anywhere, anywhere, vmem, vmem],
        out_specs=(far, vmem),
        scratch=(
            pltpu.VMEM((3, nq, group, LANES), F32),
            pltpu.VMEM((3, nq, group, LANES), F32),
            pltpu.VMEM((3, azi, group, LANES), F32),
            pltpu.VMEM((azi, 3 * group, seg), BF16),
            pltpu.SMEM((slab,), jnp.int32),
            pltpu.SMEM((slab,), F32),
            pltpu.SemaphoreType.DMA((2,)),
            pltpu.SemaphoreType.DMA((azi,)),
        ),
        name="advect",
        flops=50 * 3 * nz * slab * seg,
        bytes_accessed=12 * nz * slab * seg,
    )(cycle_shift, remainder, bulk, sides)
    moved = exchange(moved, "azi")
    turn = np.concatenate(cos_sin(k_id, l_id, length), axis=1)
    potential = call(
        functools.partial(inverse_kernel, per, local),
        shape_of((per, length)),
        name="inverse",
        flops=100_000_000,
        bytes_accessed=1_000_000,
    )(jnp.asarray(circle), jnp.asarray(turn), tables, factor, *blocks)
    results = call(
        functools.partial(settle_kernel, per),
        tuple(pltpu.HBM((nz, slab, seg), F32) for _ in range(3)),
        out_specs=(far,) * 3,
        scratch=(pltpu.VMEM((3, nz, slab, seg), F32), pltpu.SemaphoreType.DMA((6,))),
        name="settle",
        flops=20 * 3 * nz * slab * seg,
        bytes_accessed=18 * nz * slab * seg,
    )(moved, top)
    return (*results, potential)


def solution(mesh):
    split = P(None, "rad", "azi")
    in_specs = (split, split, split, P("rad"), P("rad"), P(("rad", "azi"), None, None))
    out_specs = (split, split, split, P(("rad", "azi"), None))

    return jax.shard_map(body, mesh=mesh, in_specs=in_specs, out_specs=out_specs, check_vma=False)
```

```python
import functools
import math

import jax
import jax.numpy as jnp
import numpy as np
from jax import lax
from jax.experimental import pallas as pl
from jax.experimental.pallas import tpu as pltpu
from jax.sharding import PartitionSpec as P


RADIAL_COURANT = 0.3
VISCOSITY = 0.08
LANES = 128
VMEM_BYTES = 67_043_328
SUB = 8
EXACT = lax.Precision.HIGHEST
F32 = jnp.float32
BF16 = jnp.bfloat16

POWER = 13
TOP = 2.0**9.69
GAIN = 1.25


def encode(value, scale):
    scaled = value * scale
    second = scaled * scaled
    fourth = second * second
    return (fourth * fourth) * (fourth * scaled)


def decode(code, scale):
    root = lax.exp2(lax.log(jnp.abs(code)) * (1.0 / (POWER * math.log(2.0)))) * scale
    return jnp.where(code < 0.0, -root, root)


def sent_to(place, offset, size, ring):
    return (place + offset) % size if ring else place ^ offset


def came_from(place, offset, size, ring):
    return (place - offset + size) % size if ring else place ^ offset


def row_iota(shape):
    return lax.broadcasted_iota(jnp.int32, shape, 0)


def lane_iota(shape):
    return lax.broadcasted_iota(jnp.int32, shape, 1)


def side_rows(per, tiles):
    return -(-(per * tiles + per) // SUB) * SUB


def load_kernel(rho, ur, up, field, tail, head, sems):
    nz, slab, seg = rho.shape
    lines, width = field.shape[2:]
    copies = [
        pltpu.make_async_copy(far, field.at[c, :, pl.ds(0, slab), pl.ds(0, seg)], sems.at[c])
        for c, far in enumerate((rho, ur, up))
    ]
    for copy in copies:
        copy.start()
    for c in range(3):
        for z in range(nz):
            field[c, z, :, seg:width] = jnp.zeros((lines, width - seg), F32)
    for c in range(3):
        copies[c].wait()
        tail[c] = field[c, :, slab - 2 : slab, 0:seg]
        head[c] = field[c, :, 0:2, 0:seg]


def advance(ref, tile, z, slab, scale):
    _, nz, lines, width = ref.shape
    count = lines // SUB
    sub = row_iota((SUB, width))
    near_rows = row_iota((SUB, LANES))
    cycle = tile * SUB + near_rows
    cycle = jnp.where((tile == count - 1) & (near_rows >= SUB // 2), near_rows - SUB, cycle)
    cycle = lax.axis_index("rad") * slab + cycle
    radius = 1.0 + 4.0 * (cycle.astype(F32) + 0.5) / (slab * lax.axis_size("rad"))
    power = 1.0 / (radius * jnp.sqrt(radius))
    wide = lambda x: jnp.concatenate([x] * (width // LANES), axis=1)
    courant = wide((0.5 * scale) * (0.3 / radius))
    coriolis, epicycle = wide((0.2 * scale) * power), wide((0.05 * scale) * power)
    rows = lambda t: pl.ds(pl.multiple_of(t * SUB, SUB), SUB)
    here, before, after = rows(tile), rows(lax.rem(tile + count - 1, count)), rows(lax.rem(tile + 1, count))
    z_up, z_down = min(z + 1, nz - 1), max(z - 1, 0)
    center, base, rad_diff, azi_diff = [], [], [], []
    for c in range(3):
        cur = ref[c, z, here, :]
        inward = pltpu.roll(jnp.where(sub == SUB - 1, ref[c, z, before, :], cur), 1, 0)
        outward = pltpu.roll(jnp.where(sub == 0, ref[c, z, after, :], cur), SUB - 1, 0)
        ahead = pltpu.roll(cur, width - 1, 1)
        behind = pltpu.roll(cur, 1, 1)
        near = ref[c, z_up, here, :] + ref[c, z_down, here, :] + inward + outward + ahead + behind
        base.append((scale * VISCOSITY) * near + (scale * (1.0 - 6.0 * VISCOSITY)) * cur)
        rad_diff.append(outward - inward)
        azi_diff.append(ahead - behind)
        center.append(cur)
    half = 0.5 * scale * RADIAL_COURANT
    return (
        base[0] - (half * rad_diff[1] + courant * azi_diff[2]),
        base[1] + coriolis * center[2] - half * rad_diff[0],
        base[2] - epicycle * center[1] - courant * azi_diff[0],
    )


def store_section(field, stage, slab, tile):
    for z in range(field.shape[1]):
        for c, value in enumerate(advance(field, tile, z, slab, 1.0)):
            stage[c, z, pl.ds(pl.multiple_of(tile * SUB, SUB), SUB), :] = value


def interior_kernel(field, stage):
    slab = field.shape[2] - SUB

    def section(tile, carry):
        store_section(field, stage, slab, tile)
        return carry

    lax.fori_loop(1, slab // SUB - 1, section, 0)


def hydro_kernel(
    per, seg, field_in, stage_in, low, high, bulk, surf, field, stage, block, narrow, sems
):
    _, nz, lines, width = field.shape
    slab = lines - SUB
    last = slab // SUB
    tiles = seg // LANES
    rad = lax.axis_index("rad")
    rad_count = lax.axis_size("rad")
    for c in range(3):
        for z in range(nz):
            inner = jnp.broadcast_to(field[c, z, 0:1, 0:seg], (2, seg))
            outer = jnp.broadcast_to(field[c, z, slab - 1 : slab, 0:seg], (2, seg))
            outward = jnp.where(rad == rad_count - 1, outer, high[c, z])
            inward = jnp.where(rad == 0, inner, low[c, z])
            between = jnp.zeros((SUB - 4, seg), F32)
            field[c, z, slab:lines, 0:seg] = jnp.concatenate([outward, between, inward], axis=0)

    def section(index, carry):
        store_section(field, stage, slab, lax.rem(index + last - 1, last + 1))
        return carry

    lax.fori_loop(0, 3, section, 0)

    @pl.when(rad == 0)
    def _():
        for c in range(3):
            for z in range(nz):
                stage[c, z, lines - 1 : lines, :] = stage[c, z, 0:1, :]

    @pl.when(rad == rad_count - 1)
    def _():
        for c in range(3):
            for z in range(nz):
                stage[c, z, slab : slab + 1, :] = stage[c, z, slab - 1 : slab, :]

    def second_section(tile, largest):
        here = pl.ds(pl.multiple_of(tile * SUB, SUB), SUB)
        for z in range(nz):
            for c, value in enumerate(advance(stage, tile, z, slab, 0.5)):
                value = 0.5 * field[c, z, here, :] + value
                field[c, z, here, :] = value
                largest = jnp.maximum(largest, jnp.abs(value))
        return largest

    largest = lax.fori_loop(0, last, second_section, jnp.zeros((SUB, width), F32))
    peak = jnp.maximum(jnp.max(largest, keepdims=True), 1e-30)
    scale = TOP / peak
    dests = SUB // per
    stride = -(-3 * nz * per // SUB) * SUB

    def send(index):
        at = pl.ds(index * dests, dests)
        return pltpu.make_async_copy(narrow.at[at], bulk.at[at], sems.at[index])

    def pack(tile, carry):
        here = pl.ds(pl.multiple_of(tile * SUB, SUB), SUB)
        overflow = jnp.zeros((SUB, LANES), F32)
        column = jnp.zeros((SUB, seg), F32)
        for c in range(3):
            for z in range(nz):
                value = field[c, z, here, 0:seg]
                if c == 0:
                    column = column + value
                code = encode(value, scale)
                plane = c * nz + z
                for d in range(dests):
                    for b in range(tiles):
                        line = b * stride + plane * per
                        block[tile * dests + d, line : line + per, :] = code[
                            d * per : (d + 1) * per, b * LANES : (b + 1) * LANES
                        ]
                overflow = overflow + pltpu.roll(field[c, z, here, seg:width], 2 + 4 * plane, 1)
        overflow = jnp.where(lane_iota((SUB, LANES)) < LANES // 2, overflow, peak)
        for d in range(dests):
            dest = tile * dests + d
            for k in range(per):
                row = d * per + k
                for b in range(tiles):
                    surf[dest, k * tiles + b : k * tiles + b + 1, :] = column[
                        row : row + 1, b * LANES : (b + 1) * LANES
                    ]
                line = per * tiles + k
                surf[dest, line : line + 1, :] = overflow[row : row + 1, :]
        for d in range(dests):
            dest = tile * dests + d
            narrow[dest] = block[dest].astype(BF16)
        send(tile).start()
        return carry

    lax.fori_loop(0, last, pack, 0)
    for index in range(last):
        send(index).wait()


def advect_kernel(
    per, nz, far_shift, far_remainder, bulk, sides, out, top,
    ring, tapped, over, codes, shift, remainder, scalar_sems, sems,
):
    scalars = [
        pltpu.make_async_copy(far, near, scalar_sems.at[i])
        for i, (far, near) in enumerate(((far_shift, shift), (far_remainder, remainder)))
    ]
    for copy in scalars:
        copy.start()
    sources = bulk.shape[0]
    count = ring.shape[1]
    tiles = count // sources
    group = nz * per
    stride = -(-3 * group // SUB) * SUB
    me = lax.axis_index("azi")

    def widen(a, peak):
        whole_block = bulk[a].astype(F32)
        packed = sides[a, per * tiles : per * tiles + per, :]
        mine = jnp.where(lane_iota((1, LANES)) >= LANES // 2, packed[0:1, :], 0.0)
        mine = jnp.max(mine, keepdims=True)
        unit = mine * (1.0 / TOP)
        for b in range(tiles):
            value = decode(whole_block[b * stride : (b + 1) * stride, :], unit)
            for c in range(3):
                ring[c, a * tiles + b] = value[c * group : (c + 1) * group, :]
        for c in range(3):
            for z in range(nz):
                turned = pltpu.roll(packed, LANES - 2 - 4 * (c * nz + z), 1)
                over[c, a, z * per : (z + 1) * per, :] = turned
        return jnp.maximum(peak, mine)

    peak = lax.fori_loop(0, sources, widen, jnp.zeros((1, 1), F32), unroll=8)
    top[...] = jnp.broadcast_to(peak, top.shape)
    lane = lane_iota((group, LANES))
    cycle = row_iota((group, LANES)) % per

    def spill(a, carry):
        after = lax.rem((a + 1) * tiles, count)
        before = lax.rem(a * tiles + count - 1, count)
        for c in range(3):
            extra = over[c, a]
            ring[c, after] = ring[c, after] + jnp.where(lane < 2, extra, 0.0)
            ring[c, before] = ring[c, before] + jnp.where(lane >= LANES - 2, extra, 0.0)
        return carry

    lax.fori_loop(0, sources, spill, 0, unroll=16)
    for copy in scalars:
        copy.wait()
    x = jnp.zeros((group, LANES), F32)
    whole, part = [], []
    for k in range(per):
        x = jnp.where(cycle == k, -remainder[me * per + k], x)
        amount = shift[me * per + k]
        whole.append(amount // LANES)
        part.append(lax.rem(amount, LANES))
    w_next = x * (x + 1.0) * (x + 2.0) / 6.0
    w_here = -(x - 1.0) * (x + 1.0) * (x + 2.0) / 2.0
    w_prev = (x - 1.0) * x * (x + 2.0) / 2.0
    w_prev_two = -(x - 1.0) * x * (x + 1.0) / 6.0

    def tap(a, carry):
        before = lax.rem(a * tiles + count - 1, count)
        after = lax.rem((a + 1) * tiles, count)
        for c in range(3):
            line = [ring[c, before]]
            line += [ring[c, a * tiles + b] for b in range(tiles)]
            line += [ring[c, after]]
            for b in range(tiles):
                prv, cur, nxt = line[b : b + 3]
                next_one = pltpu.roll(jnp.where(lane == 0, nxt, cur), LANES - 1, 1)
                prev_one = pltpu.roll(jnp.where(lane == LANES - 1, prv, cur), 1, 1)
                prev_two = pltpu.roll(jnp.where(lane >= LANES - 2, prv, cur), 2, 1)
                tapped[c, a * tiles + b] = (
                    w_next * next_one + w_here * cur + w_prev * prev_one + w_prev_two * prev_two
                )
        return carry

    lax.fori_loop(0, sources, tap, 0, unroll=8)
    scale = (TOP / GAIN) / peak

    def send(dest):
        return pltpu.make_async_copy(codes.at[dest], out.at[dest], sems.at[dest])

    def turned_tile(c, k, t):
        source = lax.rem(t - whole[k] + 2 * count, count)
        return pltpu.roll(tapped[c, source], part[k], 1)

    def turn(dest, carry):
        carry = list(carry)
        pieces = [[None] * tiles for _ in range(3)]
        for b in range(tiles):
            t = dest * tiles + b
            for c in range(3):
                joined = jnp.zeros((group, LANES), F32)
                for k in range(per):
                    now = turned_tile(c, k, t)
                    value = jnp.where(lane < part[k], carry[c * per + k], now)
                    joined = value if per == 1 else jnp.where(cycle == k, value, joined)
                    carry[c * per + k] = now
                pieces[c][b] = encode(joined, scale)
        columns = [jnp.concatenate([pieces[c][b] for b in range(tiles)], axis=1) for c in range(3)]
        codes[dest] = jnp.concatenate(columns, axis=0).astype(BF16)
        send(dest).start()
        return tuple(carry)

    start = tuple(turned_tile(c, k, -1) for c in range(3) for k in range(per))
    lax.fori_loop(0, sources, turn, start, unroll=8)
    for dest in range(sources):
        send(dest).wait()


def forward_kernel(per, nz, modes, fast, far_shift, far_remainder, circle, twiddle, short, steps, *rest):
    rad_count = lax.axis_size("rad")
    hops, (out, sides, rows_out, shift, remainder, scalar_sems) = rest[:fast], rest[fast:]
    scalars = [
        pltpu.make_async_copy(far, near, scalar_sems.at[i])
        for i, (far, near) in enumerate(((far_shift, shift), (far_remainder, remainder)))
    ]
    for copy in scalars:
        copy.start()
    me = lax.axis_index("azi")
    azi = lax.axis_index("azi")
    slow = sides.shape[0] // fast
    used = hops[0].shape[0] // slow
    for o_fast, hop in enumerate(hops):
        for o_slow in range(slow):
            from_slow = came_from(azi // fast, o_slow, slow, True)
            from_fast = came_from(azi % fast, o_fast, fast, False)
            sides[from_slow * fast + from_fast, 0:used, :] = hop[o_slow * used : (o_slow + 1) * used, :]
    sources = sides.shape[0]
    nq = circle.shape[0]
    tiles = nq // sources
    length = nq * LANES
    upper = modes // nq
    lane = lane_iota((sources, LANES))
    q_id, a_id = row_iota((nq, 2 * sources)), lane_iota((nq, 2 * sources))
    after = lax.rem((a_id + 1) * tiles, nq)
    before = lax.rem((a_id - sources) * tiles + nq - 1, nq)
    target = (q_id == jnp.where(a_id < sources, after, before)).astype(F32)
    dot = functools.partial(jnp.dot, precision=EXACT, preferred_element_type=F32)
    spilled = []
    for k in range(per):
        packed = sides[:, per * tiles + k, :]
        extra = jnp.zeros((sources, LANES), F32)
        for z in range(nz):
            extra = extra + pltpu.roll(packed, LANES - 2 - 4 * z, 1)
        halves = (jnp.where(lane < 2, extra, 0.0), jnp.where(lane >= LANES - 2, extra, 0.0))
        spilled.append(jnp.concatenate(halves, axis=0))
    spilled = dot(target, jnp.concatenate(spilled, axis=1))
    grids = []
    for k in range(per):
        grid = sides[:, k * tiles : (k + 1) * tiles, :].reshape(nq, LANES)
        grids.append((grid + spilled[:, k * LANES : (k + 1) * LANES]).T)
    inner = dot(jnp.concatenate(grids, axis=0), circle[...])
    turn_cos, turn_sin = twiddle[:, :nq], twiddle[:, nq:]
    turned = []
    for k in range(per):
        cos_part = inner[k * LANES : (k + 1) * LANES, :nq]
        sin_part = inner[k * LANES : (k + 1) * LANES, nq:]
        turned.append(cos_part * turn_cos - sin_part * turn_sin)
        turned.append(-(sin_part * turn_cos + cos_part * turn_sin))
    outer = dot(short[...], jnp.concatenate(turned, axis=1))
    for copy in scalars:
        copy.wait()
    mode = row_iota((upper, nq)) * nq + lane_iota((upper, nq))
    cos_one, sin_one = steps[0:upper, :nq], steps[0:upper, nq:]
    cos_two, sin_two = steps[upper:, :nq], steps[upper:, nq:]
    for k in range(per):
        at = 2 * k * nq
        real = outer[:upper, at : at + nq] + outer[upper:, at + nq : at + 2 * nq]
        imag = outer[:upper, at + nq : at + 2 * nq] - outer[upper:, at : at + nq]
        x = jnp.full((upper, nq), -remainder[me * per + k], F32)
        w_next = x * (x + 1.0) * (x + 2.0) / 6.0
        w_here = -(x - 1.0) * (x + 1.0) * (x + 2.0) / 2.0
        w_prev = (x - 1.0) * x * (x + 2.0) / 2.0
        w_prev_two = -(x - 1.0) * x * (x + 1.0) / 6.0
        tap_cos = w_here + (w_next + w_prev) * cos_one + w_prev_two * cos_two
        tap_sin = (w_prev - w_next) * sin_one + w_prev_two * sin_two
        phase = lax.rem(mode * shift[me * per + k], length)
        phase = jnp.where(phase > length // 2, phase - length, phase)
        angle = phase.astype(F32) * (2.0 * math.pi / length)
        spin_cos, spin_sin = jnp.cos(angle), jnp.sin(angle)
        gain_cos = tap_cos * spin_cos - tap_sin * spin_sin
        gain_sin = tap_sin * spin_cos + tap_cos * spin_sin
        rows_out[:, k, :] = real * gain_cos + imag * gain_sin
        rows_out[:, per + k, :] = imag * gain_cos - real * gain_sin
    share = rad_count * sources // upper
    for rad in range(rad_count):
        for a in range(sources):
            at = (a * rad_count + rad) * 2 * per
            value = rows_out[(rad * sources + a) // share]
            out[at : at + 2 * per, :] = value.astype(BF16).astype(F32)


def pick(values, index):
    chosen = values[0]
    for i, value in enumerate(values[1:]):
        chosen = jnp.where(index == i + 1, value, chosen)
    return chosen


def route_kernel(size, middle, inner, where, ring, *rest):
    count = (len(rest) - 1 - size)
    sources, outs, sorted_rows = rest[:count], rest[count:-1], rest[-1]
    for i, source in enumerate(sources):
        value = source[...]
        for m in range(middle):
            for dest in range(size):
                at = (m * size + dest) * inner
                to = (i * middle + m) * inner
                sorted_rows[dest, to : to + inner, :] = value[at : at + inner, :]
    choices = [sorted_rows[dest] for dest in range(size)]
    index = where()
    for offset, out in enumerate(outs):
        out[...] = pick(choices, sent_to(index, offset, size, ring))


def trim_kernel(size, used, where, ring, surf, *rest):
    outs, sorted_rows = rest[:-1], rest[-1]
    inner = surf.shape[0] // size
    for dest in range(size):
        for i in range(inner):
            sorted_rows[dest, i * used : (i + 1) * used, :] = surf[dest * inner + i, 0:used, :]
    choices = [sorted_rows[dest] for dest in range(size)]
    index = where()
    for offset, out in enumerate(outs):
        out[...] = pick(choices, sent_to(index, offset, size, ring))


def halve_kernel(inner, *rest):
    rad_count = lax.axis_size("rad")
    outs, sorted_rows = rest[-1 - rad_count : -1], rest[-1]
    to = 0
    for source in rest[: -1 - rad_count]:
        value = source[...]
        for m in range(value.shape[0] // (rad_count * inner)):
            for rad in range(rad_count):
                at = (m * rad_count + rad) * inner
                sorted_rows[rad, to : to + inner, :] = value[at : at + inner, :]
            to += inner
    choices = [sorted_rows[rad] for rad in range(rad_count)]
    for offset, out in enumerate(outs):
        out[...] = pick(choices, sent_to(lax.axis_index("rad"), offset, rad_count, False))


def arrival_source(slow, fast, axis_iota):
    rad_count = lax.axis_size("rad")
    azi, rad = lax.axis_index("azi"), lax.axis_index("rad")
    from_rad = came_from(rad, axis_iota % rad_count, rad_count, False)
    from_fast = came_from(azi % fast, axis_iota // rad_count % fast, fast, False)
    from_slow = came_from(azi // fast, axis_iota // (rad_count * fast) % slow, slow, True)
    return (from_rad * slow + from_slow) * fast + from_fast


def couple_kernel(per, local, fast, slow, kernel, mixed, *rest):
    rad_count = lax.axis_size("rad")
    columns, outs, (tables, factor) = rest[:rad_count], rest[rad_count:-2], rest[-2:]
    sources = slow * fast * rad_count
    nq = columns[0].shape[1]
    total = sources * per
    me = lax.axis_index("rad") * lax.axis_size("azi") + lax.axis_index("azi")
    offset = lax.rem(me * local, nq)
    row, col = row_iota((total, total)), lane_iota((total, total))
    place = col % sources
    azi_count = slow * fast
    place = place % azi_count * rad_count + place // azi_count
    source = arrival_source(slow, fast, place)
    spread = (row == source * per + col // sources).astype(F32)
    lane = lane_iota((total, nq))
    sides = []
    for c in range(2):
        stacked = jnp.concatenate(
            [
                ref[pl.ds(c * per + k, slow * fast, stride=2 * per), :]
                for k in range(per)
                for ref in columns
            ],
            axis=0,
        )
        ordered = jnp.dot(spread, stacked, preferred_element_type=F32)
        sides.append(pltpu.roll(ordered, lax.rem(nq - offset + c * local, nq), 1))
    weights = jnp.where(lane < local, sides[0], sides[1]).astype(BF16)
    result = jnp.zeros((total, nq), F32)
    for m in range(local):
        product = jnp.dot(kernel[m], weights, preferred_element_type=F32)
        result = jnp.where((lane == m) | (lane == local + m), product, result)
    rad = lax.axis_index("rad")
    share = total // len(outs)
    slabs = [result[i * share : (i + 1) * share, :] for i in range(len(outs))]
    for offset, out in enumerate(outs):
        out[...] = pick(slabs, sent_to(rad, offset, len(outs), False))
    share = nq // local
    source = arrival_source(slow, fast, row_iota((sources, sources)))
    order = (source == lane_iota((sources, sources))).astype(F32)
    ordered = jnp.dot(order, mixed[...], precision=EXACT, preferred_element_type=F32)
    own = arrival_source(slow, fast, row_iota(ordered.shape)) % share
    tables[...] = jnp.concatenate([jnp.where(own == h, ordered, 0.0) for h in range(share)], axis=1)
    source = arrival_source(slow, fast, row_iota((sources, nq)))
    constant = (source == 0) & (lane_iota((sources, nq)) % local == 0)
    factor[...] = jnp.where(constant, 1.0, 2.0) / (nq * LANES)


def three_pass_dot(left, right):
    dot = functools.partial(jnp.dot, preferred_element_type=F32)
    left_high, right_high = left.astype(BF16), right.astype(BF16)
    left_low = (left - left_high.astype(F32)).astype(BF16)
    right_low = (right - right_high.astype(F32)).astype(BF16)
    return dot(left_high, right_high) + (dot(left_low, right_high) + dot(left_high, right_low))


def settle_kernel(per, bulk, top, rho, ur, up, near, sems):
    nz = rho.shape[0]
    sources, _, seg = bulk.shape
    group = nz * per
    unit = jnp.concatenate([top[0:1, :] * (GAIN / TOP)] * (seg // LANES), axis=1)
    half = sources // 2 * per
    copies = [
        pltpu.make_async_copy(
            near.at[c, :, pl.ds(i * half, half), :], far.at[:, pl.ds(i * half, half), :], sems.at[2 * c + i]
        )
        for c, far in enumerate((rho, ur, up))
        for i in range(2)
    ]
    for c in range(3):
        for a in range(sources):
            value = decode(bulk[a, c * group : (c + 1) * group, :].astype(F32), unit)
            for z in range(nz):
                near[c, z, a * per : (a + 1) * per, :] = value[z * per : (z + 1) * per, :]
            if (a + 1) * per % half == 0:
                copies[2 * c + a * per // half].start()
    for copy in copies:
        copy.wait()


def inverse_kernel(per, local, circle, twiddle, tables, factor, *rest):
    blocks, out = rest[:-1], rest[-1]
    slow = len(blocks)
    nq = circle.shape[0]
    share = nq // local
    count = tables.shape[0]
    picked = []
    for k in range(per):
        rows = [
            ref[pl.ds(k, count // slow, stride=per), :] if per > 1 else ref[...] for ref in blocks
        ]
        picked.append(jnp.concatenate(rows, axis=0) * factor[...])
    mid = three_pass_dot(jnp.concatenate(picked, axis=1).T, tables[...])
    turn_cos, turn_sin = twiddle[:, :LANES], twiddle[:, LANES:]
    turned = []
    for k in range(per):
        real, imag = [], []
        for h in range(share):
            at = 2 * LANES * h
            upper = mid[k * nq : k * nq + local, at : at + 2 * LANES]
            lower = mid[k * nq + local : k * nq + 2 * local, at : at + 2 * LANES]
            real.append(upper[:, :LANES] - lower[:, LANES:])
            imag.append(upper[:, LANES:] + lower[:, :LANES])
        real = jnp.concatenate(real, axis=0)
        imag = jnp.concatenate(imag, axis=0)
        pair = [real * turn_cos - imag * turn_sin, -(real * turn_sin + imag * turn_cos)]
        turned.append(jnp.concatenate(pair, axis=0))
    wave = three_pass_dot(circle[...], jnp.concatenate(turned, axis=1))
    for k in range(per):
        for q in range(nq):
            out[k : k + 1, q * LANES : (q + 1) * LANES] = wave[
                q : q + 1, k * LANES : (k + 1) * LANES
            ]


def cos_sin(rows, columns, length):
    steps = np.outer(rows, columns) % length
    angle = 2.0 * np.pi * steps / length
    return np.cos(angle).astype(np.float32), np.sin(angle).astype(np.float32)


def call(body, out_shape, in_specs=None, out_specs=None, scratch=(), name=None, aliases=None, room=40 * 2**20, **cost):
    kernel = pl.pallas_call(
        body,
        out_shape=out_shape,
        **({} if in_specs is None else {"in_specs": in_specs}),
        **({} if out_specs is None else {"out_specs": out_specs}),
        scratch_shapes=list(scratch),
        input_output_aliases=aliases or {},
        compiler_params=pltpu.CompilerParams(vmem_limit_bytes=VMEM_BYTES - room),
        cost_estimate=pl.CostEstimate(**{"flops": 0, "bytes_accessed": 0, "transcendentals": 0, **cost}),
    )

    def run(*operands):
        places = [
            None if x.ndim == 1 else pltpu.HBM if name == "load" else pltpu.VMEM
            for x in operands
        ]
        near = [
            x if place is None else pltpu.with_memory_space_constraint(x, place)
            for x, place in zip(operands, places)
        ]
        return kernel(*near)

    return run


def exchange(array, axes):
    return lax.all_to_all(array, axes, 0, 0, tiled=True)


def shape_of(shape, dtype=F32):
    return jax.ShapeDtypeStruct(shape, dtype)


def body(density, radial_velocity, azimuthal_velocity, cycle_shift, remainder, kernel):
    nz, slab, seg = density.shape
    azi, rad = lax.axis_size("azi"), lax.axis_size("rad")
    devices = azi * rad
    per = slab // azi
    tiles = seg // LANES
    length = seg * azi
    nq = length // LANES
    local = kernel.shape[0]
    modes = local * devices
    upper = modes // nq
    width = seg + LANES
    group = nz * per
    stride = -(-3 * group // SUB) * SUB
    rows = tiles * stride
    side = side_rows(per, tiles)
    fast = min(4, azi)
    slow = azi // fast
    vmem, smem = pl.BlockSpec(memory_space=pltpu.VMEM), pl.BlockSpec(memory_space=pltpu.SMEM)

    fields = (density, radial_velocity, azimuthal_velocity)
    anywhere = pl.BlockSpec(memory_space=pl.ANY)
    far = pl.BlockSpec(memory_space=pltpu.HBM)
    edge = pltpu.VMEM((3, nz, 2, seg), F32)
    padded = pltpu.VMEM((3, nz, slab + SUB, width), F32)
    field, tail, head = call(
        load_kernel,
        (padded, edge, edge),
        in_specs=[far] * 3,
        scratch=(pltpu.SemaphoreType.DMA((3,)),),
        name="load",
        bytes_accessed=12 * nz * slab * seg,
    )(*fields)
    low = lax.ppermute(tail, "rad", [(i, (i + 1) % rad) for i in range(rad)])
    high = lax.ppermute(head, "rad", [((i + 1) % rad, i) for i in range(rad)])
    stage = call(interior_kernel, padded, name="interior", bytes_accessed=12 * nz * slab * seg)(field)
    bulk, surf, *_ = call(
        functools.partial(hydro_kernel, per, seg),
        (pltpu.HBM((azi, rows, LANES), BF16), pltpu.VMEM((azi, side, LANES), F32), padded, padded),
        out_specs=(far, vmem, vmem, vmem),
        aliases={0: 2, 1: 3},
        scratch=(
            pltpu.VMEM((azi, rows, LANES), F32),
            pltpu.VMEM((azi, rows, LANES), BF16),
            pltpu.SemaphoreType.DMA((slab // SUB,)),
        ),
        name="hydro",
        flops=100 * 3 * nz * slab * seg,
        bytes_accessed=24 * nz * slab * seg,
    )(field, stage, low, high)

    def hop(buffers, axis, size, step, ring=False):
        around = range(lax.axis_size(axis))
        moved = [buffers[0]]
        for o in range(1, size):
            pairs = [
                (i, i + (sent_to(i // step % size, o, size, ring) - i // step % size) * step)
                for i in around
            ]
            moved.append(lax.ppermute(buffers[o], axis, pairs))
        return moved

    def route(buffers, size, inner, step, name, ring=False):
        count = buffers[0].shape[0]
        lines = len(buffers) * count // size
        where = lambda: lax.axis_index("azi") // step % size
        buffers = call(
            functools.partial(route_kernel, size, count // (size * inner), inner, where, ring),
            tuple(pltpu.VMEM((lines, LANES), F32) for _ in range(size)),
            scratch=(pltpu.VMEM((size, lines, LANES), F32),),
            name="route_" + name,
            bytes_accessed=100_000,
        )(*buffers)
        return hop(buffers, "azi", size, step, ring)

    used = per * tiles + per
    surf = call(
        functools.partial(trim_kernel, slow, used, lambda: lax.axis_index("azi") // fast, True),
        tuple(pltpu.VMEM((fast * used, LANES), F32) for _ in range(slow)),
        scratch=(pltpu.VMEM((slow, fast * used, LANES), F32),),
        name="route_surf_slow",
        bytes_accessed=100_000,
    )(surf)
    surf = hop(surf, "azi", slow, fast, ring=True)
    bulk = exchange(bulk, "azi")
    surf = route(surf, fast, used, 1, "surf_fast")

    k_id, l_id = np.arange(nq), np.arange(LANES)
    circle = np.concatenate(cos_sin(k_id, k_id, nq), axis=1)
    twiddle = np.concatenate(cos_sin(l_id, k_id, length), axis=1)
    short = np.concatenate(cos_sin(np.arange(upper), l_id, LANES), axis=0)
    m_id = np.arange(modes)
    steps = [np.concatenate([t.reshape(upper, nq) for t in cos_sin(m_id, [n], length)], 1) for n in (1, 2)]
    steps = np.concatenate(steps, axis=0)
    spectrum, sides = call(
        functools.partial(forward_kernel, per, nz, modes, fast),
        (
            pltpu.VMEM((devices * 2 * per, nq), F32),
            pltpu.VMEM((azi, side, LANES), F32),
        ),
        in_specs=[anywhere] * 2 + [vmem] * (4 + fast),
        scratch=(
            pltpu.VMEM((upper, 2 * per, nq), F32),
            pltpu.SMEM((slab,), jnp.int32),
            pltpu.SMEM((slab,), F32),
            pltpu.SemaphoreType.DMA((2,)),
        ),
        name="forward",
        flops=100_000_000,
        bytes_accessed=1_000_000,
    )(cycle_shift, remainder, jnp.asarray(circle), jnp.asarray(twiddle), jnp.asarray(short), jnp.asarray(steps), *surf)
    columns = route([spectrum], fast, rad * 2 * per, 1, "column_fast")
    columns = route(columns, slow, rad * 2 * per, fast, "column_slow", ring=True)
    columns = call(
        functools.partial(halve_kernel, 2 * per),
        tuple(pltpu.VMEM((azi * 2 * per, nq), F32) for _ in range(rad)),
        scratch=(pltpu.VMEM((rad, azi * 2 * per, nq), F32),),
        name="route_column_rad",
        bytes_accessed=100_000,
    )(*columns)
    columns = hop(columns, "rad", rad, 1)
    j_of_block = np.arange(devices) * local // nq
    mixed = np.concatenate(cos_sin(j_of_block, l_id, LANES), axis=1)
    *blocks, tables, factor = call(
        functools.partial(couple_kernel, per, local, fast, slow),
        (
            *(pltpu.VMEM((azi * per, nq), F32) for _ in range(rad)),
            pltpu.VMEM((devices, nq // local * 2 * LANES), F32),
            pltpu.VMEM((devices, nq), F32),
        ),
        name="couple",
        flops=100_000_000,
        bytes_accessed=1_000_000,
    )(kernel, jnp.asarray(mixed), *columns)
    blocks = hop(blocks, "rad", rad, 1)
    blocks = route(blocks, fast, per, 1, "block_fast")
    blocks = route(blocks, slow, per, fast, "block_slow", ring=True)

    moved, top = call(
        functools.partial(advect_kernel, per, nz),
        (pltpu.HBM((azi, 3 * group, seg), BF16), pltpu.VMEM((SUB, LANES), F32)),
        in_specs=[anywhere, anywhere, vmem, vmem],
        out_specs=(far, vmem),
        scratch=(
            pltpu.VMEM((3, nq, group, LANES), F32),
            pltpu.VMEM((3, nq, group, LANES), F32),
            pltpu.VMEM((3, azi, group, LANES), F32),
            pltpu.VMEM((azi, 3 * group, seg), BF16),
            pltpu.SMEM((slab,), jnp.int32),
            pltpu.SMEM((slab,), F32),
            pltpu.SemaphoreType.DMA((2,)),
            pltpu.SemaphoreType.DMA((azi,)),
        ),
        name="advect",
        flops=50 * 3 * nz * slab * seg,
        bytes_accessed=12 * nz * slab * seg,
    )(cycle_shift, remainder, bulk, sides)
    moved = exchange(moved, "azi")
    turn = np.concatenate(cos_sin(k_id, l_id, length), axis=1)
    potential = call(
        functools.partial(inverse_kernel, per, local),
        shape_of((per, length)),
        name="inverse",
        flops=100_000_000,
        bytes_accessed=1_000_000,
    )(jnp.asarray(circle), jnp.asarray(turn), tables, factor, *blocks)
    results = call(
        functools.partial(settle_kernel, per),
        tuple(pltpu.HBM((nz, slab, seg), F32) for _ in range(3)),
        out_specs=(far,) * 3,
        scratch=(pltpu.VMEM((3, nz, slab, seg), F32), pltpu.SemaphoreType.DMA((6,))),
        name="settle",
        flops=20 * 3 * nz * slab * seg,
        bytes_accessed=18 * nz * slab * seg,
    )(moved, top)
    return (*results, potential)


def solution(mesh):
    split = P(None, "rad", "azi")
    in_specs = (split, split, split, P("rad"), P("rad"), P(("rad", "azi"), None, None))
    out_specs = (split, split, split, P(("rad", "azi"), None))

    return jax.shard_map(body, mesh=mesh, in_specs=in_specs, out_specs=out_specs, check_vma=False)
```

```python
import functools
import math

import jax
import jax.numpy as jnp
import numpy as np
from jax import lax
from jax.experimental import pallas as pl
from jax.experimental.pallas import tpu as pltpu
from jax.sharding import PartitionSpec as P


RADIAL_COURANT = 0.3
VISCOSITY = 0.08
LANES = 128
VMEM_BYTES = 67_043_328
SUB = 8
EXACT = lax.Precision.HIGHEST
F32 = jnp.float32
BF16 = jnp.bfloat16

POWER = 13
TOP = 2.0**9.69
GAIN = 1.25


def encode(value, scale):
    scaled = value * scale
    second = scaled * scaled
    fourth = second * second
    return (fourth * fourth) * (fourth * scaled)


def decode(code, scale):
    root = lax.exp2(lax.log(jnp.abs(code)) * (1.0 / (POWER * math.log(2.0)))) * scale
    return jnp.where(code < 0.0, -root, root)


def sent_to(place, offset, size, ring):
    return (place + offset) % size if ring else place ^ offset


def came_from(place, offset, size, ring):
    return (place - offset + size) % size if ring else place ^ offset


def row_iota(shape):
    return lax.broadcasted_iota(jnp.int32, shape, 0)


def lane_iota(shape):
    return lax.broadcasted_iota(jnp.int32, shape, 1)


def side_rows(per, tiles):
    return -(-(per * tiles + per) // SUB) * SUB


def load_kernel(rho, ur, up, field, tail, head, sems):
    nz, slab, seg = rho.shape
    lines, width = field.shape[2:]
    copies = [
        pltpu.make_async_copy(far, field.at[c, :, pl.ds(0, slab), pl.ds(0, seg)], sems.at[c])
        for c, far in enumerate((rho, ur, up))
    ]
    for copy in copies:
        copy.start()
    for c in range(3):
        for z in range(nz):
            field[c, z, :, seg:width] = jnp.zeros((lines, width - seg), F32)
    for c in range(3):
        copies[c].wait()
        tail[c] = field[c, :, slab - 2 : slab, 0:seg]
        head[c] = field[c, :, 0:2, 0:seg]


def advance(ref, tile, z, slab, scale):
    _, nz, lines, width = ref.shape
    count = lines // SUB
    sub = row_iota((SUB, width))
    near_rows = row_iota((SUB, LANES))
    cycle = tile * SUB + near_rows
    cycle = jnp.where((tile == count - 1) & (near_rows >= SUB // 2), near_rows - SUB, cycle)
    cycle = lax.axis_index("rad") * slab + cycle
    radius = 1.0 + 4.0 * (cycle.astype(F32) + 0.5) / (slab * lax.axis_size("rad"))
    power = 1.0 / (radius * jnp.sqrt(radius))
    wide = lambda x: jnp.concatenate([x] * (width // LANES), axis=1)
    courant = wide((0.5 * scale) * (0.3 / radius))
    coriolis, epicycle = wide((0.2 * scale) * power), wide((0.05 * scale) * power)
    rows = lambda t: pl.ds(pl.multiple_of(t * SUB, SUB), SUB)
    here, before, after = rows(tile), rows(lax.rem(tile + count - 1, count)), rows(lax.rem(tile + 1, count))
    z_up, z_down = min(z + 1, nz - 1), max(z - 1, 0)
    center, base, rad_diff, azi_diff = [], [], [], []
    for c in range(3):
        cur = ref[c, z, here, :]
        inward = pltpu.roll(jnp.where(sub == SUB - 1, ref[c, z, before, :], cur), 1, 0)
        outward = pltpu.roll(jnp.where(sub == 0, ref[c, z, after, :], cur), SUB - 1, 0)
        ahead = pltpu.roll(cur, width - 1, 1)
        behind = pltpu.roll(cur, 1, 1)
        near = ref[c, z_up, here, :] + ref[c, z_down, here, :] + inward + outward + ahead + behind
        base.append((scale * VISCOSITY) * near + (scale * (1.0 - 6.0 * VISCOSITY)) * cur)
        rad_diff.append(outward - inward)
        azi_diff.append(ahead - behind)
        center.append(cur)
    half = 0.5 * scale * RADIAL_COURANT
    return (
        base[0] - (half * rad_diff[1] + courant * azi_diff[2]),
        base[1] + coriolis * center[2] - half * rad_diff[0],
        base[2] - epicycle * center[1] - courant * azi_diff[0],
    )


def store_section(field, stage, slab, tile):
    for z in range(field.shape[1]):
        for c, value in enumerate(advance(field, tile, z, slab, 1.0)):
            stage[c, z, pl.ds(pl.multiple_of(tile * SUB, SUB), SUB), :] = value


def interior_kernel(field, stage):
    slab = field.shape[2] - SUB

    def section(tile, carry):
        store_section(field, stage, slab, tile)
        return carry

    lax.fori_loop(1, slab // SUB - 1, section, 0, unroll=True)


def hydro_kernel(
    per, seg, field_in, stage_in, low, high, bulk, surf, field, stage, block, narrow, sems
):
    _, nz, lines, width = field.shape
    slab = lines - SUB
    last = slab // SUB
    tiles = seg // LANES
    rad = lax.axis_index("rad")
    rad_count = lax.axis_size("rad")
    for c in range(3):
        for z in range(nz):
            inner = jnp.broadcast_to(field[c, z, 0:1, 0:seg], (2, seg))
            outer = jnp.broadcast_to(field[c, z, slab - 1 : slab, 0:seg], (2, seg))
            outward = jnp.where(rad == rad_count - 1, outer, high[c, z])
            inward = jnp.where(rad == 0, inner, low[c, z])
            between = jnp.zeros((SUB - 4, seg), F32)
            field[c, z, slab:lines, 0:seg] = jnp.concatenate([outward, between, inward], axis=0)

    def section(index, carry):
        store_section(field, stage, slab, lax.rem(index + last - 1, last + 1))
        return carry

    lax.fori_loop(0, 3, section, 0, unroll=True)

    @pl.when(rad == 0)
    def _():
        for c in range(3):
            for z in range(nz):
                stage[c, z, lines - 1 : lines, :] = stage[c, z, 0:1, :]

    @pl.when(rad == rad_count - 1)
    def _():
        for c in range(3):
            for z in range(nz):
                stage[c, z, slab : slab + 1, :] = stage[c, z, slab - 1 : slab, :]

    def second_section(tile, largest):
        here = pl.ds(pl.multiple_of(tile * SUB, SUB), SUB)
        for z in range(nz):
            for c, value in enumerate(advance(stage, tile, z, slab, 0.5)):
                value = 0.5 * field[c, z, here, :] + value
                field[c, z, here, :] = value
                largest = jnp.maximum(largest, jnp.abs(value))
        return largest

    largest = lax.fori_loop(0, last, second_section, jnp.zeros((SUB, width), F32), unroll=2)
    peak = jnp.maximum(jnp.max(largest, keepdims=True), 1e-30)
    scale = TOP / peak
    dests = SUB // per
    stride = -(-3 * nz * per // SUB) * SUB

    def send(index):
        at = pl.ds(index * dests, dests)
        return pltpu.make_async_copy(narrow.at[at], bulk.at[at], sems.at[index])

    def pack(tile, carry):
        here = pl.ds(pl.multiple_of(tile * SUB, SUB), SUB)
        overflow = jnp.zeros((SUB, LANES), F32)
        column = jnp.zeros((SUB, seg), F32)
        for c in range(3):
            for z in range(nz):
                value = field[c, z, here, 0:seg]
                if c == 0:
                    column = column + value
                code = encode(value, scale)
                plane = c * nz + z
                for d in range(dests):
                    for b in range(tiles):
                        line = b * stride + plane * per
                        block[tile * dests + d, line : line + per, :] = code[
                            d * per : (d + 1) * per, b * LANES : (b + 1) * LANES
                        ]
                overflow = overflow + pltpu.roll(field[c, z, here, seg:width], 2 + 4 * plane, 1)
        overflow = jnp.where(lane_iota((SUB, LANES)) < LANES // 2, overflow, peak)
        for d in range(dests):
            dest = tile * dests + d
            for k in range(per):
                row = d * per + k
                for b in range(tiles):
                    surf[dest, k * tiles + b : k * tiles + b + 1, :] = column[
                        row : row + 1, b * LANES : (b + 1) * LANES
                    ]
                line = per * tiles + k
                surf[dest, line : line + 1, :] = overflow[row : row + 1, :]
        for d in range(dests):
            dest = tile * dests + d
            narrow[dest] = block[dest].astype(BF16)
        send(tile).start()
        return carry

    lax.fori_loop(0, last, pack, 0, unroll=True)
    for index in range(last):
        send(index).wait()


def advect_kernel(
    per, nz, far_shift, far_remainder, bulk, sides, out, top,
    ring, tapped, over, codes, shift, remainder, scalar_sems, sems,
):
    scalars = [
        pltpu.make_async_copy(far, near, scalar_sems.at[i])
        for i, (far, near) in enumerate(((far_shift, shift), (far_remainder, remainder)))
    ]
    for copy in scalars:
        copy.start()
    sources = bulk.shape[0]
    count = ring.shape[1]
    tiles = count // sources
    group = nz * per
    stride = -(-3 * group // SUB) * SUB
    me = lax.axis_index("azi")

    def widen(a, peak):
        whole_block = bulk[a].astype(F32)
        packed = sides[a, per * tiles : per * tiles + per, :]
        mine = jnp.where(lane_iota((1, LANES)) >= LANES // 2, packed[0:1, :], 0.0)
        mine = jnp.max(mine, keepdims=True)
        unit = mine * (1.0 / TOP)
        for b in range(tiles):
            value = decode(whole_block[b * stride : (b + 1) * stride, :], unit)
            for c in range(3):
                ring[c, a * tiles + b] = value[c * group : (c + 1) * group, :]
        for c in range(3):
            for z in range(nz):
                turned = pltpu.roll(packed, LANES - 2 - 4 * (c * nz + z), 1)
                over[c, a, z * per : (z + 1) * per, :] = turned
        return jnp.maximum(peak, mine)

    peak = lax.fori_loop(0, sources, widen, jnp.zeros((1, 1), F32), unroll=8)
    top[...] = jnp.broadcast_to(peak, top.shape)
    lane = lane_iota((group, LANES))
    cycle = row_iota((group, LANES)) % per

    def spill(a, carry):
        after = lax.rem((a + 1) * tiles, count)
        before = lax.rem(a * tiles + count - 1, count)
        for c in range(3):
            extra = over[c, a]
            ring[c, after] = ring[c, after] + jnp.where(lane < 2, extra, 0.0)
            ring[c, before] = ring[c, before] + jnp.where(lane >= LANES - 2, extra, 0.0)
        return carry

    lax.fori_loop(0, sources, spill, 0, unroll=16)
    for copy in scalars:
        copy.wait()
    x = jnp.zeros((group, LANES), F32)
    whole, part = [], []
    for k in range(per):
        x = jnp.where(cycle == k, -remainder[me * per + k], x)
        amount = shift[me * per + k]
        whole.append(amount // LANES)
        part.append(lax.rem(amount, LANES))
    w_next = x * (x + 1.0) * (x + 2.0) / 6.0
    w_here = -(x - 1.0) * (x + 1.0) * (x + 2.0) / 2.0
    w_prev = (x - 1.0) * x * (x + 2.0) / 2.0
    w_prev_two = -(x - 1.0) * x * (x + 1.0) / 6.0

    def tap(a, carry):
        before = lax.rem(a * tiles + count - 1, count)
        after = lax.rem((a + 1) * tiles, count)
        for c in range(3):
            line = [ring[c, before]]
            line += [ring[c, a * tiles + b] for b in range(tiles)]
            line += [ring[c, after]]
            for b in range(tiles):
                prv, cur, nxt = line[b : b + 3]
                next_one = pltpu.roll(jnp.where(lane == 0, nxt, cur), LANES - 1, 1)
                prev_one = pltpu.roll(jnp.where(lane == LANES - 1, prv, cur), 1, 1)
                prev_two = pltpu.roll(jnp.where(lane >= LANES - 2, prv, cur), 2, 1)
                tapped[c, a * tiles + b] = (
                    w_next * next_one + w_here * cur + w_prev * prev_one + w_prev_two * prev_two
                )
        return carry

    lax.fori_loop(0, sources, tap, 0, unroll=8)
    scale = (TOP / GAIN) / peak

    def send(dest):
        return pltpu.make_async_copy(codes.at[dest], out.at[dest], sems.at[dest])

    def turned_tile(c, k, t):
        source = lax.rem(t - whole[k] + 2 * count, count)
        return pltpu.roll(tapped[c, source], part[k], 1)

    def turn(dest, carry):
        carry = list(carry)
        pieces = [[None] * tiles for _ in range(3)]
        for b in range(tiles):
            t = dest * tiles + b
            for c in range(3):
                joined = jnp.zeros((group, LANES), F32)
                for k in range(per):
                    now = turned_tile(c, k, t)
                    value = jnp.where(lane < part[k], carry[c * per + k], now)
                    joined = value if per == 1 else jnp.where(cycle == k, value, joined)
                    carry[c * per + k] = now
                pieces[c][b] = encode(joined, scale)
        columns = [jnp.concatenate([pieces[c][b] for b in range(tiles)], axis=1) for c in range(3)]
        codes[dest] = jnp.concatenate(columns, axis=0).astype(BF16)
        send(dest).start()
        return tuple(carry)

    start = tuple(turned_tile(c, k, -1) for c in range(3) for k in range(per))
    lax.fori_loop(0, sources, turn, start, unroll=8)
    for dest in range(sources):
        send(dest).wait()


def forward_kernel(per, nz, modes, fast, far_shift, far_remainder, circle, twiddle, short, steps, *rest):
    rad_count = lax.axis_size("rad")
    hops, (out, sides, rows_out, shift, remainder, scalar_sems) = rest[:fast], rest[fast:]
    scalars = [
        pltpu.make_async_copy(far, near, scalar_sems.at[i])
        for i, (far, near) in enumerate(((far_shift, shift), (far_remainder, remainder)))
    ]
    for copy in scalars:
        copy.start()
    me = lax.axis_index("azi")
    azi = lax.axis_index("azi")
    slow = sides.shape[0] // fast
    used = hops[0].shape[0] // slow
    for o_fast, hop in enumerate(hops):
        for o_slow in range(slow):
            from_slow = came_from(azi // fast, o_slow, slow, True)
            from_fast = came_from(azi % fast, o_fast, fast, False)
            sides[from_slow * fast + from_fast, 0:used, :] = hop[o_slow * used : (o_slow + 1) * used, :]
    sources = sides.shape[0]
    nq = circle.shape[0]
    tiles = nq // sources
    length = nq * LANES
    upper = modes // nq
    lane = lane_iota((sources, LANES))
    q_id, a_id = row_iota((nq, 2 * sources)), lane_iota((nq, 2 * sources))
    after = lax.rem((a_id + 1) * tiles, nq)
    before = lax.rem((a_id - sources) * tiles + nq - 1, nq)
    target = (q_id == jnp.where(a_id < sources, after, before)).astype(F32)
    dot = functools.partial(jnp.dot, precision=EXACT, preferred_element_type=F32)
    spilled = []
    for k in range(per):
        packed = sides[:, per * tiles + k, :]
        extra = jnp.zeros((sources, LANES), F32)
        for z in range(nz):
            extra = extra + pltpu.roll(packed, LANES - 2 - 4 * z, 1)
        halves = (jnp.where(lane < 2, extra, 0.0), jnp.where(lane >= LANES - 2, extra, 0.0))
        spilled.append(jnp.concatenate(halves, axis=0))
    spilled = dot(target, jnp.concatenate(spilled, axis=1))
    grids = []
    for k in range(per):
        grid = sides[:, k * tiles : (k + 1) * tiles, :].reshape(nq, LANES)
        grids.append((grid + spilled[:, k * LANES : (k + 1) * LANES]).T)
    inner = dot(jnp.concatenate(grids, axis=0), circle[...])
    turn_cos, turn_sin = twiddle[:, :nq], twiddle[:, nq:]
    turned = []
    for k in range(per):
        cos_part = inner[k * LANES : (k + 1) * LANES, :nq]
        sin_part = inner[k * LANES : (k + 1) * LANES, nq:]
        turned.append(cos_part * turn_cos - sin_part * turn_sin)
        turned.append(-(sin_part * turn_cos + cos_part * turn_sin))
    outer = dot(short[...], jnp.concatenate(turned, axis=1))
    for copy in scalars:
        copy.wait()
    mode = row_iota((upper, nq)) * nq + lane_iota((upper, nq))
    cos_one, sin_one = steps[0:upper, :nq], steps[0:upper, nq:]
    cos_two, sin_two = steps[upper:, :nq], steps[upper:, nq:]
    for k in range(per):
        at = 2 * k * nq
        real = outer[:upper, at : at + nq] + outer[upper:, at + nq : at + 2 * nq]
        imag = outer[:upper, at + nq : at + 2 * nq] - outer[upper:, at : at + nq]
        x = jnp.full((upper, nq), -remainder[me * per + k], F32)
        w_next = x * (x + 1.0) * (x + 2.0) / 6.0
        w_here = -(x - 1.0) * (x + 1.0) * (x + 2.0) / 2.0
        w_prev = (x - 1.0) * x * (x + 2.0) / 2.0
        w_prev_two = -(x - 1.0) * x * (x + 1.0) / 6.0
        tap_cos = w_here + (w_next + w_prev) * cos_one + w_prev_two * cos_two
        tap_sin = (w_prev - w_next) * sin_one + w_prev_two * sin_two
        phase = lax.rem(mode * shift[me * per + k], length)
        phase = jnp.where(phase > length // 2, phase - length, phase)
        angle = phase.astype(F32) * (2.0 * math.pi / length)
        spin_cos, spin_sin = jnp.cos(angle), jnp.sin(angle)
        gain_cos = tap_cos * spin_cos - tap_sin * spin_sin
        gain_sin = tap_sin * spin_cos + tap_cos * spin_sin
        rows_out[:, k, :] = real * gain_cos + imag * gain_sin
        rows_out[:, per + k, :] = imag * gain_cos - real * gain_sin
    share = rad_count * sources // upper
    for rad in range(rad_count):
        for a in range(sources):
            at = (a * rad_count + rad) * 2 * per
            value = rows_out[(rad * sources + a) // share]
            out[at : at + 2 * per, :] = value.astype(BF16).astype(F32)


def pick(values, index):
    chosen = values[0]
    for i, value in enumerate(values[1:]):
        chosen = jnp.where(index == i + 1, value, chosen)
    return chosen


def route_kernel(size, middle, inner, where, ring, *rest):
    count = (len(rest) - 1 - size)
    sources, outs, sorted_rows = rest[:count], rest[count:-1], rest[-1]
    for i, source in enumerate(sources):
        value = source[...]
        for m in range(middle):
            for dest in range(size):
                at = (m * size + dest) * inner
                to = (i * middle + m) * inner
                sorted_rows[dest, to : to + inner, :] = value[at : at + inner, :]
    choices = [sorted_rows[dest] for dest in range(size)]
    index = where()
    for offset, out in enumerate(outs):
        out[...] = pick(choices, sent_to(index, offset, size, ring))


def trim_kernel(size, used, where, ring, surf, *rest):
    outs, sorted_rows = rest[:-1], rest[-1]
    inner = surf.shape[0] // size
    for dest in range(size):
        for i in range(inner):
            sorted_rows[dest, i * used : (i + 1) * used, :] = surf[dest * inner + i, 0:used, :]
    choices = [sorted_rows[dest] for dest in range(size)]
    index = where()
    for offset, out in enumerate(outs):
        out[...] = pick(choices, sent_to(index, offset, size, ring))


def halve_kernel(inner, *rest):
    rad_count = lax.axis_size("rad")
    outs, sorted_rows = rest[-1 - rad_count : -1], rest[-1]
    to = 0
    for source in rest[: -1 - rad_count]:
        value = source[...]
        for m in range(value.shape[0] // (rad_count * inner)):
            for rad in range(rad_count):
                at = (m * rad_count + rad) * inner
                sorted_rows[rad, to : to + inner, :] = value[at : at + inner, :]
            to += inner
    choices = [sorted_rows[rad] for rad in range(rad_count)]
    for offset, out in enumerate(outs):
        out[...] = pick(choices, sent_to(lax.axis_index("rad"), offset, rad_count, False))


def arrival_source(slow, fast, axis_iota):
    rad_count = lax.axis_size("rad")
    azi, rad = lax.axis_index("azi"), lax.axis_index("rad")
    from_rad = came_from(rad, axis_iota % rad_count, rad_count, False)
    from_fast = came_from(azi % fast, axis_iota // rad_count % fast, fast, False)
    from_slow = came_from(azi // fast, axis_iota // (rad_count * fast) % slow, slow, True)
    return (from_rad * slow + from_slow) * fast + from_fast


def couple_kernel(per, local, fast, slow, kernel, mixed, *rest):
    rad_count = lax.axis_size("rad")
    columns, outs, (tables, factor) = rest[:rad_count], rest[rad_count:-2], rest[-2:]
    sources = slow * fast * rad_count
    nq = columns[0].shape[1]
    total = sources * per
    me = lax.axis_index("rad") * lax.axis_size("azi") + lax.axis_index("azi")
    offset = lax.rem(me * local, nq)
    row, col = row_iota((total, total)), lane_iota((total, total))
    place = col % sources
    azi_count = slow * fast
    place = place % azi_count * rad_count + place // azi_count
    source = arrival_source(slow, fast, place)
    spread = (row == source * per + col // sources).astype(F32)
    lane = lane_iota((total, nq))
    sides = []
    for c in range(2):
        stacked = jnp.concatenate(
            [
                ref[pl.ds(c * per + k, slow * fast, stride=2 * per), :]
                for k in range(per)
                for ref in columns
            ],
            axis=0,
        )
        ordered = jnp.dot(spread, stacked, preferred_element_type=F32)
        sides.append(pltpu.roll(ordered, lax.rem(nq - offset + c * local, nq), 1))
    weights = jnp.where(lane < local, sides[0], sides[1]).astype(BF16)
    result = jnp.zeros((total, nq), F32)
    for m in range(local):
        product = jnp.dot(kernel[m], weights, preferred_element_type=F32)
        result = jnp.where((lane == m) | (lane == local + m), product, result)
    rad = lax.axis_index("rad")
    share = total // len(outs)
    slabs = [result[i * share : (i + 1) * share, :] for i in range(len(outs))]
    for offset, out in enumerate(outs):
        out[...] = pick(slabs, sent_to(rad, offset, len(outs), False))
    share = nq // local
    source = arrival_source(slow, fast, row_iota((sources, sources)))
    order = (source == lane_iota((sources, sources))).astype(F32)
    ordered = jnp.dot(order, mixed[...], precision=EXACT, preferred_element_type=F32)
    own = arrival_source(slow, fast, row_iota(ordered.shape)) % share
    tables[...] = jnp.concatenate([jnp.where(own == h, ordered, 0.0) for h in range(share)], axis=1)
    source = arrival_source(slow, fast, row_iota((sources, nq)))
    constant = (source == 0) & (lane_iota((sources, nq)) % local == 0)
    factor[...] = jnp.where(constant, 1.0, 2.0) / (nq * LANES)


def three_pass_dot(left, right):
    dot = functools.partial(jnp.dot, preferred_element_type=F32)
    left_high, right_high = left.astype(BF16), right.astype(BF16)
    left_low = (left - left_high.astype(F32)).astype(BF16)
    right_low = (right - right_high.astype(F32)).astype(BF16)
    return dot(left_high, right_high) + (dot(left_low, right_high) + dot(left_high, right_low))


def settle_kernel(per, bulk, top, rho, ur, up, near, sems):
    nz = rho.shape[0]
    sources, _, seg = bulk.shape
    group = nz * per
    unit = jnp.concatenate([top[0:1, :] * (GAIN / TOP)] * (seg // LANES), axis=1)
    half = sources // 2 * per
    copies = [
        pltpu.make_async_copy(
            near.at[c, :, pl.ds(i * half, half), :], far.at[:, pl.ds(i * half, half), :], sems.at[2 * c + i]
        )
        for c, far in enumerate((rho, ur, up))
        for i in range(2)
    ]
    for c in range(3):
        for a in range(sources):
            value = decode(bulk[a, c * group : (c + 1) * group, :].astype(F32), unit)
            for z in range(nz):
                near[c, z, a * per : (a + 1) * per, :] = value[z * per : (z + 1) * per, :]
            if (a + 1) * per % half == 0:
                copies[2 * c + a * per // half].start()
    for copy in copies:
        copy.wait()


def inverse_kernel(per, local, circle, twiddle, tables, factor, *rest):
    blocks, out = rest[:-1], rest[-1]
    slow = len(blocks)
    nq = circle.shape[0]
    share = nq // local
    count = tables.shape[0]
    picked = []
    for k in range(per):
        rows = [
            ref[pl.ds(k, count // slow, stride=per), :] if per > 1 else ref[...] for ref in blocks
        ]
        picked.append(jnp.concatenate(rows, axis=0) * factor[...])
    mid = three_pass_dot(jnp.concatenate(picked, axis=1).T, tables[...])
    turn_cos, turn_sin = twiddle[:, :LANES], twiddle[:, LANES:]
    turned = []
    for k in range(per):
        real, imag = [], []
        for h in range(share):
            at = 2 * LANES * h
            upper = mid[k * nq : k * nq + local, at : at + 2 * LANES]
            lower = mid[k * nq + local : k * nq + 2 * local, at : at + 2 * LANES]
            real.append(upper[:, :LANES] - lower[:, LANES:])
            imag.append(upper[:, LANES:] + lower[:, :LANES])
        real = jnp.concatenate(real, axis=0)
        imag = jnp.concatenate(imag, axis=0)
        pair = [real * turn_cos - imag * turn_sin, -(real * turn_sin + imag * turn_cos)]
        turned.append(jnp.concatenate(pair, axis=0))
    wave = three_pass_dot(circle[...], jnp.concatenate(turned, axis=1))
    for k in range(per):
        for q in range(nq):
            out[k : k + 1, q * LANES : (q + 1) * LANES] = wave[
                q : q + 1, k * LANES : (k + 1) * LANES
            ]


def cos_sin(rows, columns, length):
    steps = np.outer(rows, columns) % length
    angle = 2.0 * np.pi * steps / length
    return np.cos(angle).astype(np.float32), np.sin(angle).astype(np.float32)


def call(body, out_shape, in_specs=None, out_specs=None, scratch=(), name=None, aliases=None, room=40 * 2**20, **cost):
    kernel = pl.pallas_call(
        body,
        out_shape=out_shape,
        **({} if in_specs is None else {"in_specs": in_specs}),
        **({} if out_specs is None else {"out_specs": out_specs}),
        scratch_shapes=list(scratch),
        input_output_aliases=aliases or {},
        compiler_params=pltpu.CompilerParams(vmem_limit_bytes=VMEM_BYTES - room),
        cost_estimate=pl.CostEstimate(**{"flops": 0, "bytes_accessed": 0, "transcendentals": 0, **cost}),
    )

    def run(*operands):
        places = [
            None if x.ndim == 1 else pltpu.HBM if name == "load" else pltpu.VMEM
            for x in operands
        ]
        near = [
            x if place is None else pltpu.with_memory_space_constraint(x, place)
            for x, place in zip(operands, places)
        ]
        return kernel(*near)

    return run


def exchange(array, axes):
    return lax.all_to_all(array, axes, 0, 0, tiled=True)


def shape_of(shape, dtype=F32):
    return jax.ShapeDtypeStruct(shape, dtype)


def body(density, radial_velocity, azimuthal_velocity, cycle_shift, remainder, kernel):
    nz, slab, seg = density.shape
    azi, rad = lax.axis_size("azi"), lax.axis_size("rad")
    devices = azi * rad
    per = slab // azi
    tiles = seg // LANES
    length = seg * azi
    nq = length // LANES
    local = kernel.shape[0]
    modes = local * devices
    upper = modes // nq
    width = seg + LANES
    group = nz * per
    stride = -(-3 * group // SUB) * SUB
    rows = tiles * stride
    side = side_rows(per, tiles)
    fast = min(4, azi)
    slow = azi // fast
    vmem, smem = pl.BlockSpec(memory_space=pltpu.VMEM), pl.BlockSpec(memory_space=pltpu.SMEM)

    fields = (density, radial_velocity, azimuthal_velocity)
    anywhere = pl.BlockSpec(memory_space=pl.ANY)
    far = pl.BlockSpec(memory_space=pltpu.HBM)
    edge = pltpu.VMEM((3, nz, 2, seg), F32)
    padded = pltpu.VMEM((3, nz, slab + SUB, width), F32)
    field, tail, head = call(
        load_kernel,
        (padded, edge, edge),
        in_specs=[far] * 3,
        scratch=(pltpu.SemaphoreType.DMA((3,)),),
        name="load",
        bytes_accessed=12 * nz * slab * seg,
    )(*fields)
    low = lax.ppermute(tail, "rad", [(i, (i + 1) % rad) for i in range(rad)])
    high = lax.ppermute(head, "rad", [((i + 1) % rad, i) for i in range(rad)])
    stage = call(interior_kernel, padded, name="interior", bytes_accessed=12 * nz * slab * seg)(field)
    bulk, surf, *_ = call(
        functools.partial(hydro_kernel, per, seg),
        (pltpu.HBM((azi, rows, LANES), BF16), pltpu.VMEM((azi, side, LANES), F32), padded, padded),
        out_specs=(far, vmem, vmem, vmem),
        aliases={0: 2, 1: 3},
        scratch=(
            pltpu.VMEM((azi, rows, LANES), F32),
            pltpu.VMEM((azi, rows, LANES), BF16),
            pltpu.SemaphoreType.DMA((slab // SUB,)),
        ),
        name="hydro",
        flops=100 * 3 * nz * slab * seg,
        bytes_accessed=24 * nz * slab * seg,
    )(field, stage, low, high)

    def hop(buffers, axis, size, step, ring=False):
        around = range(lax.axis_size(axis))
        moved = [buffers[0]]
        for o in range(1, size):
            pairs = [
                (i, i + (sent_to(i // step % size, o, size, ring) - i // step % size) * step)
                for i in around
            ]
            moved.append(lax.ppermute(buffers[o], axis, pairs))
        return moved

    def route(buffers, size, inner, step, name, ring=False):
        count = buffers[0].shape[0]
        lines = len(buffers) * count // size
        where = lambda: lax.axis_index("azi") // step % size
        buffers = call(
            functools.partial(route_kernel, size, count // (size * inner), inner, where, ring),
            tuple(pltpu.VMEM((lines, LANES), F32) for _ in range(size)),
            scratch=(pltpu.VMEM((size, lines, LANES), F32),),
            name="route_" + name,
            bytes_accessed=100_000,
        )(*buffers)
        return hop(buffers, "azi", size, step, ring)

    used = per * tiles + per
    surf = call(
        functools.partial(trim_kernel, slow, used, lambda: lax.axis_index("azi") // fast, True),
        tuple(pltpu.VMEM((fast * used, LANES), F32) for _ in range(slow)),
        scratch=(pltpu.VMEM((slow, fast * used, LANES), F32),),
        name="route_surf_slow",
        bytes_accessed=100_000,
    )(surf)
    surf = hop(surf, "azi", slow, fast, ring=True)
    bulk = exchange(bulk, "azi")
    surf = route(surf, fast, used, 1, "surf_fast")

    k_id, l_id = np.arange(nq), np.arange(LANES)
    circle = np.concatenate(cos_sin(k_id, k_id, nq), axis=1)
    twiddle = np.concatenate(cos_sin(l_id, k_id, length), axis=1)
    short = np.concatenate(cos_sin(np.arange(upper), l_id, LANES), axis=0)
    m_id = np.arange(modes)
    steps = [np.concatenate([t.reshape(upper, nq) for t in cos_sin(m_id, [n], length)], 1) for n in (1, 2)]
    steps = np.concatenate(steps, axis=0)
    spectrum, sides = call(
        functools.partial(forward_kernel, per, nz, modes, fast),
        (
            pltpu.VMEM((devices * 2 * per, nq), F32),
            pltpu.VMEM((azi, side, LANES), F32),
        ),
        in_specs=[anywhere] * 2 + [vmem] * (4 + fast),
        scratch=(
            pltpu.VMEM((upper, 2 * per, nq), F32),
            pltpu.SMEM((slab,), jnp.int32),
            pltpu.SMEM((slab,), F32),
            pltpu.SemaphoreType.DMA((2,)),
        ),
        name="forward",
        flops=100_000_000,
        bytes_accessed=1_000_000,
    )(cycle_shift, remainder, jnp.asarray(circle), jnp.asarray(twiddle), jnp.asarray(short), jnp.asarray(steps), *surf)
    columns = route([spectrum], fast, rad * 2 * per, 1, "column_fast")
    columns = route(columns, slow, rad * 2 * per, fast, "column_slow", ring=True)
    columns = call(
        functools.partial(halve_kernel, 2 * per),
        tuple(pltpu.VMEM((azi * 2 * per, nq), F32) for _ in range(rad)),
        scratch=(pltpu.VMEM((rad, azi * 2 * per, nq), F32),),
        name="route_column_rad",
        bytes_accessed=100_000,
    )(*columns)
    columns = hop(columns, "rad", rad, 1)
    j_of_block = np.arange(devices) * local // nq
    mixed = np.concatenate(cos_sin(j_of_block, l_id, LANES), axis=1)
    *blocks, tables, factor = call(
        functools.partial(couple_kernel, per, local, fast, slow),
        (
            *(pltpu.VMEM((azi * per, nq), F32) for _ in range(rad)),
            pltpu.VMEM((devices, nq // local * 2 * LANES), F32),
            pltpu.VMEM((devices, nq), F32),
        ),
        name="couple",
        flops=100_000_000,
        bytes_accessed=1_000_000,
    )(kernel, jnp.asarray(mixed), *columns)
    blocks = hop(blocks, "rad", rad, 1)
    blocks = route(blocks, fast, per, 1, "block_fast")
    blocks = route(blocks, slow, per, fast, "block_slow", ring=True)

    moved, top = call(
        functools.partial(advect_kernel, per, nz),
        (pltpu.HBM((azi, 3 * group, seg), BF16), pltpu.VMEM((SUB, LANES), F32)),
        in_specs=[anywhere, anywhere, vmem, vmem],
        out_specs=(far, vmem),
        scratch=(
            pltpu.VMEM((3, nq, group, LANES), F32),
            pltpu.VMEM((3, nq, group, LANES), F32),
            pltpu.VMEM((3, azi, group, LANES), F32),
            pltpu.VMEM((azi, 3 * group, seg), BF16),
            pltpu.SMEM((slab,), jnp.int32),
            pltpu.SMEM((slab,), F32),
            pltpu.SemaphoreType.DMA((2,)),
            pltpu.SemaphoreType.DMA((azi,)),
        ),
        name="advect",
        flops=50 * 3 * nz * slab * seg,
        bytes_accessed=12 * nz * slab * seg,
    )(cycle_shift, remainder, bulk, sides)
    moved = exchange(moved, "azi")
    turn = np.concatenate(cos_sin(k_id, l_id, length), axis=1)
    potential = call(
        functools.partial(inverse_kernel, per, local),
        shape_of((per, length)),
        name="inverse",
        flops=100_000_000,
        bytes_accessed=1_000_000,
    )(jnp.asarray(circle), jnp.asarray(turn), tables, factor, *blocks)
    results = call(
        functools.partial(settle_kernel, per),
        tuple(pltpu.HBM((nz, slab, seg), F32) for _ in range(3)),
        out_specs=(far,) * 3,
        scratch=(pltpu.VMEM((3, nz, slab, seg), F32), pltpu.SemaphoreType.DMA((6,))),
        name="settle",
        flops=20 * 3 * nz * slab * seg,
        bytes_accessed=18 * nz * slab * seg,
    )(moved, top)
    return (*results, potential)


def solution(mesh):
    split = P(None, "rad", "azi")
    in_specs = (split, split, split, P("rad"), P("rad"), P(("rad", "azi"), None, None))
    out_specs = (split, split, split, P(("rad", "azi"), None))

    return jax.shard_map(body, mesh=mesh, in_specs=in_specs, out_specs=out_specs, check_vma=False)
```

```python
import functools
import math

import jax
import jax.numpy as jnp
import numpy as np
from jax import lax
from jax.experimental import pallas as pl
from jax.experimental.pallas import tpu as pltpu
from jax.sharding import PartitionSpec as P


RADIAL_COURANT = 0.3
VISCOSITY = 0.08
LANES = 128
VMEM_BYTES = 67_043_328
SUB = 8
EXACT = lax.Precision.HIGHEST
F32 = jnp.float32
BF16 = jnp.bfloat16

POWER = 13
TOP = 2.0**9.69
GAIN = 1.25


def encode(value, scale):
    scaled = value * scale
    second = scaled * scaled
    fourth = second * second
    return (fourth * fourth) * (fourth * scaled)


def decode(code, scale):
    root = lax.exp2(lax.log(jnp.abs(code)) * (1.0 / (POWER * math.log(2.0)))) * scale
    return jnp.where(code < 0.0, -root, root)


def sent_to(place, offset, size, ring):
    return (place + offset) % size if ring else place ^ offset


def came_from(place, offset, size, ring):
    return (place - offset + size) % size if ring else place ^ offset


def row_iota(shape):
    return lax.broadcasted_iota(jnp.int32, shape, 0)


def lane_iota(shape):
    return lax.broadcasted_iota(jnp.int32, shape, 1)


def side_rows(per, tiles):
    return -(-(per * tiles + per) // SUB) * SUB


def load_kernel(rho, ur, up, field, tail, head, sems):
    nz, slab, seg = rho.shape
    lines, width = field.shape[2:]
    copies = [
        pltpu.make_async_copy(far, field.at[c, :, pl.ds(0, slab), pl.ds(0, seg)], sems.at[c])
        for c, far in enumerate((rho, ur, up))
    ]
    for copy in copies:
        copy.start()
    for c in range(3):
        for z in range(nz):
            field[c, z, :, seg:width] = jnp.zeros((lines, width - seg), F32)
    for c in range(3):
        copies[c].wait()
        tail[c] = field[c, :, slab - 2 : slab, 0:seg]
        head[c] = field[c, :, 0:2, 0:seg]


def advance(ref, tile, z, slab, scale):
    _, nz, lines, width = ref.shape
    count = lines // SUB
    sub = row_iota((SUB, width))
    near_rows = row_iota((SUB, LANES))
    cycle = tile * SUB + near_rows
    cycle = jnp.where((tile == count - 1) & (near_rows >= SUB // 2), near_rows - SUB, cycle)
    cycle = lax.axis_index("rad") * slab + cycle
    radius = 1.0 + 4.0 * (cycle.astype(F32) + 0.5) / (slab * lax.axis_size("rad"))
    power = 1.0 / (radius * jnp.sqrt(radius))
    wide = lambda x: jnp.concatenate([x] * (width // LANES), axis=1)
    courant = wide((0.5 * scale) * (0.3 / radius))
    coriolis, epicycle = wide((0.2 * scale) * power), wide((0.05 * scale) * power)
    rows = lambda t: pl.ds(pl.multiple_of(t * SUB, SUB), SUB)
    here, before, after = rows(tile), rows(lax.rem(tile + count - 1, count)), rows(lax.rem(tile + 1, count))
    z_up, z_down = min(z + 1, nz - 1), max(z - 1, 0)
    center, base, rad_diff, azi_diff = [], [], [], []
    for c in range(3):
        cur = ref[c, z, here, :]
        inward = pltpu.roll(jnp.where(sub == SUB - 1, ref[c, z, before, :], cur), 1, 0)
        outward = pltpu.roll(jnp.where(sub == 0, ref[c, z, after, :], cur), SUB - 1, 0)
        ahead = pltpu.roll(cur, width - 1, 1)
        behind = pltpu.roll(cur, 1, 1)
        near = ref[c, z_up, here, :] + ref[c, z_down, here, :] + inward + outward + ahead + behind
        base.append((scale * VISCOSITY) * near + (scale * (1.0 - 6.0 * VISCOSITY)) * cur)
        rad_diff.append(outward - inward)
        azi_diff.append(ahead - behind)
        center.append(cur)
    half = 0.5 * scale * RADIAL_COURANT
    return (
        base[0] - (half * rad_diff[1] + courant * azi_diff[2]),
        base[1] + coriolis * center[2] - half * rad_diff[0],
        base[2] - epicycle * center[1] - courant * azi_diff[0],
    )


def store_section(field, stage, slab, tile):
    for z in range(field.shape[1]):
        for c, value in enumerate(advance(field, tile, z, slab, 1.0)):
            stage[c, z, pl.ds(pl.multiple_of(tile * SUB, SUB), SUB), :] = value


def interior_kernel(field, stage):
    slab = field.shape[2] - SUB

    def section(tile, carry):
        store_section(field, stage, slab, tile)
        return carry

    lax.fori_loop(1, slab // SUB - 1, section, 0, unroll=True)


def hydro_kernel(
    per, seg, field_in, stage_in, low, high, bulk, surf, field, stage, block, narrow, sems
):
    _, nz, lines, width = field.shape
    slab = lines - SUB
    last = slab // SUB
    tiles = seg // LANES
    rad = lax.axis_index("rad")
    rad_count = lax.axis_size("rad")
    for c in range(3):
        for z in range(nz):
            inner = jnp.broadcast_to(field[c, z, 0:1, 0:seg], (2, seg))
            outer = jnp.broadcast_to(field[c, z, slab - 1 : slab, 0:seg], (2, seg))
            outward = jnp.where(rad == rad_count - 1, outer, high[c, z])
            inward = jnp.where(rad == 0, inner, low[c, z])
            between = jnp.zeros((SUB - 4, seg), F32)
            field[c, z, slab:lines, 0:seg] = jnp.concatenate([outward, between, inward], axis=0)

    def section(index, carry):
        store_section(field, stage, slab, lax.rem(index + last - 1, last + 1))
        return carry

    lax.fori_loop(0, 3, section, 0, unroll=True)

    @pl.when(rad == 0)
    def _():
        for c in range(3):
            for z in range(nz):
                stage[c, z, lines - 1 : lines, :] = stage[c, z, 0:1, :]

    @pl.when(rad == rad_count - 1)
    def _():
        for c in range(3):
            for z in range(nz):
                stage[c, z, slab : slab + 1, :] = stage[c, z, slab - 1 : slab, :]

    def second_section(tile, largest):
        here = pl.ds(pl.multiple_of(tile * SUB, SUB), SUB)
        for z in range(nz):
            for c, value in enumerate(advance(stage, tile, z, slab, 0.5)):
                value = 0.5 * field[c, z, here, :] + value
                field[c, z, here, :] = value
                largest = jnp.maximum(largest, jnp.abs(value))
        return largest

    largest = lax.fori_loop(0, last, second_section, jnp.zeros((SUB, width), F32), unroll=2)
    peak = jnp.maximum(jnp.max(largest, keepdims=True), 1e-30)
    scale = TOP / peak
    dests = SUB // per
    stride = -(-3 * nz * per // SUB) * SUB

    def send(index):
        at = pl.ds(index * dests, dests)
        return pltpu.make_async_copy(narrow.at[at], bulk.at[at], sems.at[index])

    def pack(tile, carry):
        here = pl.ds(pl.multiple_of(tile * SUB, SUB), SUB)
        overflow = jnp.zeros((SUB, LANES), F32)
        column = jnp.zeros((SUB, seg), F32)
        for c in range(3):
            for z in range(nz):
                value = field[c, z, here, 0:seg]
                if c == 0:
                    column = column + value
                code = encode(value, scale)
                plane = c * nz + z
                for d in range(dests):
                    for b in range(tiles):
                        line = b * stride + plane * per
                        block[tile * dests + d, line : line + per, :] = code[
                            d * per : (d + 1) * per, b * LANES : (b + 1) * LANES
                        ]
                overflow = overflow + pltpu.roll(field[c, z, here, seg:width], 2 + 4 * plane, 1)
        overflow = jnp.where(lane_iota((SUB, LANES)) < LANES // 2, overflow, peak)
        for d in range(dests):
            dest = tile * dests + d
            for k in range(per):
                row = d * per + k
                for b in range(tiles):
                    surf[dest, k * tiles + b : k * tiles + b + 1, :] = column[
                        row : row + 1, b * LANES : (b + 1) * LANES
                    ]
                line = per * tiles + k
                surf[dest, line : line + 1, :] = overflow[row : row + 1, :]
        for d in range(dests):
            dest = tile * dests + d
            narrow[dest] = block[dest].astype(BF16)
        send(tile).start()
        return carry

    lax.fori_loop(0, last, pack, 0, unroll=True)
    for index in range(last):
        send(index).wait()


def advect_kernel(
    per, nz, far_shift, far_remainder, bulk, sides, out, top,
    ring, tapped, over, codes, shift, remainder, scalar_sems, sems,
):
    scalars = [
        pltpu.make_async_copy(far, near, scalar_sems.at[i])
        for i, (far, near) in enumerate(((far_shift, shift), (far_remainder, remainder)))
    ]
    for copy in scalars:
        copy.start()
    sources = bulk.shape[0]
    count = ring.shape[1]
    tiles = count // sources
    group = nz * per
    stride = -(-3 * group // SUB) * SUB
    me = lax.axis_index("azi")

    def widen(a, peak):
        whole_block = bulk[a].astype(F32)
        packed = sides[a, per * tiles : per * tiles + per, :]
        mine = jnp.where(lane_iota((1, LANES)) >= LANES // 2, packed[0:1, :], 0.0)
        mine = jnp.max(mine, keepdims=True)
        unit = mine * (1.0 / TOP)
        for b in range(tiles):
            value = decode(whole_block[b * stride : (b + 1) * stride, :], unit)
            for c in range(3):
                ring[c, a * tiles + b] = value[c * group : (c + 1) * group, :]
        for c in range(3):
            for z in range(nz):
                turned = pltpu.roll(packed, LANES - 2 - 4 * (c * nz + z), 1)
                over[c, a, z * per : (z + 1) * per, :] = turned
        return jnp.maximum(peak, mine)

    peak = lax.fori_loop(0, sources, widen, jnp.zeros((1, 1), F32), unroll=True)
    top[...] = jnp.broadcast_to(peak, top.shape)
    lane = lane_iota((group, LANES))
    cycle = row_iota((group, LANES)) % per

    def spill(a, carry):
        after = lax.rem((a + 1) * tiles, count)
        before = lax.rem(a * tiles + count - 1, count)
        for c in range(3):
            extra = over[c, a]
            ring[c, after] = ring[c, after] + jnp.where(lane < 2, extra, 0.0)
            ring[c, before] = ring[c, before] + jnp.where(lane >= LANES - 2, extra, 0.0)
        return carry

    lax.fori_loop(0, sources, spill, 0, unroll=True)
    for copy in scalars:
        copy.wait()
    x = jnp.zeros((group, LANES), F32)
    whole, part = [], []
    for k in range(per):
        x = jnp.where(cycle == k, -remainder[me * per + k], x)
        amount = shift[me * per + k]
        whole.append(amount // LANES)
        part.append(lax.rem(amount, LANES))
    w_next = x * (x + 1.0) * (x + 2.0) / 6.0
    w_here = -(x - 1.0) * (x + 1.0) * (x + 2.0) / 2.0
    w_prev = (x - 1.0) * x * (x + 2.0) / 2.0
    w_prev_two = -(x - 1.0) * x * (x + 1.0) / 6.0

    def tap(a, carry):
        before = lax.rem(a * tiles + count - 1, count)
        after = lax.rem((a + 1) * tiles, count)
        for c in range(3):
            line = [ring[c, before]]
            line += [ring[c, a * tiles + b] for b in range(tiles)]
            line += [ring[c, after]]
            for b in range(tiles):
                prv, cur, nxt = line[b : b + 3]
                next_one = pltpu.roll(jnp.where(lane == 0, nxt, cur), LANES - 1, 1)
                prev_one = pltpu.roll(jnp.where(lane == LANES - 1, prv, cur), 1, 1)
                prev_two = pltpu.roll(jnp.where(lane >= LANES - 2, prv, cur), 2, 1)
                tapped[c, a * tiles + b] = (
                    w_next * next_one + w_here * cur + w_prev * prev_one + w_prev_two * prev_two
                )
        return carry

    lax.fori_loop(0, sources, tap, 0, unroll=True)
    scale = (TOP / GAIN) / peak

    def send(dest):
        return pltpu.make_async_copy(codes.at[dest], out.at[dest], sems.at[dest])

    def turned_tile(c, k, t):
        source = lax.rem(t - whole[k] + 2 * count, count)
        return pltpu.roll(tapped[c, source], part[k], 1)

    def turn(dest, carry):
        carry = list(carry)
        pieces = [[None] * tiles for _ in range(3)]
        for b in range(tiles):
            t = dest * tiles + b
            for c in range(3):
                joined = jnp.zeros((group, LANES), F32)
                for k in range(per):
                    now = turned_tile(c, k, t)
                    value = jnp.where(lane < part[k], carry[c * per + k], now)
                    joined = value if per == 1 else jnp.where(cycle == k, value, joined)
                    carry[c * per + k] = now
                pieces[c][b] = encode(joined, scale)
        columns = [jnp.concatenate([pieces[c][b] for b in range(tiles)], axis=1) for c in range(3)]
        codes[dest] = jnp.concatenate(columns, axis=0).astype(BF16)
        send(dest).start()
        return tuple(carry)

    start = tuple(turned_tile(c, k, -1) for c in range(3) for k in range(per))
    lax.fori_loop(0, sources, turn, start, unroll=True)
    for dest in range(sources):
        send(dest).wait()


def forward_kernel(per, nz, modes, fast, far_shift, far_remainder, circle, twiddle, short, steps, *rest):
    rad_count = lax.axis_size("rad")
    hops, (out, sides, rows_out, shift, remainder, scalar_sems) = rest[:fast], rest[fast:]
    scalars = [
        pltpu.make_async_copy(far, near, scalar_sems.at[i])
        for i, (far, near) in enumerate(((far_shift, shift), (far_remainder, remainder)))
    ]
    for copy in scalars:
        copy.start()
    me = lax.axis_index("azi")
    azi = lax.axis_index("azi")
    slow = sides.shape[0] // fast
    used = hops[0].shape[0] // slow
    for o_fast, hop in enumerate(hops):
        for o_slow in range(slow):
            from_slow = came_from(azi // fast, o_slow, slow, True)
            from_fast = came_from(azi % fast, o_fast, fast, False)
            sides[from_slow * fast + from_fast, 0:used, :] = hop[o_slow * used : (o_slow + 1) * used, :]
    sources = sides.shape[0]
    nq = circle.shape[0]
    tiles = nq // sources
    length = nq * LANES
    upper = modes // nq
    lane = lane_iota((sources, LANES))
    q_id, a_id = row_iota((nq, 2 * sources)), lane_iota((nq, 2 * sources))
    after = lax.rem((a_id + 1) * tiles, nq)
    before = lax.rem((a_id - sources) * tiles + nq - 1, nq)
    target = (q_id == jnp.where(a_id < sources, after, before)).astype(F32)
    dot = functools.partial(jnp.dot, precision=EXACT, preferred_element_type=F32)
    spilled = []
    for k in range(per):
        packed = sides[:, per * tiles + k, :]
        extra = jnp.zeros((sources, LANES), F32)
        for z in range(nz):
            extra = extra + pltpu.roll(packed, LANES - 2 - 4 * z, 1)
        halves = (jnp.where(lane < 2, extra, 0.0), jnp.where(lane >= LANES - 2, extra, 0.0))
        spilled.append(jnp.concatenate(halves, axis=0))
    spilled = dot(target, jnp.concatenate(spilled, axis=1))
    grids = []
    for k in range(per):
        grid = sides[:, k * tiles : (k + 1) * tiles, :].reshape(nq, LANES)
        grids.append((grid + spilled[:, k * LANES : (k + 1) * LANES]).T)
    inner = dot(jnp.concatenate(grids, axis=0), circle[...])
    turn_cos, turn_sin = twiddle[:, :nq], twiddle[:, nq:]
    turned = []
    for k in range(per):
        cos_part = inner[k * LANES : (k + 1) * LANES, :nq]
        sin_part = inner[k * LANES : (k + 1) * LANES, nq:]
        turned.append(cos_part * turn_cos - sin_part * turn_sin)
        turned.append(-(sin_part * turn_cos + cos_part * turn_sin))
    outer = dot(short[...], jnp.concatenate(turned, axis=1))
    for copy in scalars:
        copy.wait()
    mode = row_iota((upper, nq)) * nq + lane_iota((upper, nq))
    cos_one, sin_one = steps[0:upper, :nq], steps[0:upper, nq:]
    cos_two, sin_two = steps[upper:, :nq], steps[upper:, nq:]
    for k in range(per):
        at = 2 * k * nq
        real = outer[:upper, at : at + nq] + outer[upper:, at + nq : at + 2 * nq]
        imag = outer[:upper, at + nq : at + 2 * nq] - outer[upper:, at : at + nq]
        x = jnp.full((upper, nq), -remainder[me * per + k], F32)
        w_next = x * (x + 1.0) * (x + 2.0) / 6.0
        w_here = -(x - 1.0) * (x + 1.0) * (x + 2.0) / 2.0
        w_prev = (x - 1.0) * x * (x + 2.0) / 2.0
        w_prev_two = -(x - 1.0) * x * (x + 1.0) / 6.0
        tap_cos = w_here + (w_next + w_prev) * cos_one + w_prev_two * cos_two
        tap_sin = (w_prev - w_next) * sin_one + w_prev_two * sin_two
        phase = lax.rem(mode * shift[me * per + k], length)
        phase = jnp.where(phase > length // 2, phase - length, phase)
        angle = phase.astype(F32) * (2.0 * math.pi / length)
        spin_cos, spin_sin = jnp.cos(angle), jnp.sin(angle)
        gain_cos = tap_cos * spin_cos - tap_sin * spin_sin
        gain_sin = tap_sin * spin_cos + tap_cos * spin_sin
        rows_out[:, k, :] = real * gain_cos + imag * gain_sin
        rows_out[:, per + k, :] = imag * gain_cos - real * gain_sin
    share = rad_count * sources // upper
    for rad in range(rad_count):
        for a in range(sources):
            at = (a * rad_count + rad) * 2 * per
            value = rows_out[(rad * sources + a) // share]
            out[at : at + 2 * per, :] = value.astype(BF16).astype(F32)


def pick(values, index):
    chosen = values[0]
    for i, value in enumerate(values[1:]):
        chosen = jnp.where(index == i + 1, value, chosen)
    return chosen


def route_kernel(size, middle, inner, where, ring, *rest):
    count = (len(rest) - 1 - size)
    sources, outs, sorted_rows = rest[:count], rest[count:-1], rest[-1]
    for i, source in enumerate(sources):
        value = source[...]
        for m in range(middle):
            for dest in range(size):
                at = (m * size + dest) * inner
                to = (i * middle + m) * inner
                sorted_rows[dest, to : to + inner, :] = value[at : at + inner, :]
    choices = [sorted_rows[dest] for dest in range(size)]
    index = where()
    for offset, out in enumerate(outs):
        out[...] = pick(choices, sent_to(index, offset, size, ring))


def trim_kernel(size, used, where, ring, surf, *rest):
    outs, sorted_rows = rest[:-1], rest[-1]
    inner = surf.shape[0] // size
    for dest in range(size):
        for i in range(inner):
            sorted_rows[dest, i * used : (i + 1) * used, :] = surf[dest * inner + i, 0:used, :]
    choices = [sorted_rows[dest] for dest in range(size)]
    index = where()
    for offset, out in enumerate(outs):
        out[...] = pick(choices, sent_to(index, offset, size, ring))


def halve_kernel(inner, *rest):
    rad_count = lax.axis_size("rad")
    outs, sorted_rows = rest[-1 - rad_count : -1], rest[-1]
    to = 0
    for source in rest[: -1 - rad_count]:
        value = source[...]
        for m in range(value.shape[0] // (rad_count * inner)):
            for rad in range(rad_count):
                at = (m * rad_count + rad) * inner
                sorted_rows[rad, to : to + inner, :] = value[at : at + inner, :]
            to += inner
    choices = [sorted_rows[rad] for rad in range(rad_count)]
    for offset, out in enumerate(outs):
        out[...] = pick(choices, sent_to(lax.axis_index("rad"), offset, rad_count, False))


def arrival_source(slow, fast, axis_iota):
    rad_count = lax.axis_size("rad")
    azi, rad = lax.axis_index("azi"), lax.axis_index("rad")
    from_rad = came_from(rad, axis_iota % rad_count, rad_count, False)
    from_fast = came_from(azi % fast, axis_iota // rad_count % fast, fast, False)
    from_slow = came_from(azi // fast, axis_iota // (rad_count * fast) % slow, slow, True)
    return (from_rad * slow + from_slow) * fast + from_fast


def couple_kernel(per, local, fast, slow, kernel, mixed, *rest):
    rad_count = lax.axis_size("rad")
    columns, outs, (tables, factor) = rest[:rad_count], rest[rad_count:-2], rest[-2:]
    sources = slow * fast * rad_count
    nq = columns[0].shape[1]
    total = sources * per
    me = lax.axis_index("rad") * lax.axis_size("azi") + lax.axis_index("azi")
    offset = lax.rem(me * local, nq)
    row, col = row_iota((total, total)), lane_iota((total, total))
    place = col % sources
    azi_count = slow * fast
    place = place % azi_count * rad_count + place // azi_count
    source = arrival_source(slow, fast, place)
    spread = (row == source * per + col // sources).astype(F32)
    lane = lane_iota((total, nq))
    sides = []
    for c in range(2):
        stacked = jnp.concatenate(
            [
                ref[pl.ds(c * per + k, slow * fast, stride=2 * per), :]
                for k in range(per)
                for ref in columns
            ],
            axis=0,
        )
        ordered = jnp.dot(spread, stacked, preferred_element_type=F32)
        sides.append(pltpu.roll(ordered, lax.rem(nq - offset + c * local, nq), 1))
    weights = jnp.where(lane < local, sides[0], sides[1]).astype(BF16)
    result = jnp.zeros((total, nq), F32)
    for m in range(local):
        product = jnp.dot(kernel[m], weights, preferred_element_type=F32)
        result = jnp.where((lane == m) | (lane == local + m), product, result)
    rad = lax.axis_index("rad")
    share = total // len(outs)
    slabs = [result[i * share : (i + 1) * share, :] for i in range(len(outs))]
    for offset, out in enumerate(outs):
        out[...] = pick(slabs, sent_to(rad, offset, len(outs), False))
    share = nq // local
    source = arrival_source(slow, fast, row_iota((sources, sources)))
    order = (source == lane_iota((sources, sources))).astype(F32)
    ordered = jnp.dot(order, mixed[...], precision=EXACT, preferred_element_type=F32)
    own = arrival_source(slow, fast, row_iota(ordered.shape)) % share
    tables[...] = jnp.concatenate([jnp.where(own == h, ordered, 0.0) for h in range(share)], axis=1)
    source = arrival_source(slow, fast, row_iota((sources, nq)))
    constant = (source == 0) & (lane_iota((sources, nq)) % local == 0)
    factor[...] = jnp.where(constant, 1.0, 2.0) / (nq * LANES)


def three_pass_dot(left, right):
    dot = functools.partial(jnp.dot, preferred_element_type=F32)
    left_high, right_high = left.astype(BF16), right.astype(BF16)
    left_low = (left - left_high.astype(F32)).astype(BF16)
    right_low = (right - right_high.astype(F32)).astype(BF16)
    return dot(left_high, right_high) + (dot(left_low, right_high) + dot(left_high, right_low))


def settle_kernel(per, bulk, top, rho, ur, up, near, sems):
    nz = rho.shape[0]
    sources, _, seg = bulk.shape
    group = nz * per
    unit = jnp.concatenate([top[0:1, :] * (GAIN / TOP)] * (seg // LANES), axis=1)
    half = sources // 2 * per
    copies = [
        pltpu.make_async_copy(
            near.at[c, :, pl.ds(i * half, half), :], far.at[:, pl.ds(i * half, half), :], sems.at[2 * c + i]
        )
        for c, far in enumerate((rho, ur, up))
        for i in range(2)
    ]
    for c in range(3):
        for a in range(sources):
            value = decode(bulk[a, c * group : (c + 1) * group, :].astype(F32), unit)
            for z in range(nz):
                near[c, z, a * per : (a + 1) * per, :] = value[z * per : (z + 1) * per, :]
            if (a + 1) * per % half == 0:
                copies[2 * c + a * per // half].start()
    for copy in copies:
        copy.wait()


def inverse_kernel(per, local, circle, twiddle, tables, factor, *rest):
    blocks, out = rest[:-1], rest[-1]
    slow = len(blocks)
    nq = circle.shape[0]
    share = nq // local
    count = tables.shape[0]
    picked = []
    for k in range(per):
        rows = [
            ref[pl.ds(k, count // slow, stride=per), :] if per > 1 else ref[...] for ref in blocks
        ]
        picked.append(jnp.concatenate(rows, axis=0) * factor[...])
    mid = three_pass_dot(jnp.concatenate(picked, axis=1).T, tables[...])
    turn_cos, turn_sin = twiddle[:, :LANES], twiddle[:, LANES:]
    turned = []
    for k in range(per):
        real, imag = [], []
        for h in range(share):
            at = 2 * LANES * h
            upper = mid[k * nq : k * nq + local, at : at + 2 * LANES]
            lower = mid[k * nq + local : k * nq + 2 * local, at : at + 2 * LANES]
            real.append(upper[:, :LANES] - lower[:, LANES:])
            imag.append(upper[:, LANES:] + lower[:, :LANES])
        real = jnp.concatenate(real, axis=0)
        imag = jnp.concatenate(imag, axis=0)
        pair = [real * turn_cos - imag * turn_sin, -(real * turn_sin + imag * turn_cos)]
        turned.append(jnp.concatenate(pair, axis=0))
    wave = three_pass_dot(circle[...], jnp.concatenate(turned, axis=1))
    for k in range(per):
        for q in range(nq):
            out[k : k + 1, q * LANES : (q + 1) * LANES] = wave[
                q : q + 1, k * LANES : (k + 1) * LANES
            ]


def cos_sin(rows, columns, length):
    steps = np.outer(rows, columns) % length
    angle = 2.0 * np.pi * steps / length
    return np.cos(angle).astype(np.float32), np.sin(angle).astype(np.float32)


def call(body, out_shape, in_specs=None, out_specs=None, scratch=(), name=None, aliases=None, room=40 * 2**20, **cost):
    kernel = pl.pallas_call(
        body,
        out_shape=out_shape,
        **({} if in_specs is None else {"in_specs": in_specs}),
        **({} if out_specs is None else {"out_specs": out_specs}),
        scratch_shapes=list(scratch),
        input_output_aliases=aliases or {},
        compiler_params=pltpu.CompilerParams(vmem_limit_bytes=VMEM_BYTES - room),
        cost_estimate=pl.CostEstimate(**{"flops": 0, "bytes_accessed": 0, "transcendentals": 0, **cost}),
    )

    def run(*operands):
        places = [
            None if x.ndim == 1 else pltpu.HBM if name == "load" else pltpu.VMEM
            for x in operands
        ]
        near = [
            x if place is None else pltpu.with_memory_space_constraint(x, place)
            for x, place in zip(operands, places)
        ]
        return kernel(*near)

    return run


def exchange(array, axes):
    return lax.all_to_all(array, axes, 0, 0, tiled=True)


def shape_of(shape, dtype=F32):
    return jax.ShapeDtypeStruct(shape, dtype)


def body(density, radial_velocity, azimuthal_velocity, cycle_shift, remainder, kernel):
    nz, slab, seg = density.shape
    azi, rad = lax.axis_size("azi"), lax.axis_size("rad")
    devices = azi * rad
    per = slab // azi
    tiles = seg // LANES
    length = seg * azi
    nq = length // LANES
    local = kernel.shape[0]
    modes = local * devices
    upper = modes // nq
    width = seg + LANES
    group = nz * per
    stride = -(-3 * group // SUB) * SUB
    rows = tiles * stride
    side = side_rows(per, tiles)
    fast = min(4, azi)
    slow = azi // fast
    vmem, smem = pl.BlockSpec(memory_space=pltpu.VMEM), pl.BlockSpec(memory_space=pltpu.SMEM)

    fields = (density, radial_velocity, azimuthal_velocity)
    anywhere = pl.BlockSpec(memory_space=pl.ANY)
    far = pl.BlockSpec(memory_space=pltpu.HBM)
    edge = pltpu.VMEM((3, nz, 2, seg), F32)
    padded = pltpu.VMEM((3, nz, slab + SUB, width), F32)
    field, tail, head = call(
        load_kernel,
        (padded, edge, edge),
        in_specs=[far] * 3,
        scratch=(pltpu.SemaphoreType.DMA((3,)),),
        name="load",
        bytes_accessed=12 * nz * slab * seg,
    )(*fields)
    low = lax.ppermute(tail, "rad", [(i, (i + 1) % rad) for i in range(rad)])
    high = lax.ppermute(head, "rad", [((i + 1) % rad, i) for i in range(rad)])
    stage = call(interior_kernel, padded, name="interior", bytes_accessed=12 * nz * slab * seg)(field)
    bulk, surf, *_ = call(
        functools.partial(hydro_kernel, per, seg),
        (pltpu.HBM((azi, rows, LANES), BF16), pltpu.VMEM((azi, side, LANES), F32), padded, padded),
        out_specs=(far, vmem, vmem, vmem),
        aliases={0: 2, 1: 3},
        scratch=(
            pltpu.VMEM((azi, rows, LANES), F32),
            pltpu.VMEM((azi, rows, LANES), BF16),
            pltpu.SemaphoreType.DMA((slab // SUB,)),
        ),
        name="hydro",
        flops=100 * 3 * nz * slab * seg,
        bytes_accessed=24 * nz * slab * seg,
    )(field, stage, low, high)

    def hop(buffers, axis, size, step, ring=False):
        around = range(lax.axis_size(axis))
        moved = [buffers[0]]
        for o in range(1, size):
            pairs = [
                (i, i + (sent_to(i // step % size, o, size, ring) - i // step % size) * step)
                for i in around
            ]
            moved.append(lax.ppermute(buffers[o], axis, pairs))
        return moved

    def route(buffers, size, inner, step, name, ring=False):
        count = buffers[0].shape[0]
        lines = len(buffers) * count // size
        where = lambda: lax.axis_index("azi") // step % size
        buffers = call(
            functools.partial(route_kernel, size, count // (size * inner), inner, where, ring),
            tuple(pltpu.VMEM((lines, LANES), F32) for _ in range(size)),
            scratch=(pltpu.VMEM((size, lines, LANES), F32),),
            name="route_" + name,
            bytes_accessed=100_000,
        )(*buffers)
        return hop(buffers, "azi", size, step, ring)

    used = per * tiles + per
    surf = call(
        functools.partial(trim_kernel, slow, used, lambda: lax.axis_index("azi") // fast, True),
        tuple(pltpu.VMEM((fast * used, LANES), F32) for _ in range(slow)),
        scratch=(pltpu.VMEM((slow, fast * used, LANES), F32),),
        name="route_surf_slow",
        bytes_accessed=100_000,
    )(surf)
    surf = hop(surf, "azi", slow, fast, ring=True)
    bulk = exchange(bulk, "azi")
    surf = route(surf, fast, used, 1, "surf_fast")

    k_id, l_id = np.arange(nq), np.arange(LANES)
    circle = np.concatenate(cos_sin(k_id, k_id, nq), axis=1)
    twiddle = np.concatenate(cos_sin(l_id, k_id, length), axis=1)
    short = np.concatenate(cos_sin(np.arange(upper), l_id, LANES), axis=0)
    m_id = np.arange(modes)
    steps = [np.concatenate([t.reshape(upper, nq) for t in cos_sin(m_id, [n], length)], 1) for n in (1, 2)]
    steps = np.concatenate(steps, axis=0)
    spectrum, sides = call(
        functools.partial(forward_kernel, per, nz, modes, fast),
        (
            pltpu.VMEM((devices * 2 * per, nq), F32),
            pltpu.VMEM((azi, side, LANES), F32),
        ),
        in_specs=[anywhere] * 2 + [vmem] * (4 + fast),
        scratch=(
            pltpu.VMEM((upper, 2 * per, nq), F32),
            pltpu.SMEM((slab,), jnp.int32),
            pltpu.SMEM((slab,), F32),
            pltpu.SemaphoreType.DMA((2,)),
        ),
        name="forward",
        flops=100_000_000,
        bytes_accessed=1_000_000,
    )(cycle_shift, remainder, jnp.asarray(circle), jnp.asarray(twiddle), jnp.asarray(short), jnp.asarray(steps), *surf)
    columns = route([spectrum], fast, rad * 2 * per, 1, "column_fast")
    columns = route(columns, slow, rad * 2 * per, fast, "column_slow", ring=True)
    columns = call(
        functools.partial(halve_kernel, 2 * per),
        tuple(pltpu.VMEM((azi * 2 * per, nq), F32) for _ in range(rad)),
        scratch=(pltpu.VMEM((rad, azi * 2 * per, nq), F32),),
        name="route_column_rad",
        bytes_accessed=100_000,
    )(*columns)
    columns = hop(columns, "rad", rad, 1)
    j_of_block = np.arange(devices) * local // nq
    mixed = np.concatenate(cos_sin(j_of_block, l_id, LANES), axis=1)
    *blocks, tables, factor = call(
        functools.partial(couple_kernel, per, local, fast, slow),
        (
            *(pltpu.VMEM((azi * per, nq), F32) for _ in range(rad)),
            pltpu.VMEM((devices, nq // local * 2 * LANES), F32),
            pltpu.VMEM((devices, nq), F32),
        ),
        name="couple",
        flops=100_000_000,
        bytes_accessed=1_000_000,
    )(kernel, jnp.asarray(mixed), *columns)
    blocks = hop(blocks, "rad", rad, 1)
    blocks = route(blocks, fast, per, 1, "block_fast")
    blocks = route(blocks, slow, per, fast, "block_slow", ring=True)

    moved, top = call(
        functools.partial(advect_kernel, per, nz),
        (pltpu.HBM((azi, 3 * group, seg), BF16), pltpu.VMEM((SUB, LANES), F32)),
        in_specs=[anywhere, anywhere, vmem, vmem],
        out_specs=(far, vmem),
        scratch=(
            pltpu.VMEM((3, nq, group, LANES), F32),
            pltpu.VMEM((3, nq, group, LANES), F32),
            pltpu.VMEM((3, azi, group, LANES), F32),
            pltpu.VMEM((azi, 3 * group, seg), BF16),
            pltpu.SMEM((slab,), jnp.int32),
            pltpu.SMEM((slab,), F32),
            pltpu.SemaphoreType.DMA((2,)),
            pltpu.SemaphoreType.DMA((azi,)),
        ),
        name="advect",
        flops=50 * 3 * nz * slab * seg,
        bytes_accessed=12 * nz * slab * seg,
    )(cycle_shift, remainder, bulk, sides)
    moved = exchange(moved, "azi")
    turn = np.concatenate(cos_sin(k_id, l_id, length), axis=1)
    potential = call(
        functools.partial(inverse_kernel, per, local),
        shape_of((per, length)),
        name="inverse",
        flops=100_000_000,
        bytes_accessed=1_000_000,
    )(jnp.asarray(circle), jnp.asarray(turn), tables, factor, *blocks)
    results = call(
        functools.partial(settle_kernel, per),
        tuple(pltpu.HBM((nz, slab, seg), F32) for _ in range(3)),
        out_specs=(far,) * 3,
        scratch=(pltpu.VMEM((3, nz, slab, seg), F32), pltpu.SemaphoreType.DMA((6,))),
        name="settle",
        flops=20 * 3 * nz * slab * seg,
        bytes_accessed=18 * nz * slab * seg,
    )(moved, top)
    return (*results, potential)


def solution(mesh):
    split = P(None, "rad", "azi")
    in_specs = (split, split, split, P("rad"), P("rad"), P(("rad", "azi"), None, None))
    out_specs = (split, split, split, P(("rad", "azi"), None))

    return jax.shard_map(body, mesh=mesh, in_specs=in_specs, out_specs=out_specs, check_vma=False)
```
